32 devices in a mesh: seq: 2 (over x), shard: 16 (over z, y, core).
Axes of the slice: x: 2, y: 2, z: 4, core: 2. Of those that a mesh axis runs over, the one named last changes fastest.
Arguments:
- layer_input: bfloat16 [16, 256, 2048], P('shard', 'seq'), may hold values from -6 to 6
- seq_lengths: int32 [16, 3], P('shard'), may hold values from 1 to 192, 256 in all within a row
- seq_order: int32 [16, 3], P('shard'), may hold values from 0 to 2, each once within a row
- expert_ids: int32 [16, 256, 8], P('shard', 'seq'), may hold values from 0 to 15, all different within a row; in each aligned block of 128 rows (0 to 127, 128 to 255, ..., all dimensions but the last counted through in order) at most 96 rows name the same one
- expert_probs: float32 [16, 256, 8], P('shard', 'seq'), may hold values from 0.05 to 0.3
- weight_qkv: bfloat16 [2048, 6144], P('shard'), may hold values from -0.125 to 0.125
- weight_out: bfloat16 [2048, 2048], P('shard'), may hold values from -1.5 to 1.5
- norm_gains: bfloat16 [2048, 4], P('shard'), may hold values from 0.25 to 1.75
- weight_gate: bfloat16 [16, 2048, 1024], P('shard'), may hold values from -0.125 to 0.125
- weight_up: bfloat16 [16, 2048, 1024], P('shard'), may hold values from -0.125 to 0.125
- weight_down: bfloat16 [16, 1024, 2048], P('shard'), may hold values from -0.75 to 0.75
- out_cotangent: bfloat16 [16, 256, 2048], P('shard', 'seq'), may hold values from -6 to 6
Outputs:
- layer_output: bfloat16 [16, 256, 2048], P('shard', 'seq')
- input_grad: bfloat16 [16, 256, 2048], P('shard', 'seq')
- grad_qkv: float32 [2048, 6144], P('shard')
- grad_out: float32 [2048, 2048], P('shard')
- grad_gains: float32 [2048, 4], P('shard')
- grad_gate: float32 [16, 2048, 1024], P('shard', 'seq')
- grad_up: float32 [16, 2048, 1024], P('shard', 'seq')
- grad_down: float32 [16, 1024, 2048], P('shard', 'seq')
The draws below stay inside these ranges and needn't reach their ends.
Inputs may be any that keep to these rules, and one draw needn't show every extreme that they name: `seq_lengths`: in each group the 3 lengths add up to 256, and the longest is exactly 192. `seq_order`: each group's row is a permutation of 0 to 2. `expert_ids`: each token names 8 different experts. Among the 128 tokens of one device (aligned blocks of 128 tokens in order of group and position) no expert is named more than 96 times, and in every draw some expert is named exactly 96 times within some block.
All inputs are finite; a program needn't handle non-finite values.
Results may differ from the reference program's by a relative error of at most 0.02.
Values may be sent and summed in bfloat16 or wider, within the bound.
A program may use at most 320 MiB of HBM per device.

```python
import math
from functools import partial
import jax
import jax.numpy as jnp
import numpy as np
from jax import lax

D = 2048
FF = 1024
HEADS = 16
HEAD_DIM = 128
TOP = 8
TOK_DEV = 128
SEQ_G = 3
NGROUPS = 16
GROUP_TOK = 256
MOST_LEN = 192
EXPERTS = 16
CAP = 96


def block_levels(key, dims, cuts, low, top_value):
    gain, own = 1.0, jax.random.fold_in(key, 6)
    for dim, blocks in cuts:
        steps = jnp.exp(jax.random.uniform(jax.random.fold_in(own, dim), (blocks,), jnp.float32, low / len(cuts), top_value / len(cuts)))
        gain = gain * jnp.repeat(steps, dims[dim] // blocks).reshape([-1 if axis == dim else 1 for axis in range(len(dims))])
    return gain


def split_up(count, total, limit, slope):
    portions = [(1 << 20) // math.isqrt(rank ** slope) + 1 for rank in range(2, count + 1)]
    surplus, given = total - limit - (count - 1), [1] * (count - 1)
    while surplus > 0:
        free = [i for i in range(count - 1) if given[i] < limit]
        mass, remaining = sum([portions[i] for i in free]), surplus
        for i in free:
            addition = min(limit - given[i], max(1, remaining * portions[i] // mass), surplus)
            given[i] = given[i] + addition
            surplus = surplus - addition
    return np.array([limit] + given)


def ragged(rng, number_of, total, most, skew):
    if number_of == 2:
        one = jax.random.randint(rng, (), max(1, total - most), min(most, total - 1) + 1)
        return jnp.stack([one, total - one])
    sizes = jnp.asarray(split_up(number_of, total, most, skew), jnp.int32)
    pairs = (number_of - 1) // 2
    donor, receiver = sizes[1:1 + 2 * pairs:2], sizes[2:2 + 2 * pairs:2]
    room = jnp.minimum(donor - 1, most - receiver)
    moved = jax.random.randint(jax.random.fold_in(rng, 1), (pairs,), 0, 1 << 20) % (room + 1)
    sizes = sizes.at[1:1 + 2 * pairs:2].set(donor - moved).at[2:2 + 2 * pairs:2].set(receiver + moved)
    return sizes[jax.random.permutation(jax.random.fold_in(rng, 2), number_of)]


def routed_block(key, own, number, rows, number_of, top, bound, lean):
    ranking = jax.random.permutation(key, number_of)
    heavy_load, usual = shares(number_of, rows * top, bound, lean, True), shares(number_of, rows * top, bound, lean, False)
    places = jnp.arange(number_of)

    def named(sizes, rotation):
        used = int((sizes > 0).sum())
        fixed = max(1, used // 4)
        passed = fixed + (places - fixed + rotation * (used - fixed)) % max(1, number_of - fixed)
        return jnp.zeros((number_of,), jnp.int32).at[ranking[jnp.where(places < fixed, places, passed)]].set(jnp.asarray(sizes, jnp.int32))

    sizes = jnp.where(number % 4 == 0, named(heavy_load, number // 4), named(usual, number - number // 4 - 1))
    mixed = jax.random.permutation(jax.random.fold_in(own, 3), number_of)
    source_of, receiver = mixed[0:number_of // 2 * 2:2], mixed[1:number_of // 2 * 2:2]
    slack = jnp.minimum(sizes[source_of] - 1, bound - sizes[receiver]) // 2
    slack = jnp.where((source_of == ranking[0]) | (receiver == ranking[0]) | (sizes[receiver] == 0), 0, jnp.maximum(slack, 0))
    passed = jax.random.randint(jax.random.fold_in(own, 4), (number_of // 2,), 0, 1 << 20) % (slack + 1)
    sizes = sizes.at[source_of].add(-passed).at[receiver].add(passed)
    members = jnp.searchsorted(jnp.cumsum(sizes), jnp.arange(rows * top), side="right").astype(jnp.int32)
    listing = members.reshape(top, rows).T
    listing = listing[jax.random.permutation(jax.random.fold_in(own, 1), rows)]
    rotation = jax.random.randint(jax.random.fold_in(own, 2), (rows, 1), 0, top)
    return jnp.take_along_axis(listing, (jnp.arange(top)[None, :] + rotation) % top, axis=1)


def shares(number_of, total, bound, lean, full):
    portions = [(1 << 20) // math.isqrt(standing ** lean) + 1 for standing in range(1, number_of + 1)]
    largest = bound if full else min(bound, max(-(-total // number_of), total * portions[0] // sum(portions)))
    least = 1 if total - largest >= number_of - 1 else 0
    holding, surplus = [largest] + [least] * (number_of - 1), total - largest - least * (number_of - 1)
    while surplus > 0:
        movable = [i for i in range(1, number_of) if holding[i] < largest] or [i for i in range(1, number_of) if holding[i] < bound]
        whole, budget = sum([portions[i] for i in movable]), surplus
        for i in movable:
            extra = min(bound - holding[i], max(1, budget * portions[i] // whole), surplus)
            holding[i] = holding[i] + extra
            surplus = surplus - extra
    return np.array(holding)


def noise(own_key, extent, scale, bound, cuts=(), kind=jnp.bfloat16):
    result = jax.random.normal(own_key, extent, jnp.float32) * scale
    if len(cuts) > 0:
        result = block_levels(own_key, extent, cuts, -0.22, 0.18) * result
    return jnp.clip(result, min=-bound, max=bound).astype(kind)


def setup_inputs(seed: int = 0) -> dict:
    key_list = jax.random.split(jax.random.key(seed), 13)
    layer_input = noise(key_list[0], (NGROUPS, GROUP_TOK, D), 1.0, 6.0, ((0, 16), (1, 2)))
    seq_lengths = jax.vmap(lambda own: ragged(own, SEQ_G, GROUP_TOK, MOST_LEN, 2))(jax.random.split(key_list[1], NGROUPS)).reshape((NGROUPS, SEQ_G)).astype(jnp.int32)
    seq_order = jax.vmap(lambda own: jax.random.permutation(own, SEQ_G))(jax.random.split(key_list[2], NGROUPS)).reshape((NGROUPS, SEQ_G)).astype(jnp.int32)
    expert_ids_keys = jax.random.split(jax.random.fold_in(key_list[3], 1), NGROUPS * GROUP_TOK // TOK_DEV)
    expert_ids_turns = jax.random.permutation(jax.random.fold_in(key_list[3], 3), NGROUPS * GROUP_TOK // TOK_DEV)
    expert_ids = jax.vmap(lambda own, number: routed_block(jax.random.fold_in(key_list[3], 2), own, number, TOK_DEV, EXPERTS, TOP, CAP, 1))(expert_ids_keys, expert_ids_turns).reshape((NGROUPS, GROUP_TOK, TOP))
    expert_probs = jnp.clip(0.05 + 0.25 * jax.random.uniform(key_list[4], (NGROUPS, GROUP_TOK, TOP), jnp.float32) ** block_levels(key_list[4], (NGROUPS, GROUP_TOK, TOP), ((0, 16), (1, 2)), -0.2, 0.2), 0.05, 0.3)
    weight_qkv = noise(key_list[5], (D, 3 * D), D ** -0.5, 0.125, ((0, 16),))
    weight_out = noise(key_list[6], (D, D), (max(D // 128, 4)) ** -0.5, 1.5, ((0, 16),))
    norm_gains = jnp.clip(1.0 + 0.15 * jax.random.normal(key_list[7], (D, 4), jnp.float32), 0.25, 1.75).astype(jnp.bfloat16)
    weight_gate = noise(key_list[8], (EXPERTS, D, FF), D ** -0.5, 0.125, ((0, 16),))
    weight_up = noise(key_list[9], (EXPERTS, D, FF), D ** -0.5, 0.125, ((0, 16),))
    weight_down = noise(key_list[10], (EXPERTS, FF, D), (FF // 16) ** -0.5, 0.75, ((0, 16),))
    out_cotangent = noise(key_list[11], (NGROUPS, GROUP_TOK, D), 1.0, 6.0, ((0, 16), (1, 2)))
    return {"layer_input": layer_input, "seq_lengths": seq_lengths, "seq_order": seq_order, "expert_ids": expert_ids, "expert_probs": expert_probs, "weight_qkv": weight_qkv, "weight_out": weight_out, "norm_gains": norm_gains, "weight_gate": weight_gate, "weight_up": weight_up, "weight_down": weight_down, "out_cotangent": out_cotangent}


norm_eps = 1e-05
rope_base = 10000.0
highest = lax.Precision.HIGHEST

@jax.custom_vjp
def low(v):
    return lax.optimization_barrier(v.astype(jnp.bfloat16)).astype(jnp.float32)

@jax.custom_vjp
def low_back(v):
    return v

def low_keep(v):
    return (low(v), None)

def low_pass(kept, grad):
    return (grad,)

def back_keep(v):
    return (v, None)

def back_low(kept, grad):
    return (low(grad),)
low.defvjp(low_keep, low_pass)
low_back.defvjp(back_keep, back_low)

def rms_scale(values, gain_col):
    return values * lax.rsqrt(lax.optimization_barrier(jnp.mean(values * values, axis=-1, keepdims=True)) + norm_eps) * gain_col

def rotate(values, cosine, sine_part):
    half_dim = values.shape[-1] // 2
    first_half = values[..., :half_dim]
    second_half = values[..., half_dim:]
    return jnp.concatenate([first_half * cosine - second_half * sine_part, second_half * cosine + first_half * sine_part], axis=-1)

def rope_tables(position, head_size):
    half_dim = head_size // 2
    frequency = rope_base ** (-2.0 * jnp.arange(half_dim, dtype=jnp.float32) / head_size)
    angles = position.astype(jnp.float32)[:, None] * frequency[None, :]
    return (jnp.cos(angles)[:, None, :], jnp.sin(angles)[:, None, :])

def group_layout(lengths, seq_perm, group_tok):
    seq_count = lengths.shape[0]
    numbers = jnp.arange(seq_count, dtype=jnp.int32)
    packed = lax.optimization_barrier(jnp.sum(jnp.where(seq_perm[:, None] == numbers[None, :], lengths[None, :], 0), axis=1)).astype(jnp.int32)
    seq_ends = jnp.cumsum(packed).astype(jnp.int32)
    seq_starts = (seq_ends - packed).astype(jnp.int32)
    places = jnp.arange(group_tok, dtype=jnp.int32)
    segment = lax.optimization_barrier(jnp.sum((places[:, None] >= seq_ends[None, :]).astype(jnp.int32), axis=1)).astype(jnp.int32)
    begins = lax.optimization_barrier(jnp.sum(jnp.where(segment[:, None] == numbers[None, :], seq_starts[None, :], 0), axis=1)).astype(jnp.int32)
    return (segment, (places - begins).astype(jnp.int32))

def slot_tables(expert_list, expert_count, capacity):
    rows_here, top_count = expert_list.shape
    flat_ids = expert_list.reshape(-1)
    onehot = (flat_ids[:, None] == jnp.arange(expert_count, dtype=jnp.int32)[None, :]).astype(jnp.int32)
    slot_rank = lax.optimization_barrier(jnp.sum((jnp.cumsum(onehot, axis=0).astype(jnp.int32) - 1) * onehot, axis=1)).astype(jnp.int32)
    slot_index = (flat_ids * capacity + slot_rank).astype(jnp.int32)
    owners = (jnp.arange(rows_here * top_count, dtype=jnp.int32) // top_count).astype(jnp.int32)
    sources = jnp.full((expert_count * capacity,), rows_here, dtype=jnp.int32).at[slot_index].set(owners)
    return (sources, slot_index)

def attend_group(pieces):
    query_group, key_group, value_group, segment = pieces
    places = jnp.arange(GROUP_TOK, dtype=jnp.int32)
    allowed = (segment[:, None] == segment[None, :]) & (places[None, :] <= places[:, None])
    scores = low_back(jnp.einsum('ihd,jhd->hij', query_group, key_group, precision=highest) * HEAD_DIM ** (-0.5))
    masked = jnp.where(allowed[None], scores, -1e+30)
    score_peak = lax.optimization_barrier(jnp.max(masked, axis=-1, keepdims=True))
    weights_exp = jnp.exp(masked - score_peak)
    attn_probs = weights_exp / lax.optimization_barrier(jnp.sum(weights_exp, axis=-1, keepdims=True))
    return jnp.einsum('hij,jhd->ihd', low(attn_probs), value_group, precision=highest)

def reference(layer_input, seq_lengths, seq_order, expert_ids, expert_probs, weight_qkv, weight_out, norm_gains, weight_gate, weight_up, weight_down, out_cotangent):
    segment, position = jax.vmap(partial(group_layout, group_tok=GROUP_TOK))(seq_lengths, seq_order)
    cosine, sine_part = rope_tables(position.reshape(-1), HEAD_DIM)
    block_count = NGROUPS * GROUP_TOK // TOK_DEV
    sources, slot_index = jax.vmap(partial(slot_tables, expert_count=EXPERTS, capacity=CAP))(expert_ids.reshape(block_count, TOK_DEV, TOP))
    block_probs = expert_probs.reshape(block_count, TOK_DEV, TOP).astype(jnp.float32)

    def forward(tokens_f32, qkv_f32, out_f32, gain_cols, gate_f32, up_f32, down_f32):
        flat_tokens = tokens_f32.reshape(-1, D)
        attn_in = low(rms_scale(flat_tokens, gain_cols[:, 0]))
        q_raw = low_back(jnp.dot(attn_in, qkv_f32[:, :D], precision=highest))
        k_raw = low_back(jnp.dot(attn_in, qkv_f32[:, D:2 * D], precision=highest))
        v_val = low_back(low(jnp.dot(attn_in, qkv_f32[:, 2 * D:], precision=highest)))
        query = low_back(low(rotate(rms_scale(q_raw, gain_cols[:, 1]).reshape(-1, HEADS, HEAD_DIM), cosine, sine_part)))
        key_rot = low_back(low(rotate(rms_scale(k_raw, gain_cols[:, 2]).reshape(-1, HEADS, HEAD_DIM), cosine, sine_part)))
        group_shape = (NGROUPS, GROUP_TOK, HEADS, HEAD_DIM)
        mix_groups = lax.map(jax.checkpoint(attend_group), (query.reshape(group_shape), key_rot.reshape(group_shape), v_val.reshape(group_shape), segment))
        attn_mix = low_back(low(mix_groups.reshape(-1, D)))
        resid = flat_tokens + low_back(jnp.dot(attn_mix, out_f32, precision=highest))
        ffn_in = low(rms_scale(resid, gain_cols[:, 3]))

        def mix_block(pieces):
            block_in, block_sources, block_slots, block_weights = pieces
            padded = jnp.concatenate([block_in, jnp.zeros((1, D), block_in.dtype)], axis=0)
            slot_rows = low_back(padded[block_sources].reshape(EXPERTS, CAP, D))
            gate_vals = low_back(jnp.einsum('ecd,edf->ecf', slot_rows, gate_f32, precision=highest))
            up_vals = low_back(jnp.einsum('ecd,edf->ecf', slot_rows, up_f32, precision=highest))
            hidden = low(jax.nn.silu(gate_vals) * up_vals)
            expert_out = low_back(low(jnp.einsum('ecf,efd->ecd', hidden, down_f32, precision=highest)))
            picked = expert_out.reshape(EXPERTS * CAP, D)[block_slots].reshape(TOK_DEV, TOP, D)
            return lax.optimization_barrier(jnp.sum(picked * block_weights[..., None], axis=1))
        mixed_out = lax.map(jax.checkpoint(mix_block), (ffn_in.reshape(block_count, TOK_DEV, D), sources, slot_index, block_probs))
        return (resid + mixed_out.reshape(-1, D)).reshape(NGROUPS, GROUP_TOK, D)
    primals = (layer_input.astype(jnp.float32), weight_qkv.astype(jnp.float32), weight_out.astype(jnp.float32), norm_gains.astype(jnp.float32), weight_gate.astype(jnp.float32), weight_up.astype(jnp.float32), weight_down.astype(jnp.float32))
    layer_out, pullback = jax.vjp(forward, *primals)
    gradients = pullback(out_cotangent.astype(jnp.float32))
    return (layer_out.astype(jnp.bfloat16), gradients[0].astype(jnp.bfloat16), gradients[1], gradients[2], gradients[3], gradients[4], gradients[5], gradients[6])
```

```python
import functools

import jax
import jax.numpy as jnp
from jax import lax
from jax.experimental import pallas as pl
from jax.experimental.pallas import tpu as pltpu
from jax.sharding import PartitionSpec as P

HEADS = 16
HEAD_DIM = 128


norm_eps = 1e-05
rope_base = 10000.0


def rms_scale(values, gain_col):
    return (
        values * lax.rsqrt(jnp.mean(values * values, axis=-1, keepdims=True) + norm_eps) * gain_col
    )


def rotate(values, cosine, sine_part):
    half_dim = values.shape[-1] // 2
    first_half = values[..., :half_dim]
    second_half = values[..., half_dim:]
    return jnp.concatenate(
        [
            first_half * cosine - second_half * sine_part,
            second_half * cosine + first_half * sine_part,
        ],
        axis=-1,
    )


def rope_tables(position, head_size):
    half_dim = head_size // 2
    frequency = rope_base ** (-2.0 * jnp.arange(half_dim, dtype=jnp.float32) / head_size)
    angles = position.astype(jnp.float32)[:, None] * frequency[None, :]
    return (jnp.cos(angles)[:, None, :], jnp.sin(angles)[:, None, :])


def group_layout(lengths, seq_perm, group_tok):
    seq_count = lengths.shape[0]
    numbers = jnp.arange(seq_count, dtype=jnp.int32)
    packed = jnp.sum(jnp.where(seq_perm[:, None] == numbers[None, :], lengths[None, :], 0), axis=1)
    seq_ends = jnp.cumsum(packed)
    seq_starts = seq_ends - packed
    places = jnp.arange(group_tok, dtype=jnp.int32)
    segment = jnp.sum((places[:, None] >= seq_ends[None, :]).astype(jnp.int32), axis=1)
    begins = jnp.sum(
        jnp.where(segment[:, None] == numbers[None, :], seq_starts[None, :], 0), axis=1
    )
    return (segment, places - begins)


def contract_rows(left_side, right_side):
    return lax.dot_general(
        left_side, right_side, (((0,), (0,)), ((), ())), preferred_element_type=jnp.float32
    )


def contract_cols(left_side, right_side):
    return lax.dot_general(
        left_side, right_side, (((1,), (1,)), ((), ())), preferred_element_type=jnp.float32
    )


MESH_ID = pl.DeviceIdType.MESH
ROW_TILE = 16


def shard_stages(count):
    inner = 2 if count <= 16 else 4
    return (inner, 2, count // (2 * inner))


def scatter_kernel(stages, part_ref, total_ref, *scratch):
    in_one, sum_one, in_two, sum_two, in_three = scratch[:5]
    send_one, recv_one, send_two, recv_two, send_three, recv_three = scratch[5:]
    n1, n2, n3 = stages
    rows = total_ref.shape[0]
    me = lax.axis_index("shard")
    seq = lax.axis_index("seq")
    c = lax.rem(me, n1)
    y = lax.rem(me // n1, n2)
    z = me // (n1 * n2)

    def device(z_to, y_to, c_to):
        return (seq, (z_to * n2 + y_to) * n1 + c_to)

    barrier = pltpu.get_barrier_semaphore()
    for j in range(1, n1):
        pl.semaphore_signal(
            barrier, 1, device_id=device(z, y, lax.rem(c + j, n1)), device_id_type=MESH_ID
        )
    for j in range(1, n2):
        pl.semaphore_signal(
            barrier, 1, device_id=device(z, lax.rem(y + j, n2), c), device_id_type=MESH_ID
        )
    for j in range(1, n3):
        pl.semaphore_signal(
            barrier, 1, device_id=device(lax.rem(z + j, n3), y, c), device_id_type=MESH_ID
        )
    pl.semaphore_wait(barrier, n1 + n2 + n3 - 3)

    first, second, third = [], [], []
    for k in range(n3):
        z_to = lax.rem(z + k + 1, n3)
        copies = []
        for j in range(1, n1):
            c_to = lax.rem(c + j, n1)
            slot = n1 - 1 - j
            copy = pltpu.make_async_remote_copy(
                src_ref=part_ref.at[z_to, :, c_to],
                dst_ref=in_one.at[k, slot],
                send_sem=send_one.at[k, j - 1],
                recv_sem=recv_one.at[k, slot],
                device_id=device(z, y, c_to),
                device_id_type=MESH_ID,
            )
            copy.start()
            copies.append(copy)
        first.append(copies)

    def fold_one(k):
        z_to = lax.rem(z + k + 1, n3)
        for copy in first[k]:
            copy.wait_recv()

        def step(i, carry):
            at = pl.ds(pl.multiple_of(i * ROW_TILE, ROW_TILE), ROW_TILE)
            for y_to in range(n2):
                value = part_ref[z_to, y_to, c, at, :].astype(jnp.float32)
                for slot in range(n1 - 1):
                    value += in_one[k, slot, y_to, at, :].astype(jnp.float32)
                sum_one[k, y_to, at, :] = value.astype(sum_one.dtype)
            return carry

        lax.fori_loop(0, rows // ROW_TILE, step, 0)
        copies = []
        for j in range(1, n2):
            y_to = lax.rem(y + j, n2)
            slot = n2 - 1 - j
            copy = pltpu.make_async_remote_copy(
                src_ref=sum_one.at[k, y_to],
                dst_ref=in_two.at[k, slot],
                send_sem=send_two.at[k, j - 1],
                recv_sem=recv_two.at[k, slot],
                device_id=device(z, y_to, c),
                device_id_type=MESH_ID,
            )
            copy.start()
            copies.append(copy)
        second.append(copies)

    def fold_two(k):
        for copy in second[k]:
            copy.wait_recv()

        def step(i, carry):
            at = pl.ds(pl.multiple_of(i * ROW_TILE, ROW_TILE), ROW_TILE)
            value = sum_one[k, y, at, :].astype(jnp.float32)
            for slot in range(n2 - 1):
                value += in_two[k, slot, at, :].astype(jnp.float32)
            sum_two[k, at, :] = value.astype(sum_two.dtype)
            return carry

        lax.fori_loop(0, rows // ROW_TILE, step, 0)
        if k < n3 - 1:
            slot = n3 - 2 - k
            copy = pltpu.make_async_remote_copy(
                src_ref=sum_two.at[k],
                dst_ref=in_three.at[slot],
                send_sem=send_three.at[k],
                recv_sem=recv_three.at[slot],
                device_id=device(lax.rem(z + k + 1, n3), y, c),
                device_id_type=MESH_ID,
            )
            copy.start()
            third.append(copy)

    for k in range(n3 + 1):
        if k < n3:
            fold_one(k)
        if k > 0:
            fold_two(k - 1)
    for copy in third:
        copy.wait_recv()

    def finish(i, carry):
        at = pl.ds(pl.multiple_of(i * ROW_TILE, ROW_TILE), ROW_TILE)
        value = sum_two[n3 - 1, at, :].astype(jnp.float32)
        for slot in range(n3 - 1):
            value += in_three[slot, at, :].astype(jnp.float32)
        total_ref[at, :] = value.astype(total_ref.dtype)
        return carry

    lax.fori_loop(0, rows // ROW_TILE, finish, 0)
    for copies in first + second:
        for copy in copies:
            copy.wait_send()
    for copy in third:
        copy.wait_send()


def scatter_sum(part, collective_id, out_dtype):
    count, rows, cols = part.shape
    stages = shard_stages(count)
    n1, n2, n3 = stages
    low = part.dtype
    return pl.pallas_call(
        functools.partial(scatter_kernel, stages),
        out_shape=jax.ShapeDtypeStruct((rows, cols), out_dtype),
        in_specs=[pl.BlockSpec(memory_space=pltpu.VMEM)],
        out_specs=pl.BlockSpec(memory_space=pltpu.VMEM),
        scratch_shapes=[
            pltpu.VMEM((n3, n1 - 1, n2, rows, cols), low),
            pltpu.VMEM((n3, n2, rows, cols), low),
            pltpu.VMEM((n3, n2 - 1, rows, cols), low),
            pltpu.VMEM((n3, rows, cols), low),
            pltpu.VMEM((n3 - 1, rows, cols), low),
            pltpu.SemaphoreType.DMA((n3, n1 - 1)),
            pltpu.SemaphoreType.DMA((n3, n1 - 1)),
            pltpu.SemaphoreType.DMA((n3, n2 - 1)),
            pltpu.SemaphoreType.DMA((n3, n2 - 1)),
            pltpu.SemaphoreType.DMA((n3 - 1,)),
            pltpu.SemaphoreType.DMA((n3 - 1,)),
        ],
        compiler_params=pltpu.CompilerParams(
            collective_id=collective_id,
            has_side_effects=True,
            vmem_limit_bytes=60 * 1024 * 1024,
        ),
        name="scatter_sum_%d" % collective_id,
    )(part.reshape(n3, n2, n1, rows, cols))


def pair_tables(expert_list, prob_list, expert_count):
    numbers = jnp.arange(expert_count, dtype=jnp.int32)
    named = expert_list[None, :, :] == numbers[:, None, None]
    return jnp.sum(jnp.where(named, prob_list[None], 0.0), axis=2)


def shards(
    layer_input,
    seq_lengths,
    seq_order,
    expert_ids,
    expert_probs,
    weight_qkv,
    weight_out,
    norm_gains,
    weight_gate,
    weight_up,
    weight_down,
    out_cotangent,
):
    width = layer_input.shape[-1]
    tok_rows = layer_input.shape[1]
    seq_count = lax.axis_size("seq")
    seq_at = lax.axis_index("seq")
    group_tok = tok_rows * seq_count
    experts = lax.axis_size("shard")
    shard_at = lax.axis_index("shard")
    top_count = expert_ids.shape[-1]
    capacity = min(tok_rows, 3 * tok_rows * top_count // (2 * experts))
    weight_rows = weight_qkv.shape[0]
    heads_local = HEADS // seq_count
    local_width = heads_local * HEAD_DIM
    out_cols = width // seq_count
    score_scale = HEAD_DIM ** (-0.5)
    low = jnp.bfloat16
    f32 = jnp.float32

    def take_seq(array, axis):
        return lax.dynamic_index_in_dim(array, seq_at, axis, keepdims=False)

    own_cols = take_seq(weight_qkv.reshape(weight_rows, 3, seq_count, local_width), 2)
    qkv_cols = lax.all_gather(
        own_cols.reshape(weight_rows, 3 * local_width), "shard", axis=0, tiled=True
    )
    gain_cols = lax.all_gather(norm_gains, "shard", axis=0, tiled=True).astype(f32)
    group_in = lax.all_gather(layer_input[0], "seq", axis=0, tiled=True).astype(f32)
    table = pair_tables(expert_ids[0], expert_probs[0], experts)
    full_out = lax.all_gather(weight_out, "shard", axis=0, tiled=True)
    grad_all = lax.all_gather(out_cotangent[0], "shard", axis=0, tiled=False)
    tables_all = lax.all_gather(table, "shard", axis=0, tiled=False)
    pair_weight = lax.dynamic_index_in_dim(tables_all, shard_at, 1, keepdims=False)

    segment, position = group_layout(seq_lengths[0], seq_order[0], group_tok)
    places = jnp.arange(group_tok, dtype=jnp.int32)
    allowed = (segment[:, None] == segment[None, :]) & (places[None, :] <= places[:, None])
    cosine, sine_part = rope_tables(position, HEAD_DIM)

    def rope(values):
        return rotate(
            values.reshape(group_tok, heads_local, HEAD_DIM), cosine, sine_part
        ).reshape(group_tok, local_width)

    def rope_back(grads):
        return rotate(
            grads.reshape(group_tok, heads_local, HEAD_DIM), cosine, -sine_part
        ).reshape(group_tok, local_width)

    gain_q = lax.dynamic_slice_in_dim(gain_cols[:, 1], seq_at * local_width, local_width)
    gain_k = lax.dynamic_slice_in_dim(gain_cols[:, 2], seq_at * local_width, local_width)

    group_r = lax.rsqrt(jnp.mean(group_in * group_in, axis=-1, keepdims=True) + norm_eps)
    group_n = group_in * group_r
    attn_in = (group_n * gain_cols[:, 0]).astype(low)
    projected = jnp.dot(attn_in, qkv_cols, preferred_element_type=f32)
    q_raw = projected[:, :local_width]
    k_raw = projected[:, local_width : 2 * local_width]
    value = projected[:, 2 * local_width :].astype(low)
    squares = jnp.stack([jnp.sum(q_raw * q_raw, axis=-1), jnp.sum(k_raw * k_raw, axis=-1)])
    squares = lax.psum(squares, "seq")
    q_r, k_r = (lax.rsqrt(row / width + norm_eps)[:, None] for row in squares)
    q_n = q_raw * q_r
    k_n = k_raw * k_r
    query = rope(q_n * gain_q).astype(low)
    key = rope(k_n * gain_k).astype(low)
    query_head = query.reshape(group_tok, heads_local, HEAD_DIM)
    key_head = key.reshape(group_tok, heads_local, HEAD_DIM)
    value_head = value.reshape(group_tok, heads_local, HEAD_DIM)
    scores = jnp.einsum("ihd,jhd->hij", query_head, key_head, preferred_element_type=f32)
    scores = jnp.where(allowed[None], scores * score_scale, -1e30)
    score_peak = jnp.max(scores, axis=-1, keepdims=True)
    weights_exp = jnp.exp(scores - score_peak)
    attn_probs = weights_exp / jnp.sum(weights_exp, axis=-1, keepdims=True)
    probs_low = attn_probs.astype(low)
    mix_head = jnp.einsum("hij,jhd->ihd", probs_low, value_head, preferred_element_type=f32)
    mix_head = mix_head.astype(low).reshape(group_tok, local_width)
    attn_mix = lax.all_to_all(mix_head, "seq", split_axis=0, concat_axis=1, tiled=True)
    mix_all = lax.all_gather(mix_head, "seq", axis=1, tiled=True)
    resid = layer_input[0].astype(f32) + jnp.dot(attn_mix, full_out, preferred_element_type=f32)
    ffn_r = lax.rsqrt(jnp.mean(resid * resid, axis=-1, keepdims=True) + norm_eps)
    ffn_n = resid * ffn_r
    ffn_in = (ffn_n * gain_cols[:, 3]).astype(low)

    ffn_all = lax.all_gather(ffn_in, "shard", axis=0, tiled=False)
    named = pair_weight > 0.0
    rank = jnp.cumsum(named.astype(jnp.int32), axis=1) - 1
    slots = jnp.arange(capacity, dtype=jnp.int32)
    pick = (rank[:, None, :] == slots[None, :, None]) & named[:, None, :]
    pick_low = pick.astype(low)
    slot_weight = jnp.sum(jnp.where(pick, pair_weight[:, None, :], 0.0), axis=2)

    def gather_rows(rows):
        return jnp.einsum("brt,btd->brd", pick_low, rows, preferred_element_type=f32)

    def spread_rows(rows):
        return jnp.einsum(
            "brt,brd->btd",
            pick_low,
            rows.reshape(experts, capacity, width),
            preferred_element_type=f32,
        )

    gate_weight = weight_gate[0]
    up_weight = weight_up[0]
    down_weight = weight_down[0]
    rows_in = gather_rows(ffn_all).astype(low).reshape(-1, width)
    gate = jnp.dot(rows_in, gate_weight, preferred_element_type=f32)
    up = jnp.dot(rows_in, up_weight, preferred_element_type=f32)
    sigma = jax.nn.sigmoid(gate)
    silu = gate * sigma
    hidden = (silu * up).astype(low)
    d_expert = (gather_rows(grad_all) * slot_weight[:, :, None]).astype(low).reshape(-1, width)
    d_hidden = contract_cols(d_expert, down_weight)
    d_gate = (d_hidden * up * sigma * (1.0 + gate * (1.0 - sigma))).astype(low)
    d_up = (d_hidden * silu).astype(low)
    d_pair = (contract_cols(d_gate, gate_weight) + contract_cols(d_up, up_weight)).astype(low)
    d_ffn_in = scatter_sum(spread_rows(d_pair).astype(low), 1, f32)

    expert_out = jnp.dot(hidden, down_weight, preferred_element_type=f32).astype(low)
    out_part = (spread_rows(expert_out) * pair_weight[:, :, None]).astype(low)
    mixed_out = scatter_sum(out_part, 2, f32)
    layer_output = (resid + mixed_out).astype(low)
    part_down = contract_rows(hidden, d_expert).astype(low)
    part_gate = contract_rows(rows_in, d_gate).astype(low)
    part_up = contract_rows(rows_in, d_up).astype(low)
    sum_gate, sum_up, sum_down = (
        lax.psum_scatter(part, "seq", scatter_dimension=0, tiled=True).astype(f32)
        for part in (part_gate, part_up, part_down)
    )

    grad_tokens = out_cotangent[0].astype(f32)
    d_scaled = d_ffn_in * gain_cols[:, 3]
    d_resid = grad_tokens + ffn_r * (
        d_scaled - ffn_n * jnp.mean(d_scaled * ffn_n, axis=-1, keepdims=True)
    )
    grad_g_ffn = jnp.sum(d_ffn_in * ffn_n, axis=0)
    d_branch = d_resid.astype(low)
    d_mix = contract_cols(d_branch, full_out).astype(low)
    d_mix_head = lax.all_to_all(d_mix, "seq", split_axis=1, concat_axis=0, tiled=True).reshape(
        group_tok, heads_local, HEAD_DIM
    )
    branch_cols = lax.all_to_all(d_branch, "seq", split_axis=1, concat_axis=0, tiled=True)
    d_probs = jnp.einsum("ihd,jhd->hij", d_mix_head, value_head, preferred_element_type=f32)
    delta_rows = jnp.sum(attn_probs * d_probs, axis=-1, keepdims=True)
    d_scores = (attn_probs * (d_probs - delta_rows)).astype(low)
    d_query = (
        jnp.einsum("hij,jhd->ihd", d_scores, key_head, preferred_element_type=f32) * score_scale
    ).astype(low)
    d_key = (
        jnp.einsum("hij,ihd->jhd", d_scores, query_head, preferred_element_type=f32) * score_scale
    ).astype(low)
    d_value = jnp.einsum(
        "hij,ihd->jhd", probs_low, d_mix_head, preferred_element_type=f32
    ).astype(low)
    dq_rot = rope_back(d_query.reshape(group_tok, local_width).astype(f32))
    dk_rot = rope_back(d_key.reshape(group_tok, local_width).astype(f32))
    grad_g_q = jnp.sum(dq_rot * q_n, axis=0)
    grad_g_k = jnp.sum(dk_rot * k_n, axis=0)
    dq_scaled = dq_rot * gain_q
    dk_scaled = dk_rot * gain_k
    dots = jnp.stack([jnp.sum(dq_scaled * q_n, axis=-1), jnp.sum(dk_scaled * k_n, axis=-1)])
    dots = lax.psum(dots, "seq") / width
    dq_raw = q_r * (dq_scaled - q_n * dots[0][:, None])
    dk_raw = k_r * (dk_scaled - k_n * dots[1][:, None])
    d_qkv = jnp.concatenate(
        [dq_raw.astype(low), dk_raw.astype(low), d_value.reshape(group_tok, local_width)], axis=1
    )
    d_attn_part = contract_cols(d_qkv, qkv_cols).astype(low)
    d_attn_in = lax.psum_scatter(d_attn_part, "seq", scatter_dimension=0, tiled=True).astype(f32)
    own_n = lax.dynamic_slice_in_dim(group_n, seq_at * tok_rows, tok_rows)
    own_r = lax.dynamic_slice_in_dim(group_r, seq_at * tok_rows, tok_rows)
    dx_scaled = d_attn_in * gain_cols[:, 0]
    dx_norm = own_r * (dx_scaled - own_n * jnp.mean(dx_scaled * own_n, axis=-1, keepdims=True))
    grad_g_attn = jnp.sum(d_attn_in * own_n, axis=0)
    input_grad = (d_resid + dx_norm).astype(low)

    term_qkv = contract_rows(attn_in, d_qkv).astype(low)
    term_out = contract_rows(mix_all, branch_cols).astype(low)
    terms = jnp.concatenate([term_qkv, term_out], axis=1).reshape(experts, weight_rows, -1)
    sums = scatter_sum(terms, 3, low)
    sums_all = lax.all_gather(sums, "seq", axis=0, tiled=False).astype(f32)
    rows_qkv = (
        sums_all[:, :, : 3 * local_width]
        .reshape(seq_count, weight_rows, 3, local_width)
        .transpose(1, 2, 0, 3)
        .reshape(weight_rows, 3 * width)
    )
    rows_out = sums_all[:, :, 3 * local_width :].transpose(1, 0, 2).reshape(weight_rows, width)
    zeros = jnp.zeros((width,), f32)
    gain_terms = jnp.stack(
        [
            grad_g_attn,
            lax.dynamic_update_slice_in_dim(zeros, grad_g_q, seq_at * local_width, 0),
            lax.dynamic_update_slice_in_dim(zeros, grad_g_k, seq_at * local_width, 0),
            grad_g_ffn,
        ]
    )
    gain_terms = lax.psum(gain_terms, ("seq", "shard"))
    rows_gain = lax.dynamic_slice_in_dim(gain_terms, shard_at * weight_rows, weight_rows, 1).T
    return (
        layer_output[None],
        input_grad[None],
        rows_qkv,
        rows_out,
        rows_gain,
        sum_gate[None],
        sum_up[None],
        sum_down[None],
    )


def solution(mesh):
    in_specs = (
        P("shard", "seq", None),
        P("shard", None),
        P("shard", None),
        P("shard", "seq", None),
        P("shard", "seq", None),
        P("shard", None),
        P("shard", None),
        P("shard", None),
        P("shard", None, None),
        P("shard", None, None),
        P("shard", None, None),
        P("shard", "seq", None),
    )
    out_specs = (
        P("shard", "seq", None),
        P("shard", "seq", None),
        P("shard", None),
        P("shard", None),
        P("shard", None),
        P("shard", "seq", None),
        P("shard", "seq", None),
        P("shard", "seq", None),
    )
    return jax.shard_map(shards, mesh=mesh, in_specs=in_specs, out_specs=out_specs, check_vma=False)
```

```python
import functools

import jax
import jax.numpy as jnp
from jax import lax
from jax.experimental import pallas as pl
from jax.experimental.pallas import tpu as pltpu
from jax.sharding import PartitionSpec as P

HEADS = 16
HEAD_DIM = 128


norm_eps = 1e-05
rope_base = 10000.0


def rms_scale(values, gain_col):
    return (
        values * lax.rsqrt(jnp.mean(values * values, axis=-1, keepdims=True) + norm_eps) * gain_col
    )


def rotate(values, cosine, sine_part):
    half_dim = values.shape[-1] // 2
    first_half = values[..., :half_dim]
    second_half = values[..., half_dim:]
    return jnp.concatenate(
        [
            first_half * cosine - second_half * sine_part,
            second_half * cosine + first_half * sine_part,
        ],
        axis=-1,
    )


def rope_tables(position, head_size):
    half_dim = head_size // 2
    frequency = rope_base ** (-2.0 * jnp.arange(half_dim, dtype=jnp.float32) / head_size)
    angles = position.astype(jnp.float32)[:, None] * frequency[None, :]
    return (jnp.cos(angles)[:, None, :], jnp.sin(angles)[:, None, :])


def group_layout(lengths, seq_perm, group_tok):
    seq_count = lengths.shape[0]
    numbers = jnp.arange(seq_count, dtype=jnp.int32)
    packed = jnp.sum(jnp.where(seq_perm[:, None] == numbers[None, :], lengths[None, :], 0), axis=1)
    seq_ends = jnp.cumsum(packed)
    seq_starts = seq_ends - packed
    places = jnp.arange(group_tok, dtype=jnp.int32)
    segment = jnp.sum((places[:, None] >= seq_ends[None, :]).astype(jnp.int32), axis=1)
    begins = jnp.sum(
        jnp.where(segment[:, None] == numbers[None, :], seq_starts[None, :], 0), axis=1
    )
    return (segment, places - begins)


def contract_rows(left_side, right_side):
    return lax.dot_general(
        left_side, right_side, (((0,), (0,)), ((), ())), preferred_element_type=jnp.float32
    )


def contract_cols(left_side, right_side):
    return lax.dot_general(
        left_side, right_side, (((1,), (1,)), ((), ())), preferred_element_type=jnp.float32
    )


MESH_ID = pl.DeviceIdType.MESH
VMEM_LIMIT = 60 * 1024 * 1024
ROW_TILE = 16


def low_bit(index):
    return index & -index


def bit_list(count):
    return [1 << b for b in range(count.bit_length() - 1)]


def relative_place(count, me):
    values = [(bit, lax.rem(me // bit, 2)) for bit in bit_list(count)]

    def place(r):
        total = 0
        for bit, value in values:
            total = total + bit * ((1 - value) if r & bit else value)
        return total

    return place


def meet(count, place, seq, seq_count=1):
    barrier = pltpu.get_barrier_semaphore()
    for bit in bit_list(count):
        pl.semaphore_signal(barrier, 1, device_id=(seq, place(bit)), device_id_type=MESH_ID)
    for j in range(1, seq_count):
        pl.semaphore_signal(
            barrier, 1, device_id=(lax.rem(seq + j, seq_count), place(0)), device_id_type=MESH_ID
        )
    pl.semaphore_wait(barrier, len(bit_list(count)) + seq_count - 1)


def remote(src, dst, send_sem, recv_sem, device):
    return pltpu.make_async_remote_copy(
        src_ref=src,
        dst_ref=dst,
        send_sem=send_sem,
        recv_sem=recv_sem,
        device_id=device,
        device_id_type=MESH_ID,
    )


def arrival_order(count):
    def key(r):
        later = r >> 2
        return (later + ((r >> 1) & 1), (r >> 1) & 1)

    return sorted(range(2, count, 2), key=key)


def gather_kernel(count, groups, *refs):
    arrays = sum(len(group) for group in groups)
    own, full = refs[:arrays], refs[arrays : 2 * arrays]
    send, recv, local = refs[2 * arrays :]
    me = lax.axis_index("shard")
    seq = lax.axis_index("seq")
    place = relative_place(count, me)
    meet(count, place, seq)
    copies = {}

    def send_on(a, r):
        source = own[a] if r == 0 else full[a].at[place(r)]
        below = low_bit(r) if r else count
        for bit in reversed(bit_list(count)):
            if bit < below:
                copy = remote(
                    source,
                    full[a].at[place(r)],
                    send.at[a, r | bit],
                    recv.at[a, r | bit],
                    (seq, place(bit)),
                )
                copies[a, r | bit] = copy

    def start(a, r):
        send_on(a, r)
        below = low_bit(r) if r else count
        bits = [bit for bit in bit_list(count) if bit < below]
        for bit in sorted(bits, key=lambda bit: (bit < 4, bit)):
            copies[a, r | bit].start()

    keeps = []
    for a in range(arrays):
        keep = pltpu.make_async_copy(own[a], full[a].at[me], local.at[a])
        keep.start()
        keeps.append(keep)
    arrivals = arrival_order(count)
    last = max(i for i, r in enumerate(arrivals) if not r & 2) + 1
    events = [(0, 0)]
    for g in range(len(groups)):
        events += [(g, r) for r in arrivals[:last]]
        if g + 1 < len(groups):
            events.append((g + 1, 0))
        events += [(g, r) for r in arrivals[last:]]
    for g, r in events:
        for a in groups[g]:
            if r:
                copies[a, r].wait_recv()
            start(a, r)
    for a in range(arrays):
        for r in range(1, count, 2):
            copies[a, r].wait_recv()
    for copy in copies.values():
        copy.wait_send()
    for keep in keeps:
        keep.wait()


def gather_blocks(blocks, collective_id, groups=((0,),)):
    count = lax.axis_size("shard")
    arrays = len(blocks)
    return pl.pallas_call(
        functools.partial(gather_kernel, count, groups),
        out_shape=[jax.ShapeDtypeStruct((count,) + b.shape, b.dtype) for b in blocks],
        in_specs=[pl.BlockSpec(memory_space=pltpu.VMEM)] * arrays,
        out_specs=[pl.BlockSpec(memory_space=pl.ANY)] * arrays,
        scratch_shapes=[
            pltpu.SemaphoreType.DMA((arrays, count)),
            pltpu.SemaphoreType.DMA((arrays, count)),
            pltpu.SemaphoreType.DMA((arrays,)),
        ],
        compiler_params=pltpu.CompilerParams(collective_id=collective_id, has_side_effects=True),
        name="gather_blocks_%d" % collective_id,
    )(*blocks)


def scatter_kernel(count, seq_count, arrays, sides, *refs):
    parts, refs = refs[:arrays], refs[arrays:]
    side_from, refs = refs[:sides], refs[sides:]
    totals, refs = refs[:arrays], refs[arrays:]
    side_to, refs = refs[:sides], refs[sides:]
    held = refs[:arrays]
    send, recv, seq_send, seq_recv, side_send, side_recv = refs[arrays:]
    planes = seq_count if seq_count > 1 else 1 + (sides > 0)
    me = lax.axis_index("shard")
    seq = lax.axis_index("seq")
    place = relative_place(count, me)
    bits = bit_list(count)
    meet(count, place, seq, planes)
    copies = {}
    shared = []
    for i in range(sides):
        half = side_to[i].shape[0]
        copy = remote(
            side_from[i].at[pl.ds(pl.multiple_of((1 - seq) * half, half), half)],
            side_to[i],
            side_send.at[i],
            side_recv.at[i],
            (1 - seq, me),
        )
        copy.start()
        shared.append(copy)

    def share(a):
        for j in range(1, seq_count):
            copy = remote(
                totals[a].at[seq],
                totals[a].at[seq],
                seq_send.at[a, j - 1],
                seq_recv.at[a, j - 1],
                (lax.rem(seq + j, seq_count), me),
            )
            copy.start()
            shared.append(copy)

    def start(a, r, source):
        copy = remote(
            source, held[a].at[r], send.at[a, r], recv.at[a, r], (seq, place(low_bit(r)))
        )
        copy.start()
        copies[a, r] = copy

    def fold(a, r, bit):
        came = r | bit
        copies[a, came].wait_recv()
        rows = held[a].shape[1]
        last = bit == bits[-1]

        def step(i, carry):
            at = pl.ds(pl.multiple_of(i * ROW_TILE, ROW_TILE), ROW_TILE)
            if bit == 1:
                mine = parts[a][place(r), at, :]
            else:
                mine = held[a][r | (bit >> 1), at, :]
            value = mine.astype(jnp.float32) + held[a][came, at, :].astype(jnp.float32)
            if last and seq_count > 1:
                totals[a][seq, at, :] = value.astype(totals[a].dtype)
            elif last:
                totals[a][at, :] = value.astype(totals[a].dtype)
            else:
                held[a][came, at, :] = value.astype(held[a].dtype)
            return carry

        lax.fori_loop(0, rows // ROW_TILE, step, 0)
        upper = bit << 1
        if last:
            share(a)
        elif r & upper:
            start(a, r, held[a].at[came])

    def reversed_bits(u):
        return sum(1 << (len(bits) - 3 - b) for b in range(len(bits) - 2) if u >> b & 1)

    order = sorted(range(count // 4), key=reversed_bits, reverse=True)
    chunks = [(a, u) for a in range(arrays) for u in order]
    for a, u in chunks:
        for r in (4 * u + 3, 4 * u + 1):
            start(a, r, parts[a].at[place(r)])
    for i in range(len(chunks) + len(bits) - 1):
        for stage in range(len(bits)):
            bit = bits[stage]
            at = i - max(stage, 0)
            if 0 <= at < len(chunks):
                a, u = chunks[at]
                if stage == 0:
                    fold(a, 4 * u + 2, bit)
                    fold(a, 4 * u, bit)
                elif stage == 1 or 4 * u % (2 * bit) == 0:
                    fold(a, 4 * u, bit)
    for copy in shared:
        copy.wait_recv()
    for copy in list(copies.values()) + shared:
        copy.wait_send()


def scatter_sum(parts, collective_id, out_dtype, seq_count=1, sides=()):
    count = lax.axis_size("shard")
    arrays = len(parts)
    lead = (seq_count,) if seq_count > 1 else ()
    others = max(seq_count - 1, 1)
    return pl.pallas_call(
        functools.partial(scatter_kernel, count, seq_count, arrays, len(sides)),
        out_shape=[jax.ShapeDtypeStruct(lead + p.shape[1:], out_dtype) for p in parts]
        + [jax.ShapeDtypeStruct((s.shape[0] // 2, s.shape[1]), s.dtype) for s in sides],
        in_specs=[pl.BlockSpec(memory_space=pltpu.VMEM)] * arrays
        + [pl.BlockSpec(memory_space=pl.ANY)] * len(sides),
        out_specs=[pl.BlockSpec(memory_space=pltpu.VMEM)] * arrays
        + [pl.BlockSpec(memory_space=pl.ANY)] * len(sides),
        scratch_shapes=[pltpu.VMEM(p.shape, p.dtype) for p in parts]
        + [
            pltpu.SemaphoreType.DMA((arrays, count)),
            pltpu.SemaphoreType.DMA((arrays, count)),
            pltpu.SemaphoreType.DMA((arrays, others)),
            pltpu.SemaphoreType.DMA((arrays, others)),
            pltpu.SemaphoreType.DMA((max(len(sides), 1),)),
            pltpu.SemaphoreType.DMA((max(len(sides), 1),)),
        ],
        compiler_params=pltpu.CompilerParams(
            collective_id=collective_id, has_side_effects=True, vmem_limit_bytes=VMEM_LIMIT
        ),
        name="scatter_sum_%d" % collective_id,
    )(*parts, *sides)


def place_kernel(refs_in, seq_count, *refs):
    for i, o in enumerate(refs_in):
        out_ref, base = refs[len(refs_in) + o[0]], o[1]
        cols = refs[i].shape[2]
        for s in range(seq_count):
            out_ref[:, base + s * cols : base + (s + 1) * cols] = refs[i][s].astype(out_ref.dtype)


def place_rows(pieces, targets, out_cols):
    seq_count, rows, _ = pieces[0].shape
    return pl.pallas_call(
        functools.partial(place_kernel, targets, seq_count),
        out_shape=[jax.ShapeDtypeStruct((rows, cols), jnp.float32) for cols in out_cols],
        in_specs=[pl.BlockSpec(memory_space=pltpu.VMEM)] * len(pieces),
        out_specs=[pl.BlockSpec(memory_space=pltpu.VMEM)] * len(out_cols),
        name="place_rows",
    )(*pieces)


GAIN_LANES = 128


def pair_tables(expert_list, prob_list, expert_count):
    numbers = jnp.arange(expert_count, dtype=jnp.int32)
    named = expert_list[None, :, :] == numbers[:, None, None]
    return jnp.sum(jnp.where(named, prob_list[None], 0.0), axis=2)


def shards(
    layer_input,
    seq_lengths,
    seq_order,
    expert_ids,
    expert_probs,
    weight_qkv,
    weight_out,
    norm_gains,
    weight_gate,
    weight_up,
    weight_down,
    out_cotangent,
):
    width = layer_input.shape[-1]
    tok_rows = layer_input.shape[1]
    seq_count = lax.axis_size("seq")
    seq_at = lax.axis_index("seq")
    group_tok = tok_rows * seq_count
    experts = lax.axis_size("shard")
    shard_at = lax.axis_index("shard")
    top_count = expert_ids.shape[-1]
    capacity = min(tok_rows, 3 * tok_rows * top_count // (2 * experts))
    weight_rows = weight_qkv.shape[0]
    heads_local = HEADS // seq_count
    local_width = heads_local * HEAD_DIM
    out_cols = width // seq_count
    score_scale = HEAD_DIM ** (-0.5)
    low = jnp.bfloat16
    f32 = jnp.float32

    def take_seq(array, axis):
        return lax.dynamic_index_in_dim(array, seq_at, axis, keepdims=False)

    def seq_sum(part):
        if seq_count != 2:
            return lax.psum_scatter(part, "seq", scatter_dimension=0, tiled=True).astype(f32)
        halves = part.reshape(2, part.shape[0] // 2, part.shape[1])
        there = lax.dynamic_index_in_dim(halves, 1 - seq_at, 0, keepdims=False)
        here = lax.dynamic_index_in_dim(halves, seq_at, 0, keepdims=False)
        came = lax.ppermute(there, "seq", [(0, 1), (1, 0)])
        return here.astype(f32) + came.astype(f32)

    own_cols = take_seq(weight_qkv.reshape(weight_rows, 3, seq_count, local_width), 2)
    own_gains = jnp.pad(norm_gains, ((0, 0), (0, GAIN_LANES - norm_gains.shape[1])))
    table = pair_tables(expert_ids[0], expert_probs[0], experts)
    own_block = jnp.concatenate(
        [own_cols.reshape(weight_rows, 3 * local_width), own_gains], axis=1
    )
    qkv_cols, full_out, tables_all = gather_blocks(
        [own_block, weight_out, table], 1, ((0,), (1, 2))
    )
    own_grad, qkv_cols = lax.optimization_barrier((out_cotangent[0], qkv_cols))
    grad_all = lax.all_gather(own_grad, "shard", axis=0, tiled=False)
    qkv_cols = qkv_cols.reshape(width, 3 * local_width + GAIN_LANES)
    gain_cols = qkv_cols[:, 3 * local_width :][:, : norm_gains.shape[1]].astype(f32)
    qkv_cols = qkv_cols[:, : 3 * local_width]
    full_out = full_out.reshape(width, width)
    group_in = lax.all_gather(layer_input[0], "seq", axis=0, tiled=True).astype(f32)
    pair_weight = lax.dynamic_index_in_dim(tables_all, shard_at, 1, keepdims=False)

    segment, position = group_layout(seq_lengths[0], seq_order[0], group_tok)
    places = jnp.arange(group_tok, dtype=jnp.int32)
    allowed = (segment[:, None] == segment[None, :]) & (places[None, :] <= places[:, None])
    cosine, sine_part = rope_tables(position, HEAD_DIM)

    def rope(values):
        return rotate(
            values.reshape(group_tok, heads_local, HEAD_DIM), cosine, sine_part
        ).reshape(group_tok, local_width)

    def rope_back(grads):
        return rotate(
            grads.reshape(group_tok, heads_local, HEAD_DIM), cosine, -sine_part
        ).reshape(group_tok, local_width)

    gain_q = lax.dynamic_slice_in_dim(gain_cols[:, 1], seq_at * local_width, local_width)
    gain_k = lax.dynamic_slice_in_dim(gain_cols[:, 2], seq_at * local_width, local_width)

    group_r = lax.rsqrt(jnp.mean(group_in * group_in, axis=-1, keepdims=True) + norm_eps)
    group_n = group_in * group_r
    attn_in = (group_n * gain_cols[:, 0]).astype(low)
    projected = jnp.dot(attn_in, qkv_cols, preferred_element_type=f32)
    q_raw = projected[:, :local_width]
    k_raw = projected[:, local_width : 2 * local_width]
    value = projected[:, 2 * local_width :].astype(low)
    squares = jnp.stack([jnp.sum(q_raw * q_raw, axis=-1), jnp.sum(k_raw * k_raw, axis=-1)])
    squares = lax.psum(squares, "seq")
    q_r, k_r = (lax.rsqrt(row / width + norm_eps)[:, None] for row in squares)
    q_n = q_raw * q_r
    k_n = k_raw * k_r
    query = rope(q_n * gain_q).astype(low)
    key = rope(k_n * gain_k).astype(low)
    query_head = query.reshape(group_tok, heads_local, HEAD_DIM)
    key_head = key.reshape(group_tok, heads_local, HEAD_DIM)
    value_head = value.reshape(group_tok, heads_local, HEAD_DIM)
    scores = jnp.einsum("ihd,jhd->hij", query_head, key_head, preferred_element_type=f32)
    scores = jnp.where(allowed[None], scores * score_scale, -1e30)
    score_peak = jnp.max(scores, axis=-1, keepdims=True)
    weights_exp = jnp.exp(scores - score_peak)
    attn_probs = weights_exp / jnp.sum(weights_exp, axis=-1, keepdims=True)
    probs_low = attn_probs.astype(low)
    mix_head = jnp.einsum("hij,jhd->ihd", probs_low, value_head, preferred_element_type=f32)
    mix_head = mix_head.astype(low).reshape(group_tok, local_width)
    attn_mix = lax.all_to_all(mix_head, "seq", split_axis=0, concat_axis=1, tiled=True)
    mix_all = lax.all_gather(mix_head, "seq", axis=1, tiled=True)
    resid = layer_input[0].astype(f32) + jnp.dot(attn_mix, full_out, preferred_element_type=f32)
    ffn_r = lax.rsqrt(jnp.mean(resid * resid, axis=-1, keepdims=True) + norm_eps)
    ffn_n = resid * ffn_r
    ffn_in = (ffn_n * gain_cols[:, 3]).astype(low)

    (ffn_all,) = gather_blocks([ffn_in], 2)
    named = pair_weight > 0.0
    rank = jnp.cumsum(named.astype(jnp.int32), axis=1) - 1
    slots = jnp.arange(capacity, dtype=jnp.int32)
    pick = (rank[:, None, :] == slots[None, :, None]) & named[:, None, :]
    pick_low = pick.astype(low)
    slot_weight = jnp.sum(jnp.where(pick, pair_weight[:, None, :], 0.0), axis=2)

    def gather_rows(rows):
        return jnp.einsum("brt,btd->brd", pick_low, rows, preferred_element_type=f32)

    def spread_rows(rows):
        return jnp.einsum(
            "brt,brd->btd",
            pick_low,
            rows.reshape(experts, capacity, width),
            preferred_element_type=f32,
        )

    gate_weight = weight_gate[0]
    up_weight = weight_up[0]
    down_weight = weight_down[0]
    rows_in = gather_rows(ffn_all).astype(low).reshape(-1, width)
    gate = jnp.dot(rows_in, gate_weight, preferred_element_type=f32)
    up = jnp.dot(rows_in, up_weight, preferred_element_type=f32)
    sigma = jax.nn.sigmoid(gate)
    silu = gate * sigma
    hidden = (silu * up).astype(low)
    d_expert = (gather_rows(grad_all) * slot_weight[:, :, None]).astype(low).reshape(-1, width)
    d_hidden = contract_cols(d_expert, down_weight)
    d_gate = (d_hidden * up * sigma * (1.0 + gate * (1.0 - sigma))).astype(low)
    d_up = (d_hidden * silu).astype(low)
    d_pair = (contract_cols(d_gate, gate_weight) + contract_cols(d_up, up_weight)).astype(low)
    expert_out = jnp.dot(hidden, down_weight, preferred_element_type=f32).astype(low)
    out_part = (spread_rows(expert_out) * pair_weight[:, :, None]).astype(low)
    part_down = contract_rows(hidden, d_expert).astype(low)
    part_gate = contract_rows(rows_in, d_gate).astype(low)
    part_up = contract_rows(rows_in, d_up).astype(low)
    d_spread = spread_rows(d_pair).astype(low)
    pairs = seq_count == 2
    d_ffn_in, *came_down = scatter_sum([d_spread], 3, f32, sides=[part_down] if pairs else [])
    out_part, d_ffn_in = lax.optimization_barrier((out_part, d_ffn_in))
    mixed_out = lax.psum_scatter(
        out_part.reshape(experts * tok_rows, width), "shard", scatter_dimension=0, tiled=True
    ).astype(f32)
    layer_output = (resid + mixed_out).astype(low)

    grad_tokens = out_cotangent[0].astype(f32)
    d_scaled = d_ffn_in * gain_cols[:, 3]
    d_resid = grad_tokens + ffn_r * (
        d_scaled - ffn_n * jnp.mean(d_scaled * ffn_n, axis=-1, keepdims=True)
    )
    grad_g_ffn = jnp.sum(d_ffn_in * ffn_n, axis=0)
    d_branch = d_resid.astype(low)
    d_mix = contract_cols(d_branch, full_out).astype(low)
    d_mix_head = lax.all_to_all(d_mix, "seq", split_axis=1, concat_axis=0, tiled=True).reshape(
        group_tok, heads_local, HEAD_DIM
    )
    branch_cols = lax.all_to_all(d_branch, "seq", split_axis=1, concat_axis=0, tiled=True)
    d_probs = jnp.einsum("ihd,jhd->hij", d_mix_head, value_head, preferred_element_type=f32)
    delta_rows = jnp.sum(attn_probs * d_probs, axis=-1, keepdims=True)
    d_scores = (attn_probs * (d_probs - delta_rows)).astype(low)
    d_query = (
        jnp.einsum("hij,jhd->ihd", d_scores, key_head, preferred_element_type=f32) * score_scale
    ).astype(low)
    d_key = (
        jnp.einsum("hij,ihd->jhd", d_scores, query_head, preferred_element_type=f32) * score_scale
    ).astype(low)
    d_value = jnp.einsum(
        "hij,ihd->jhd", probs_low, d_mix_head, preferred_element_type=f32
    ).astype(low)
    dq_rot = rope_back(d_query.reshape(group_tok, local_width).astype(f32))
    dk_rot = rope_back(d_key.reshape(group_tok, local_width).astype(f32))
    grad_g_q = jnp.sum(dq_rot * q_n, axis=0)
    grad_g_k = jnp.sum(dk_rot * k_n, axis=0)
    dq_scaled = dq_rot * gain_q
    dk_scaled = dk_rot * gain_k
    dots = jnp.stack([jnp.sum(dq_scaled * q_n, axis=-1), jnp.sum(dk_scaled * k_n, axis=-1)])
    dots = lax.psum(dots, "seq") / width
    dq_raw = q_r * (dq_scaled - q_n * dots[0][:, None])
    dk_raw = k_r * (dk_scaled - k_n * dots[1][:, None])
    d_qkv = jnp.concatenate(
        [dq_raw.astype(low), dk_raw.astype(low), d_value.reshape(group_tok, local_width)], axis=1
    )
    d_attn_in = seq_sum(contract_cols(d_qkv, qkv_cols).astype(low))
    own_n = lax.dynamic_slice_in_dim(group_n, seq_at * tok_rows, tok_rows)
    own_r = lax.dynamic_slice_in_dim(group_r, seq_at * tok_rows, tok_rows)
    dx_scaled = d_attn_in * gain_cols[:, 0]
    dx_norm = own_r * (dx_scaled - own_n * jnp.mean(dx_scaled * own_n, axis=-1, keepdims=True))
    grad_g_attn = jnp.sum(d_attn_in * own_n, axis=0)
    input_grad = (d_resid + dx_norm).astype(low)

    zeros = jnp.zeros((width,), f32)
    gain_terms = jnp.stack(
        [
            grad_g_attn,
            lax.dynamic_update_slice_in_dim(zeros, grad_g_q, seq_at * local_width, 0),
            lax.dynamic_update_slice_in_dim(zeros, grad_g_k, seq_at * local_width, 0),
            grad_g_ffn,
        ],
        axis=1,
    )
    gain_terms = jnp.pad(gain_terms, ((0, 0), (0, GAIN_LANES - gain_terms.shape[1])))
    terms = [
        contract_rows(attn_in, d_qkv[:, i * local_width : (i + 1) * local_width]) for i in range(3)
    ]
    terms += [contract_rows(mix_all, branch_cols), gain_terms]
    terms = [term.astype(low).reshape(experts, weight_rows, -1) for term in terms]
    results = scatter_sum(
        terms, 4, low, seq_count, sides=[part_gate, part_up] if pairs else []
    )
    *sums, sum_gains = results[: len(terms)]
    came = list(results[len(terms) :]) + came_down
    if pairs:
        sum_gate, sum_up, sum_down = (
            lax.dynamic_slice_in_dim(part, seq_at * other.shape[0], other.shape[0]).astype(f32)
            + other.astype(f32)
            for part, other in zip((part_gate, part_up, part_down), came)
        )
    else:
        sum_gate, sum_up, sum_down = (seq_sum(p) for p in (part_gate, part_up, part_down))
    targets = [(0, 0), (0, width), (0, 2 * width), (1, 0)]
    rows_qkv, rows_out = place_rows(sums, targets, (3 * width, width))
    rows_gain = jnp.sum(sum_gains[:, :, : norm_gains.shape[1]].astype(f32), axis=0)
    return (
        layer_output[None],
        input_grad[None],
        rows_qkv,
        rows_out,
        rows_gain,
        sum_gate[None],
        sum_up[None],
        sum_down[None],
    )


def solution(mesh):
    in_specs = (
        P("shard", "seq", None),
        P("shard", None),
        P("shard", None),
        P("shard", "seq", None),
        P("shard", "seq", None),
        P("shard", None),
        P("shard", None),
        P("shard", None),
        P("shard", None, None),
        P("shard", None, None),
        P("shard", None, None),
        P("shard", "seq", None),
    )
    out_specs = (
        P("shard", "seq", None),
        P("shard", "seq", None),
        P("shard", None),
        P("shard", None),
        P("shard", None),
        P("shard", "seq", None),
        P("shard", "seq", None),
        P("shard", "seq", None),
    )
    return jax.shard_map(shards, mesh=mesh, in_specs=in_specs, out_specs=out_specs, check_vma=False)
```

```python
import functools

import jax
import jax.numpy as jnp
from jax import lax
from jax.experimental import pallas as pl
from jax.experimental.pallas import tpu as pltpu
from jax.sharding import PartitionSpec as P

HEADS = 16
HEAD_DIM = 128


norm_eps = 1e-05
rope_base = 10000.0


def rms_scale(values, gain_col):
    return (
        values * lax.rsqrt(jnp.mean(values * values, axis=-1, keepdims=True) + norm_eps) * gain_col
    )


def rotate(values, cosine, sine_part):
    half_dim = values.shape[-1] // 2
    first_half = values[..., :half_dim]
    second_half = values[..., half_dim:]
    return jnp.concatenate(
        [
            first_half * cosine - second_half * sine_part,
            second_half * cosine + first_half * sine_part,
        ],
        axis=-1,
    )


def rope_tables(position, head_size):
    half_dim = head_size // 2
    frequency = rope_base ** (-2.0 * jnp.arange(half_dim, dtype=jnp.float32) / head_size)
    angles = position.astype(jnp.float32)[:, None] * frequency[None, :]
    return (jnp.cos(angles)[:, None, :], jnp.sin(angles)[:, None, :])


def group_layout(lengths, seq_perm, group_tok):
    seq_count = lengths.shape[0]
    numbers = jnp.arange(seq_count, dtype=jnp.int32)
    packed = jnp.sum(jnp.where(seq_perm[:, None] == numbers[None, :], lengths[None, :], 0), axis=1)
    seq_ends = jnp.cumsum(packed)
    seq_starts = seq_ends - packed
    places = jnp.arange(group_tok, dtype=jnp.int32)
    segment = jnp.sum((places[:, None] >= seq_ends[None, :]).astype(jnp.int32), axis=1)
    begins = jnp.sum(
        jnp.where(segment[:, None] == numbers[None, :], seq_starts[None, :], 0), axis=1
    )
    return (segment, places - begins)


def contract_rows(left_side, right_side):
    return lax.dot_general(
        left_side, right_side, (((0,), (0,)), ((), ())), preferred_element_type=jnp.float32
    )


def contract_cols(left_side, right_side):
    return lax.dot_general(
        left_side, right_side, (((1,), (1,)), ((), ())), preferred_element_type=jnp.float32
    )


MESH_ID = pl.DeviceIdType.MESH
VMEM_LIMIT = 60 * 1024 * 1024
ROW_TILE = 16
AHEAD = 2
GRAD_TILE = 256


def low_bit(index):
    return index & -index


def bit_list(count):
    return [1 << b for b in range(count.bit_length() - 1)]


def relative_place(count, me):
    values = [(bit, lax.rem(me // bit, 2)) for bit in bit_list(count)]

    def place(r):
        total = 0
        for bit, value in values:
            total = total + bit * ((1 - value) if r & bit else value)
        return total

    return place


def meet(count, place, seq, seq_count=1):
    barrier = pltpu.get_barrier_semaphore()
    for bit in bit_list(count):
        pl.semaphore_signal(barrier, 1, device_id=(seq, place(bit)), device_id_type=MESH_ID)
    for j in range(1, seq_count):
        pl.semaphore_signal(
            barrier, 1, device_id=(lax.rem(seq + j, seq_count), place(0)), device_id_type=MESH_ID
        )
    pl.semaphore_wait(barrier, len(bit_list(count)) + seq_count - 1)


def remote(src, dst, send_sem, recv_sem, device):
    return pltpu.make_async_remote_copy(
        src_ref=src,
        dst_ref=dst,
        send_sem=send_sem,
        recv_sem=recv_sem,
        device_id=device,
        device_id_type=MESH_ID,
    )


def arrival_order(count):
    def key(r):
        later = r >> 2
        return (later + ((r >> 1) & 1), (r >> 1) & 1)

    return sorted(range(2, count, 2), key=key)


def gather_kernel(count, groups, *refs):
    arrays = sum(len(group) for group in groups)
    own, full = refs[:arrays], refs[arrays : 2 * arrays]
    send, recv, local = refs[2 * arrays :]
    me = lax.axis_index("shard")
    seq = lax.axis_index("seq")
    place = relative_place(count, me)
    meet(count, place, seq)
    copies = {}

    def send_on(a, r):
        source = own[a] if r == 0 else full[a].at[place(r)]
        below = low_bit(r) if r else count
        for bit in reversed(bit_list(count)):
            if bit < below:
                copy = remote(
                    source,
                    full[a].at[place(r)],
                    send.at[a, r | bit],
                    recv.at[a, r | bit],
                    (seq, place(bit)),
                )
                copies[a, r | bit] = copy

    def start(a, r):
        send_on(a, r)
        below = low_bit(r) if r else count
        bits = [bit for bit in bit_list(count) if bit < below]
        for bit in sorted(bits, key=lambda bit: (bit < 4, bit)):
            copies[a, r | bit].start()

    keeps = []
    for a in range(arrays):
        keep = pltpu.make_async_copy(own[a], full[a].at[me], local.at[a])
        keep.start()
        keeps.append(keep)
    arrivals = arrival_order(count)
    last = max(i for i, r in enumerate(arrivals) if not r & 2) + 1
    events = [(0, 0)]
    for g in range(len(groups)):
        events += [(g, r) for r in arrivals[:last]]
        if g + 1 < len(groups):
            events.append((g + 1, 0))
        events += [(g, r) for r in arrivals[last:]]
    for g, r in events:
        for a in groups[g]:
            if r:
                copies[a, r].wait_recv()
            start(a, r)
    for a in range(arrays):
        for r in range(1, count, 2):
            copies[a, r].wait_recv()
    for copy in copies.values():
        copy.wait_send()
    for keep in keeps:
        keep.wait()


def gather_blocks(blocks, collective_id, groups=((0,),)):
    count = lax.axis_size("shard")
    arrays = len(blocks)
    return pl.pallas_call(
        functools.partial(gather_kernel, count, groups),
        out_shape=[jax.ShapeDtypeStruct((count,) + b.shape, b.dtype) for b in blocks],
        in_specs=[pl.BlockSpec(memory_space=pltpu.VMEM)] * arrays,
        out_specs=[pl.BlockSpec(memory_space=pl.ANY)] * arrays,
        scratch_shapes=[
            pltpu.SemaphoreType.DMA((arrays, count)),
            pltpu.SemaphoreType.DMA((arrays, count)),
            pltpu.SemaphoreType.DMA((arrays,)),
        ],
        compiler_params=pltpu.CompilerParams(collective_id=collective_id, has_side_effects=True),
        name="gather_blocks_%d" % collective_id,
    )(*blocks)


def scatter_kernel(count, seq_count, arrays, sides, work, *refs):
    parts, refs = refs[:arrays], refs[arrays:]
    side_from, refs = refs[:sides], refs[sides:]
    work_in, refs = refs[: work.inputs], refs[work.inputs :]
    totals, refs = refs[:arrays], refs[arrays:]
    side_to, refs = refs[:sides], refs[sides:]
    work_out, refs = refs[: work.outputs], refs[work.outputs :]
    held, refs = refs[:arrays], refs[arrays:]
    send, recv, seq_send, seq_recv, side_send, side_recv = refs[:6]
    planes = seq_count if seq_count > 1 else 1 + (sides > 0 or work.outputs > 0)
    me = lax.axis_index("shard")
    seq = lax.axis_index("seq")
    place = relative_place(count, me)
    bits = bit_list(count)
    meet(count, place, seq, planes)
    copies = {}
    shared = []
    for i in range(sides):
        copy = remote(
            side_from[i],
            side_to[i],
            side_send.at[i],
            side_recv.at[i],
            (1 - seq, me),
        )
        copy.start()
        shared.append(copy)

    def share(a):
        for j in range(1, seq_count):
            copy = remote(
                totals[a].at[seq],
                totals[a].at[seq],
                seq_send.at[a, j - 1],
                seq_recv.at[a, j - 1],
                (lax.rem(seq + j, seq_count), me),
            )
            copy.start()
            shared.append(copy)

    def start(a, r, source):
        copy = remote(
            source, held[a].at[r], send.at[a, r], recv.at[a, r], (seq, place(low_bit(r)))
        )
        copy.start()
        copies[a, r] = copy

    def fold(a, r, bit):
        came = r | bit
        copies[a, came].wait_recv()
        rows = held[a].shape[1]
        last = bit == bits[-1]

        def step(i, carry):
            at = pl.ds(pl.multiple_of(i * ROW_TILE, ROW_TILE), ROW_TILE)
            if bit == 1:
                mine = parts[a][place(r), at, :]
            else:
                mine = held[a][r | (bit >> 1), at, :]
            value = mine.astype(jnp.float32) + held[a][came, at, :].astype(jnp.float32)
            if last and seq_count > 1:
                totals[a][seq, at, :] = value.astype(totals[a].dtype)
            elif last:
                totals[a][at, :] = value.astype(totals[a].dtype)
            else:
                held[a][came, at, :] = value.astype(held[a].dtype)
            return carry

        lax.fori_loop(0, rows // ROW_TILE, step, 0)
        upper = bit << 1
        if last:
            share(a)
        elif r & upper:
            start(a, r, held[a].at[came])

    chunks = [(a, u) for a in range(arrays) for u in reversed(range(count // 4))]
    for a, u in chunks:
        for r in (4 * u + 3, 4 * u + 1):
            start(a, r, parts[a].at[place(r)])
    tasks = work.tasks(seq, me, work_in, work_out, refs[6:])
    steps = len(chunks) + AHEAD
    for i in range(steps):
        if i < len(chunks):
            a, u = chunks[i]
            fold(a, 4 * u + 2, 1)
            fold(a, 4 * u, 1)
        if i >= AHEAD:
            a, u = chunks[i - AHEAD]
            for bit in bits[1:]:
                if 4 * u % (2 * bit) == 0:
                    fold(a, 4 * u, bit)
        for task in tasks[len(tasks) * i // steps : len(tasks) * (i + 1) // steps]:
            task()
    for copy in shared:
        copy.wait_recv()
    for copy in list(copies.values()) + shared:
        copy.wait_send()
    work.finish()


class NoWork:
    inputs = outputs = 0
    operands, results, scratch = (), (), ()

    def tasks(self, seq, me, arrays, results, scratch):
        return []

    def finish(self):
        pass


class ExpertGrads:
    def __init__(self, products):
        self.operands = []
        for pair in products:
            for array in pair:
                if not any(array is other for other in self.operands):
                    self.operands.append(array)
        self.pairs = [
            tuple(next(i for i, o in enumerate(self.operands) if o is array) for array in pair)
            for pair in products
        ]
        low = products[0][0].dtype
        shapes = [(left.shape[1] // 2, right.shape[1]) for left, right in products]
        halves = [jax.ShapeDtypeStruct(shape, low) for shape in shapes for _ in range(2)]
        self.results = halves
        self.inputs, self.outputs = len(self.operands), len(self.results)
        self.scratch = [pltpu.VMEM(a.shape, a.dtype) for a in self.operands]
        self.scratch += [pltpu.VMEM(h.shape, h.dtype) for h in halves]
        self.scratch += [
            pltpu.SemaphoreType.DMA((self.inputs,)),
            pltpu.SemaphoreType.DMA((self.outputs,)),
            pltpu.SemaphoreType.DMA((2,)),
        ]

    def tasks(self, seq, me, arrays, results, scratch):
        here, scratch = scratch[: self.inputs], scratch[self.inputs :]
        tiles, (in_sem, out_sem, side_sem) = scratch[: self.outputs], scratch[self.outputs :]
        loads = [
            pltpu.make_async_copy(arrays[i], here[i], in_sem.at[i]) for i in range(self.inputs)
        ]
        for load in loads:
            load.start()
        waited = set()
        self.open = []
        self.remote = None

        def multiply(p, k, first, last):
            left, right = self.pairs[p]
            out = tiles[2 * p + k]
            for i in (left, right):
                if i not in waited:
                    loads[i].wait()
                    waited.add(i)
            base = ((1 - seq) if k == 0 else seq) * out.shape[0]

            def step(i, carry):
                from_at = pl.ds(pl.multiple_of(base + i * GRAD_TILE, GRAD_TILE), GRAD_TILE)
                to_at = pl.ds(pl.multiple_of(i * GRAD_TILE, GRAD_TILE), GRAD_TILE)
                out[to_at, :] = contract_rows(here[left][:, from_at], here[right][...]).astype(
                    out.dtype
                )
                return carry

            lax.fori_loop(first, last, step, 0)
            if last * GRAD_TILE == out.shape[0]:
                if p == 0 and k == 0:
                    copy = remote(
                        out, results[0], side_sem.at[0], side_sem.at[1], (1 - seq, me)
                    )
                    self.remote = copy
                else:
                    copy = pltpu.make_async_copy(
                        out, results[2 * p + k], out_sem.at[2 * p + k]
                    )
                    self.open.append(copy)
                copy.start()

        found = []
        for p in range(len(self.pairs)):
            for k in range(2):
                count = tiles[2 * p + k].shape[0] // GRAD_TILE
                step = max(count // 2, 1)
                for first in range(0, count, step):
                    found.append(functools.partial(multiply, p, k, first, first + step))
        return found

    def finish(self):
        for copy in self.open:
            copy.wait()
        self.remote.wait()


def scatter_sum(parts, collective_id, out_dtype, seq_count=1, sides=(), work=None):
    work = work or NoWork()
    count = lax.axis_size("shard")
    arrays = len(parts)
    lead = (seq_count,) if seq_count > 1 else ()
    others = max(seq_count - 1, 1)
    return pl.pallas_call(
        functools.partial(scatter_kernel, count, seq_count, arrays, len(sides), work),
        out_shape=[jax.ShapeDtypeStruct(lead + p.shape[1:], out_dtype) for p in parts]
        + [jax.ShapeDtypeStruct(s.shape, s.dtype) for s in sides]
        + list(work.results),
        in_specs=[pl.BlockSpec(memory_space=pltpu.VMEM)] * arrays
        + [pl.BlockSpec(memory_space=pl.ANY)] * (len(sides) + work.inputs),
        out_specs=[pl.BlockSpec(memory_space=pltpu.VMEM)] * arrays
        + [pl.BlockSpec(memory_space=pl.ANY)] * (len(sides) + work.outputs),
        scratch_shapes=[pltpu.VMEM(p.shape, p.dtype) for p in parts]
        + [
            pltpu.SemaphoreType.DMA((arrays, count)),
            pltpu.SemaphoreType.DMA((arrays, count)),
            pltpu.SemaphoreType.DMA((arrays, others)),
            pltpu.SemaphoreType.DMA((arrays, others)),
            pltpu.SemaphoreType.DMA((max(len(sides), 1),)),
            pltpu.SemaphoreType.DMA((max(len(sides), 1),)),
        ]
        + list(work.scratch),
        compiler_params=pltpu.CompilerParams(
            collective_id=collective_id, has_side_effects=True, vmem_limit_bytes=VMEM_LIMIT
        ),
        name="scatter_sum_%d" % collective_id,
    )(*parts, *sides, *work.operands)


def place_kernel(refs_in, seq_count, *refs):
    for i, o in enumerate(refs_in):
        out_ref, base = refs[len(refs_in) + o[0]], o[1]
        cols = refs[i].shape[2]
        for s in range(seq_count):
            out_ref[:, base + s * cols : base + (s + 1) * cols] = refs[i][s].astype(out_ref.dtype)


def place_rows(pieces, targets, out_cols):
    seq_count, rows, _ = pieces[0].shape
    return pl.pallas_call(
        functools.partial(place_kernel, targets, seq_count),
        out_shape=[jax.ShapeDtypeStruct((rows, cols), jnp.float32) for cols in out_cols],
        in_specs=[pl.BlockSpec(memory_space=pltpu.VMEM)] * len(pieces),
        out_specs=[pl.BlockSpec(memory_space=pltpu.VMEM)] * len(out_cols),
        name="place_rows",
    )(*pieces)


class Tree:
    def __init__(self, count, own, full, send, recv, seq, place):
        self.count, self.own, self.full = count, own, full
        self.copies = {}
        for r in range(count):
            below = low_bit(r) if r else count
            for bit in bit_list(count):
                if bit < below:
                    self.copies[r | bit] = remote(
                        own if r == 0 else full.at[place(r)],
                        full.at[place(r)],
                        send.at[r | bit],
                        recv.at[r | bit],
                        (seq, place(bit)),
                    )

    def start(self, r):
        below = low_bit(r) if r else self.count
        bits = [bit for bit in bit_list(self.count) if bit < below]
        for bit in sorted(bits, key=lambda bit: (bit < 4, bit)):
            self.copies[r | bit].start()

    def arrive(self, r):
        self.copies[r].wait_recv()
        self.start(r)

    def steps(self):
        order, done, found = arrival_order(self.count), 0, []
        for i in range(self.count // 2):
            upto = order.index(2 * i) + 1 if i else 0
            found.append(order[done:upto])
            done = max(done, upto)
        return found

    def finish(self):
        for copy in self.copies.values():
            copy.wait_send()


def expert_kernel(count, *refs):
    (ffn_own, grad_own, weight), refs = refs[:3], refs[3:]
    matrices, refs = refs[:3], refs[3:]
    (rows_out, hidden_out, mixed_out, expert_out, gate_out, up_out), refs = refs[:6], refs[6:]
    pair_out, refs = refs[:2], refs[2:]
    (ffn_all, grad_all, gate_w, up_w, down_w, gate_all, up_all), refs = refs[:7], refs[7:]
    (hidden_at, mixed_at, expert_at, gate_at, up_at, left_at, right_at), refs = refs[:7], refs[7:]
    ffn_send, ffn_recv, grad_send, grad_recv, load, own_sem, rows_sem, out_sem = refs
    me = lax.axis_index("shard")
    seq = lax.axis_index("seq")
    place = relative_place(count, me)
    tiles = count // 2
    low, f32 = ffn_own.dtype, jnp.float32
    meet(count, place, seq)
    ffn = Tree(count, ffn_own, ffn_all, ffn_send, ffn_recv, seq, place)
    grad = Tree(count, grad_own, grad_all, grad_send, grad_recv, seq, place)
    ffn.start(0)
    loads = [
        pltpu.make_async_copy(source, target, load.at[i])
        for i, (source, target) in enumerate(zip(matrices, (gate_w, up_w, down_w)))
    ]
    for copy in loads:
        copy.start()
    ffn_keep = pltpu.make_async_copy(ffn_own, ffn_all.at[me], own_sem.at[0])
    grad_keep = pltpu.make_async_copy(grad_own, grad_all.at[me], own_sem.at[1])
    ffn_keep.start()
    grad_keep.start()
    ffn_keep.wait()
    for copy in loads:
        copy.wait()

    pair = me // 2

    def tile_of(i):
        total = 0
        for bit in bit_list(tiles):
            mine, other = lax.rem(pair // bit, 2), lax.rem(i // bit, 2)
            total = total + bit * (mine + other - 2 * mine * other)
        return total

    def put(number, slot, staged, target, tile):
        return pltpu.make_async_copy(staged.at[slot], target.at[tile], out_sem.at[number, slot])

    def keep_rows(tile):
        return pltpu.make_async_copy(
            ffn_all.at[pl.ds(2 * tile, 2)], rows_out.at[pl.ds(2 * tile, 2)], rows_sem.at[tile]
        )

    def arrivals(tree, i, extra):
        for at, order in enumerate(tree.steps()):

            @pl.when(i == at)
            def _(at=at, order=order):
                for r in order:
                    tree.arrive(r)
                if at in extra:
                    extra[at]()
                tree.copies[2 * at + 1].wait_recv()

    columns = gate_w.shape[1] // 2

    def forward(i, carry):
        arrivals(ffn, i, {tiles - 3: lambda: grad.start(0)})
        tile = tile_of(i)
        slot = lax.rem(i, 2)
        keep_rows(tile).start()

        @pl.when(i >= 2)
        def _():
            put(0, slot, hidden_at, hidden_out, tile_of(i - 2)).wait()
            put(1, slot, mixed_at, mixed_out, tile_of(i - 2)).wait()

        rows = ffn_all[pl.ds(2 * tile, 2)].reshape(-1, ffn_all.shape[2])
        for c in range(2):
            at = slice(c * columns, (c + 1) * columns)
            gate = jnp.dot(rows, gate_w[:, at], preferred_element_type=f32)
            up = jnp.dot(rows, up_w[:, at], preferred_element_type=f32)
            gate_all[i, :, at] = gate
            up_all[i, :, at] = up
            hidden_at[slot, :, at] = (gate * jax.nn.sigmoid(gate) * up).astype(low)
        put(0, slot, hidden_at, hidden_out, tile).start()
        half = down_w.shape[1] // 2
        for c in range(2):
            at = slice(c * half, (c + 1) * half)
            result = jnp.dot(hidden_at[slot], down_w[:, at], preferred_element_type=f32)
            mixed_at[slot, :, at] = (result.astype(low).astype(f32) * weight[tile]).astype(low)
        put(1, slot, mixed_at, mixed_out, tile).start()
        return carry

    lax.fori_loop(0, tiles, forward, 0)
    grad_keep.wait()

    def backward(i, carry):
        arrivals(grad, i, {})
        tile = tile_of(i)
        slot = lax.rem(i, 2)

        @pl.when(i >= 2)
        def _():
            before = tile_of(i - 2)
            put(2, slot, expert_at, expert_out, before).wait()
            put(3, slot, gate_at, gate_out, before).wait()
            put(4, slot, up_at, up_out, before).wait()
            put(5, slot, left_at, pair_out[0], before).wait()
            put(6, slot, right_at, pair_out[1], before).wait()

        rows = grad_all[pl.ds(2 * tile, 2)].reshape(-1, grad_all.shape[2])
        expert_at[slot] = (rows.astype(f32) * weight[tile]).astype(low)
        put(2, slot, expert_at, expert_out, tile).start()
        for c in range(2):
            at = slice(c * columns, (c + 1) * columns)
            d_hidden = contract_cols(expert_at[slot], down_w[at, :])
            gate, up = gate_all[i, :, at], up_all[i, :, at]
            sigma = jax.nn.sigmoid(gate)
            gate_at[slot, :, at] = (
                d_hidden * up * sigma * (1.0 + gate * (1.0 - sigma))
            ).astype(low)
            up_at[slot, :, at] = (d_hidden * (gate * sigma)).astype(low)
        put(3, slot, gate_at, gate_out, tile).start()
        put(4, slot, up_at, up_out, tile).start()
        half = gate_w.shape[0] // 2
        for c, staged in enumerate((left_at, right_at)):
            at = slice(c * half, (c + 1) * half)
            staged[slot] = (
                contract_cols(gate_at[slot], gate_w[at, :]) + contract_cols(up_at[slot], up_w[at, :])
            ).astype(low)
            put(5 + c, slot, staged, pair_out[c], tile).start()
        return carry

    lax.fori_loop(0, tiles, backward, 0)
    ffn.finish()
    grad.finish()
    for i in range(tiles):
        keep_rows(i).wait()
    outs = (hidden_out, mixed_out, expert_out, gate_out, up_out, pair_out[0], pair_out[1])
    staged = (hidden_at, mixed_at, expert_at, gate_at, up_at, left_at, right_at)
    for i in (tiles - 2, tiles - 1):
        for number in range(7):
            put(number, i % 2, staged[number], outs[number], tile_of(i)).wait()


def run_experts(ffn_in, own_grad, weight, gate_w, up_w, down_w, collective_id):
    count = lax.axis_size("shard")
    rows, width = ffn_in.shape
    inner = gate_w.shape[1]
    tiles, two = count // 2, 2 * rows
    low = ffn_in.dtype
    shape = jax.ShapeDtypeStruct
    wide, narrow = (tiles, two, width), (tiles, two, inner)
    outs = [shape((count, rows, width), low)]
    outs += [shape(s, low) for s in (narrow, wide, wide, narrow, narrow)]
    outs += [shape((tiles, two, width // 2), low)] * 2
    vmem, hbm = pl.BlockSpec(memory_space=pltpu.VMEM), pl.BlockSpec(memory_space=pl.ANY)
    staged = [inner, width, width, inner, inner, width // 2, width // 2]
    return pl.pallas_call(
        functools.partial(expert_kernel, count),
        out_shape=outs,
        in_specs=[vmem] * 3 + [hbm] * 3,
        out_specs=[hbm] * len(outs),
        scratch_shapes=[
            pltpu.VMEM((count, rows, width), low),
            pltpu.VMEM((count, rows, width), low),
            pltpu.VMEM(gate_w.shape, low),
            pltpu.VMEM(up_w.shape, low),
            pltpu.VMEM(down_w.shape, low),
            pltpu.VMEM((tiles, two, inner), jnp.float32),
            pltpu.VMEM((tiles, two, inner), jnp.float32),
        ]
        + [pltpu.VMEM((2, two, cols), low) for cols in staged]
        + [pltpu.SemaphoreType.DMA((count,))] * 4
        + [
            pltpu.SemaphoreType.DMA((3,)),
            pltpu.SemaphoreType.DMA((2,)),
            pltpu.SemaphoreType.DMA((tiles,)),
            pltpu.SemaphoreType.DMA((len(staged), 2)),
        ],
        compiler_params=pltpu.CompilerParams(
            collective_id=collective_id, has_side_effects=True, vmem_limit_bytes=VMEM_LIMIT
        ),
        name="run_experts",
    )(ffn_in, own_grad, weight, gate_w, up_w, down_w)


GAIN_LANES = 128


def pair_tables(expert_list, prob_list, expert_count):
    numbers = jnp.arange(expert_count, dtype=jnp.int32)
    named = expert_list[None, :, :] == numbers[:, None, None]
    return jnp.sum(jnp.where(named, prob_list[None], 0.0), axis=2)


def shards(
    layer_input,
    seq_lengths,
    seq_order,
    expert_ids,
    expert_probs,
    weight_qkv,
    weight_out,
    norm_gains,
    weight_gate,
    weight_up,
    weight_down,
    out_cotangent,
):
    width = layer_input.shape[-1]
    tok_rows = layer_input.shape[1]
    seq_count = lax.axis_size("seq")
    seq_at = lax.axis_index("seq")
    group_tok = tok_rows * seq_count
    experts = lax.axis_size("shard")
    shard_at = lax.axis_index("shard")
    weight_rows = weight_qkv.shape[0]
    heads_local = HEADS // seq_count
    local_width = heads_local * HEAD_DIM
    out_cols = width // seq_count
    score_scale = HEAD_DIM ** (-0.5)
    low = jnp.bfloat16
    f32 = jnp.float32

    def take_seq(array, axis):
        return lax.dynamic_index_in_dim(array, seq_at, axis, keepdims=False)

    def seq_sum(part):
        if seq_count != 2:
            return lax.psum_scatter(part, "seq", scatter_dimension=0, tiled=True).astype(f32)
        halves = part.reshape(2, part.shape[0] // 2, part.shape[1])
        there = lax.dynamic_index_in_dim(halves, 1 - seq_at, 0, keepdims=False)
        here = lax.dynamic_index_in_dim(halves, seq_at, 0, keepdims=False)
        came = lax.ppermute(there, "seq", [(0, 1), (1, 0)])
        return here.astype(f32) + came.astype(f32)

    own_cols = take_seq(weight_qkv.reshape(weight_rows, 3, seq_count, local_width), 2)
    own_gains = jnp.pad(norm_gains, ((0, 0), (0, GAIN_LANES - norm_gains.shape[1])))
    table = pair_tables(expert_ids[0], expert_probs[0], experts)
    own_block = jnp.concatenate(
        [own_cols.reshape(weight_rows, 3 * local_width), own_gains], axis=1
    )
    qkv_cols, full_out, tables_all = gather_blocks(
        [own_block, weight_out, table], 1, ((0,), (1, 2))
    )
    qkv_cols = qkv_cols.reshape(width, 3 * local_width + GAIN_LANES)
    gain_cols = qkv_cols[:, 3 * local_width :][:, : norm_gains.shape[1]].astype(f32)
    qkv_cols = qkv_cols[:, : 3 * local_width]
    full_out = full_out.reshape(width, width)
    group_in = lax.all_gather(layer_input[0], "seq", axis=0, tiled=True).astype(f32)
    pair_weight = lax.dynamic_index_in_dim(tables_all, shard_at, 1, keepdims=False)

    segment, position = group_layout(seq_lengths[0], seq_order[0], group_tok)
    places = jnp.arange(group_tok, dtype=jnp.int32)
    allowed = (segment[:, None] == segment[None, :]) & (places[None, :] <= places[:, None])
    cosine, sine_part = rope_tables(position, HEAD_DIM)

    def rope(values):
        return rotate(
            values.reshape(group_tok, heads_local, HEAD_DIM), cosine, sine_part
        ).reshape(group_tok, local_width)

    def rope_back(grads):
        return rotate(
            grads.reshape(group_tok, heads_local, HEAD_DIM), cosine, -sine_part
        ).reshape(group_tok, local_width)

    gain_q = lax.dynamic_slice_in_dim(gain_cols[:, 1], seq_at * local_width, local_width)
    gain_k = lax.dynamic_slice_in_dim(gain_cols[:, 2], seq_at * local_width, local_width)

    group_r = lax.rsqrt(jnp.mean(group_in * group_in, axis=-1, keepdims=True) + norm_eps)
    group_n = group_in * group_r
    attn_in = (group_n * gain_cols[:, 0]).astype(low)
    projected = jnp.dot(attn_in, qkv_cols, preferred_element_type=f32)
    q_raw = projected[:, :local_width]
    k_raw = projected[:, local_width : 2 * local_width]
    value = projected[:, 2 * local_width :].astype(low)
    squares = jnp.stack([jnp.sum(q_raw * q_raw, axis=-1), jnp.sum(k_raw * k_raw, axis=-1)])
    squares = lax.psum(squares, "seq")
    q_r, k_r = (lax.rsqrt(row / width + norm_eps)[:, None] for row in squares)
    q_n = q_raw * q_r
    k_n = k_raw * k_r
    query = rope(q_n * gain_q).astype(low)
    key = rope(k_n * gain_k).astype(low)
    query_head = query.reshape(group_tok, heads_local, HEAD_DIM)
    key_head = key.reshape(group_tok, heads_local, HEAD_DIM)
    value_head = value.reshape(group_tok, heads_local, HEAD_DIM)
    scores = jnp.einsum("ihd,jhd->hij", query_head, key_head, preferred_element_type=f32)
    scores = jnp.where(allowed[None], scores * score_scale, -1e30)
    score_peak = jnp.max(scores, axis=-1, keepdims=True)
    weights_exp = jnp.exp(scores - score_peak)
    attn_probs = weights_exp / jnp.sum(weights_exp, axis=-1, keepdims=True)
    probs_low = attn_probs.astype(low)
    mix_head = jnp.einsum("hij,jhd->ihd", probs_low, value_head, preferred_element_type=f32)
    mix_head = mix_head.astype(low).reshape(group_tok, local_width)
    attn_mix = lax.all_to_all(mix_head, "seq", split_axis=0, concat_axis=1, tiled=True)
    mix_all = lax.all_gather(mix_head, "seq", axis=1, tiled=True)
    resid = layer_input[0].astype(f32) + jnp.dot(attn_mix, full_out, preferred_element_type=f32)
    ffn_r = lax.rsqrt(jnp.mean(resid * resid, axis=-1, keepdims=True) + norm_eps)
    ffn_n = resid * ffn_r
    ffn_in = (ffn_n * gain_cols[:, 3]).astype(low)

    pairs = seq_count == 2
    gate_weight = weight_gate[0]
    up_weight = weight_up[0]
    down_weight = weight_down[0]
    if experts <= 16:
        tile_weight = pair_weight.reshape(experts // 2, 2 * tok_rows, 1)
        results = run_experts(
            ffn_in, out_cotangent[0], tile_weight, gate_weight, up_weight, down_weight, 2
        )
        rows_in, hidden, out_part, d_expert, d_gate, d_up, *halves = (
            result.reshape(experts * tok_rows, -1) for result in results
        )
    else:
        slot_weight = pair_weight.reshape(-1, 1)
        (ffn_all, grad_all) = gather_blocks([ffn_in, out_cotangent[0]], 2, ((0,), (1,)))
        rows_in = ffn_all.reshape(-1, width)
        gate = jnp.dot(rows_in, gate_weight, preferred_element_type=f32)
        up = jnp.dot(rows_in, up_weight, preferred_element_type=f32)
        sigma = jax.nn.sigmoid(gate)
        silu = gate * sigma
        hidden = (silu * up).astype(low)
        expert_out = jnp.dot(hidden, down_weight, preferred_element_type=f32).astype(low)
        out_part = (expert_out.astype(f32) * slot_weight).astype(low)
        d_expert = (grad_all.reshape(-1, width).astype(f32) * slot_weight).astype(low)
        d_hidden = contract_cols(d_expert, down_weight)
        d_gate = (d_hidden * up * sigma * (1.0 + gate * (1.0 - sigma))).astype(low)
        d_up = (d_hidden * silu).astype(low)
        d_pair = contract_cols(d_gate, gate_weight) + contract_cols(d_up, up_weight)
        halves = jnp.split(d_pair.astype(low), 2, axis=1)
    halves = [part.reshape(experts, tok_rows, -1) for part in halves]
    products = [(hidden, d_expert), (rows_in, d_gate), (rows_in, d_up)]
    if pairs:
        results = scatter_sum(halves, 3, f32, work=ExpertGrads(products))
        d_left, d_right, down_came, down_mine, gate_there, gate_mine, up_there, up_mine = results
    else:
        d_left, d_right = scatter_sum(halves, 3, f32)
    d_ffn_in = jnp.concatenate([d_left, d_right], axis=1)
    out_part, d_ffn_in = lax.optimization_barrier((out_part, d_ffn_in))
    mixed_out = lax.psum_scatter(
        out_part, "shard", scatter_dimension=0, tiled=True
    ).astype(f32)
    layer_output = (resid + mixed_out).astype(low)

    grad_tokens = out_cotangent[0].astype(f32)
    d_scaled = d_ffn_in * gain_cols[:, 3]
    d_resid = grad_tokens + ffn_r * (
        d_scaled - ffn_n * jnp.mean(d_scaled * ffn_n, axis=-1, keepdims=True)
    )
    grad_g_ffn = jnp.sum(d_ffn_in * ffn_n, axis=0)
    d_branch = d_resid.astype(low)
    d_mix = contract_cols(d_branch, full_out).astype(low)
    d_mix_head = lax.all_to_all(d_mix, "seq", split_axis=1, concat_axis=0, tiled=True).reshape(
        group_tok, heads_local, HEAD_DIM
    )
    branch_cols = lax.all_to_all(d_branch, "seq", split_axis=1, concat_axis=0, tiled=True)
    d_probs = jnp.einsum("ihd,jhd->hij", d_mix_head, value_head, preferred_element_type=f32)
    delta_rows = jnp.sum(attn_probs * d_probs, axis=-1, keepdims=True)
    d_scores = (attn_probs * (d_probs - delta_rows)).astype(low)
    d_query = (
        jnp.einsum("hij,jhd->ihd", d_scores, key_head, preferred_element_type=f32) * score_scale
    ).astype(low)
    d_key = (
        jnp.einsum("hij,ihd->jhd", d_scores, query_head, preferred_element_type=f32) * score_scale
    ).astype(low)
    d_value = jnp.einsum(
        "hij,ihd->jhd", probs_low, d_mix_head, preferred_element_type=f32
    ).astype(low)
    dq_rot = rope_back(d_query.reshape(group_tok, local_width).astype(f32))
    dk_rot = rope_back(d_key.reshape(group_tok, local_width).astype(f32))
    grad_g_q = jnp.sum(dq_rot * q_n, axis=0)
    grad_g_k = jnp.sum(dk_rot * k_n, axis=0)
    dq_scaled = dq_rot * gain_q
    dk_scaled = dk_rot * gain_k
    dots = jnp.stack([jnp.sum(dq_scaled * q_n, axis=-1), jnp.sum(dk_scaled * k_n, axis=-1)])
    dots = lax.psum(dots, "seq") / width
    dq_raw = q_r * (dq_scaled - q_n * dots[0][:, None])
    dk_raw = k_r * (dk_scaled - k_n * dots[1][:, None])
    d_qkv = jnp.concatenate(
        [dq_raw.astype(low), dk_raw.astype(low), d_value.reshape(group_tok, local_width)], axis=1
    )
    d_attn_in = seq_sum(contract_cols(d_qkv, qkv_cols).astype(low))
    own_n = lax.dynamic_slice_in_dim(group_n, seq_at * tok_rows, tok_rows)
    own_r = lax.dynamic_slice_in_dim(group_r, seq_at * tok_rows, tok_rows)
    dx_scaled = d_attn_in * gain_cols[:, 0]
    dx_norm = own_r * (dx_scaled - own_n * jnp.mean(dx_scaled * own_n, axis=-1, keepdims=True))
    grad_g_attn = jnp.sum(d_attn_in * own_n, axis=0)
    input_grad = (d_resid + dx_norm).astype(low)

    zeros = jnp.zeros((width,), f32)
    gain_terms = jnp.stack(
        [
            grad_g_attn,
            lax.dynamic_update_slice_in_dim(zeros, grad_g_q, seq_at * local_width, 0),
            lax.dynamic_update_slice_in_dim(zeros, grad_g_k, seq_at * local_width, 0),
            grad_g_ffn,
        ],
        axis=1,
    )
    gain_terms = jnp.pad(gain_terms, ((0, 0), (0, GAIN_LANES - gain_terms.shape[1])))
    terms = [
        contract_rows(attn_in, d_qkv[:, i * local_width : (i + 1) * local_width]) for i in range(3)
    ]
    terms += [contract_rows(mix_all, branch_cols), gain_terms]
    terms = [term.astype(low).reshape(experts, weight_rows, -1) for term in terms]
    sides = [gate_there, up_there] if pairs else []
    results = scatter_sum(terms, 4, low, seq_count, sides=sides)
    *sums, sum_gains = results[: len(terms)]
    if pairs:
        gate_came, up_came = results[len(terms) :]
        sum_gate, sum_up, sum_down = (
            mine.astype(f32) + came.astype(f32)
            for mine, came in ((gate_mine, gate_came), (up_mine, up_came), (down_mine, down_came))
        )
    else:
        sum_down, sum_gate, sum_up = (
            lax.psum_scatter(
                contract_rows(left, right).astype(low), "seq", scatter_dimension=0, tiled=True
            ).astype(f32)
            for left, right in products
        )
    targets = [(0, 0), (0, width), (0, 2 * width), (1, 0)]
    rows_qkv, rows_out = place_rows(sums, targets, (3 * width, width))
    rows_gain = jnp.sum(sum_gains[:, :, : norm_gains.shape[1]].astype(f32), axis=0)
    return (
        layer_output[None],
        input_grad[None],
        rows_qkv,
        rows_out,
        rows_gain,
        sum_gate[None],
        sum_up[None],
        sum_down[None],
    )


def solution(mesh):
    in_specs = (
        P("shard", "seq", None),
        P("shard", None),
        P("shard", None),
        P("shard", "seq", None),
        P("shard", "seq", None),
        P("shard", None),
        P("shard", None),
        P("shard", None),
        P("shard", None, None),
        P("shard", None, None),
        P("shard", None, None),
        P("shard", "seq", None),
    )
    out_specs = (
        P("shard", "seq", None),
        P("shard", "seq", None),
        P("shard", None),
        P("shard", None),
        P("shard", None),
        P("shard", "seq", None),
        P("shard", "seq", None),
        P("shard", "seq", None),
    )
    return jax.shard_map(shards, mesh=mesh, in_specs=in_specs, out_specs=out_specs, check_vma=False)
```

```python
import functools

import jax
import jax.numpy as jnp
from jax import lax
from jax.experimental import pallas as pl
from jax.experimental.pallas import tpu as pltpu
from jax.sharding import PartitionSpec as P

HEADS = 16
HEAD_DIM = 128


norm_eps = 1e-05
rope_base = 10000.0


def rms_scale(values, gain_col):
    return (
        values * lax.rsqrt(jnp.mean(values * values, axis=-1, keepdims=True) + norm_eps) * gain_col
    )


def rotate(values, cosine, sine_part):
    half_dim = values.shape[-1] // 2
    first_half = values[..., :half_dim]
    second_half = values[..., half_dim:]
    return jnp.concatenate(
        [
            first_half * cosine - second_half * sine_part,
            second_half * cosine + first_half * sine_part,
        ],
        axis=-1,
    )


def rope_tables(position, head_size):
    half_dim = head_size // 2
    frequency = rope_base ** (-2.0 * jnp.arange(half_dim, dtype=jnp.float32) / head_size)
    angles = position.astype(jnp.float32)[:, None] * frequency[None, :]
    return (jnp.cos(angles)[:, None, :], jnp.sin(angles)[:, None, :])


def group_layout(lengths, seq_perm, group_tok):
    seq_count = lengths.shape[0]
    numbers = jnp.arange(seq_count, dtype=jnp.int32)
    packed = jnp.sum(jnp.where(seq_perm[:, None] == numbers[None, :], lengths[None, :], 0), axis=1)
    seq_ends = jnp.cumsum(packed)
    seq_starts = seq_ends - packed
    places = jnp.arange(group_tok, dtype=jnp.int32)
    segment = jnp.sum((places[:, None] >= seq_ends[None, :]).astype(jnp.int32), axis=1)
    begins = jnp.sum(
        jnp.where(segment[:, None] == numbers[None, :], seq_starts[None, :], 0), axis=1
    )
    return (segment, places - begins)


def contract_rows(left_side, right_side):
    return lax.dot_general(
        left_side, right_side, (((0,), (0,)), ((), ())), preferred_element_type=jnp.float32
    )


def contract_cols(left_side, right_side):
    return lax.dot_general(
        left_side, right_side, (((1,), (1,)), ((), ())), preferred_element_type=jnp.float32
    )


MESH_ID = pl.DeviceIdType.MESH
VMEM_LIMIT = 60 * 1024 * 1024
ROW_TILE = 16
AHEAD = 2
GRAD_TILE = 256


def low_bit(index):
    return index & -index


def bit_list(count):
    return [1 << b for b in range(count.bit_length() - 1)]


def relative_place(count, me):
    values = [(bit, lax.rem(me // bit, 2)) for bit in bit_list(count)]

    def place(r):
        total = 0
        for bit, value in values:
            total = total + bit * ((1 - value) if r & bit else value)
        return total

    return place


def meet(count, place, seq, seq_count=1):
    barrier = pltpu.get_barrier_semaphore()
    for bit in bit_list(count):
        pl.semaphore_signal(barrier, 1, device_id=(seq, place(bit)), device_id_type=MESH_ID)
    for j in range(1, seq_count):
        pl.semaphore_signal(
            barrier, 1, device_id=(lax.rem(seq + j, seq_count), place(0)), device_id_type=MESH_ID
        )
    pl.semaphore_wait(barrier, len(bit_list(count)) + seq_count - 1)


def remote(src, dst, send_sem, recv_sem, device):
    return pltpu.make_async_remote_copy(
        src_ref=src,
        dst_ref=dst,
        send_sem=send_sem,
        recv_sem=recv_sem,
        device_id=device,
        device_id_type=MESH_ID,
    )


def arrival_order(count):
    def key(r):
        later = r >> 2
        return (later + ((r >> 1) & 1), (r >> 1) & 1)

    return sorted(range(2, count, 2), key=key)


LINE = 16


class Line:
    def __init__(self, count, own, full, send, recv, seq, pieces=1):
        me = lax.axis_index("shard")
        spot = me // 4
        self.upper = spot // 2
        self.inner = spot + self.upper * (3 - 2 * spot)
        self.y = lax.rem(me // 2, 2)
        self.core = lax.rem(me, 2)
        low = lax.rem(me, 4)
        near = (seq, self.block(1) * 4 + low)
        far = (seq, (3 - spot) * 4 + low)
        across = (seq, spot * 4 + (1 - self.y) * 2 + self.core)
        twin = (seq, spot * 4 + self.y * 2 + 1 - self.core)
        self.peers = (near, far, across, twin)
        self.copies = []
        self.inward = []
        rows = own.shape[0] // pieces
        for p in range(pieces):
            at = pl.ds(p * rows, rows)
            target = [full.at[self.place(r), at] for r in range(count)]
            source = [own.at[at]] + target[1:]

            def copy(r, sent, received, device, source=source, target=target, p=p):
                return remote(
                    source[r], target[r], send.at[p, sent], recv.at[p, received], device
                )

            copies = {4: copy(0, 4, 4, near)}
            for r in range(0, count, 4):
                copies[r | 2] = copy(r, r | 2, r | 2, across)
            for r in range(0, count, 2):
                copies[r | 1] = copy(r, r | 1, r | 1, twin)
            inward = {0: copy(0, 8, 8, far), 4: copy(4, 12, 12, far)}
            inward[8] = copy(8, 0, 8, near)
            inward[12] = copy(12, count, 12, near)
            copies[8] = inward[0]
            copies[12] = inward[4]
            self.copies.append(copies)
            self.inward.append(inward)

    def block(self, k):
        if isinstance(k, int):
            spot = k if k >= 2 else self.inner + k * (1 - 2 * self.inner)
        else:
            far = k // 2
            spot = far * k + (1 - far) * lax.rem(k + self.inner, 2)
        return spot + self.upper * (3 - 2 * spot)

    def place(self, r):
        y = (1 - self.y) if r & 2 else self.y
        core = (1 - self.core) if r & 1 else self.core
        return self.block(r >> 2) * 4 + y * 2 + core

    def pair(self, i):
        k, y = i // 2, lax.rem(i, 2)
        return self.block(k) * 2 + self.y + y - 2 * self.y * y

    def meet(self):
        barrier = pltpu.get_barrier_semaphore()
        for peer in self.peers:
            pl.semaphore_signal(barrier, 1, device_id=peer, device_id_type=MESH_ID)
        pl.semaphore_wait(barrier, len(self.peers))

    def start(self, r):
        for p in range(len(self.copies)):
            self.start_piece(p, r)

    def start_piece(self, p, r):
        copies, inward = self.copies[p], self.inward[p]
        if r == 0:
            copies[4].start()
        if r % 4 == 0:

            @pl.when(self.inner == 1)
            def _():
                inward[r].start()

            copies[r | 2].start()
        copies[r | 1].start()

    def arrive(self, r):
        for p in range(len(self.copies)):
            self.copies[p][r].wait_recv()
            self.start_piece(p, r)

    def wait_twin(self, r):
        for copies in self.copies:
            copies[r | 1].wait_recv()

    order = (4, 2, 8, 6, 12, 10, 14)

    def finish(self):
        for copies, inward in zip(self.copies, self.inward):
            for r in (4, 2, 6, 10, 14, 1, 3, 5, 7, 9, 11, 13, 15):
                copies[r].wait_send()

            @pl.when(self.inner == 1)
            def _(inward=inward):
                for copy in inward.values():
                    copy.wait_send()


class Tree:
    def __init__(self, count, own, full, send, recv, seq, pieces=1):
        self.count, self.seq = count, seq
        self.place = relative_place(count, lax.axis_index("shard"))
        self.order = arrival_order(count)
        self.copies = {}
        for r in range(count):
            below = low_bit(r) if r else count
            for bit in bit_list(count):
                if bit < below:
                    self.copies[r | bit] = remote(
                        own if r == 0 else full.at[self.place(r)],
                        full.at[self.place(r)],
                        send.at[0, r | bit],
                        recv.at[0, r | bit],
                        (seq, self.place(bit)),
                    )

    def meet(self):
        meet(self.count, self.place, self.seq)

    def start(self, r):
        below = low_bit(r) if r else self.count
        bits = [bit for bit in bit_list(self.count) if bit < below]
        for bit in sorted(bits, key=lambda bit: (bit < 4, bit)):
            self.copies[r | bit].start()

    def arrive(self, r):
        self.copies[r].wait_recv()
        self.start(r)

    def wait_twin(self, r):
        self.copies[r | 1].wait_recv()

    def finish(self):
        for copy in self.copies.values():
            copy.wait_send()


def gather_kernel(count, groups, pieces, *refs):
    arrays = sum(len(group) for group in groups)
    own, full = refs[:arrays], refs[arrays : 2 * arrays]
    send, recv, local = refs[2 * arrays :]
    me = lax.axis_index("shard")
    seq = lax.axis_index("seq")
    kind = Line if count == LINE else Tree
    ways = [
        kind(count, own[a], full[a], send.at[a], recv.at[a], seq, pieces[a])
        for a in range(arrays)
    ]
    ways[0].meet()
    keeps = []
    for a in range(arrays):
        keep = pltpu.make_async_copy(own[a], full[a].at[me], local.at[a])
        keep.start()
        keeps.append(keep)
    for group in groups:
        for a in group:
            ways[a].start(0)
        for r in ways[0].order:
            for a in group:
                ways[a].arrive(r)
    for a in range(arrays):
        for r in range(0, count, 2):
            ways[a].wait_twin(r)
    for way in ways:
        way.finish()
    for keep in keeps:
        keep.wait()


def gather_blocks(blocks, collective_id, groups=((0,),), pieces=(1,)):
    count = lax.axis_size("shard")
    arrays = len(blocks)
    return pl.pallas_call(
        functools.partial(gather_kernel, count, groups, pieces),
        out_shape=[jax.ShapeDtypeStruct((count,) + b.shape, b.dtype) for b in blocks],
        in_specs=[pl.BlockSpec(memory_space=pltpu.VMEM)] * arrays,
        out_specs=[pl.BlockSpec(memory_space=pl.ANY)] * arrays,
        scratch_shapes=[
            pltpu.SemaphoreType.DMA((arrays, max(pieces), count + 1)),
            pltpu.SemaphoreType.DMA((arrays, max(pieces), count + 1)),
            pltpu.SemaphoreType.DMA((arrays,)),
        ],
        compiler_params=pltpu.CompilerParams(collective_id=collective_id, has_side_effects=True),
        name="gather_blocks_%d" % collective_id,
    )(*blocks)


def scatter_kernel(count, seq_count, arrays, sides, work, *refs):
    given = 0 if work.part_shapes else arrays
    parts, refs = refs[:given], refs[given:]
    side_from, refs = refs[:sides], refs[sides:]
    work_in, refs = refs[: work.inputs], refs[work.inputs :]
    totals, refs = refs[:arrays], refs[arrays:]
    side_to, refs = refs[:sides], refs[sides:]
    work_out, refs = refs[: work.outputs], refs[work.outputs :]
    if work.part_shapes:
        parts, refs = refs[:arrays], refs[arrays:]
    held, refs = refs[:arrays], refs[arrays:]
    send, recv, seq_send, seq_recv, side_send, side_recv = refs[:6]
    planes = seq_count if seq_count > 1 else 1 + (sides > 0 or work.outputs > 0)
    me = lax.axis_index("shard")
    seq = lax.axis_index("seq")
    place = relative_place(count, me)
    bits = bit_list(count)
    meet(count, place, seq, planes)
    copies = {}
    shared = []

    def start_sides():
        for i in range(sides):
            copy = remote(
                side_from[i], side_to[i], side_send.at[i], side_recv.at[i], (1 - seq, me)
            )
            copy.start()
            shared.append(copy)

    def share(a):
        for j in range(1, seq_count):
            copy = remote(
                totals[a].at[seq],
                totals[a].at[seq],
                seq_send.at[a, j - 1],
                seq_recv.at[a, j - 1],
                (lax.rem(seq + j, seq_count), me),
            )
            copy.start()
            shared.append(copy)

    def start(a, r, source):
        copy = remote(
            source, held[a].at[r], send.at[a, r], recv.at[a, r], (seq, place(low_bit(r)))
        )
        copy.start()
        copies[a, r] = copy

    def fold(a, r, bit):
        came = r | bit
        copies[a, came].wait_recv()
        rows = held[a].shape[1]
        last = bit == bits[-1]

        def step(i, carry):
            at = pl.ds(pl.multiple_of(i * ROW_TILE, ROW_TILE), ROW_TILE)
            if bit == 1:
                mine = parts[a][place(r), at, :]
            else:
                mine = held[a][r | (bit >> 1), at, :]
            value = mine.astype(jnp.float32) + held[a][came, at, :].astype(jnp.float32)
            if last and seq_count > 1:
                totals[a][seq, at, :] = value.astype(totals[a].dtype)
            elif last:
                totals[a][at, :] = value.astype(totals[a].dtype)
            else:
                held[a][came, at, :] = value.astype(held[a].dtype)
            return carry

        lax.fori_loop(0, rows // ROW_TILE, step, 0)
        upper = bit << 1
        if last:
            share(a)
        elif r & upper:
            start(a, r, held[a].at[came])

    chunks = [
        (a, u) for a in work.order or range(arrays) for u in reversed(range(count // 4))
    ]

    def prepare(a, u):
        work.fill(parts, a, place(4 * u) - lax.rem(me, 4))
        for r in (4 * u + 3, 4 * u + 1):
            start(a, r, parts[a].at[place(r)])

    tasks = work.tasks(seq, me, work_in, work_out, refs[6:], start_sides)
    lead = AHEAD if work.part_shapes else len(chunks)
    for a, u in chunks[:lead]:
        prepare(a, u)
    steps = len(chunks) + AHEAD
    for i in range(steps):
        if i + lead < len(chunks):
            prepare(*chunks[i + lead])
        if i < len(chunks):
            a, u = chunks[i]
            fold(a, 4 * u + 2, 1)
            fold(a, 4 * u, 1)
        if i >= AHEAD:
            a, u = chunks[i - AHEAD]
            for bit in bits[1:]:
                if 4 * u % (2 * bit) == 0:
                    fold(a, 4 * u, bit)
        for task in work.at_step(tasks, i, steps):
            task()
    for copy in shared:
        copy.wait_recv()
    for copy in list(copies.values()) + shared:
        copy.wait_send()
    work.finish()


class NoWork:
    inputs = outputs = 0
    operands, results, scratch, part_shapes, order = (), (), (), (), ()

    def fill(self, parts, a, base):
        pass

    def tasks(self, seq, me, arrays, results, scratch, start_sides):
        start_sides()
        return []

    def at_step(self, tasks, i, steps):
        return tasks[len(tasks) * i // steps : len(tasks) * (i + 1) // steps]

    def finish(self):
        pass


class ExpertGrads(NoWork):
    def __init__(self, products):
        self.operands = []
        for pair in products:
            for array in pair:
                if not any(array is other for other in self.operands):
                    self.operands.append(array)
        self.pairs = [
            tuple(next(i for i, o in enumerate(self.operands) if o is array) for array in pair)
            for pair in products
        ]
        low = products[0][0].dtype
        shapes = [(left.shape[1] // 2, right.shape[1]) for left, right in products]
        halves = [jax.ShapeDtypeStruct(shape, low) for shape in shapes for _ in range(2)]
        self.results = halves
        self.inputs, self.outputs = len(self.operands), len(self.results)
        self.scratch = [pltpu.VMEM(a.shape, a.dtype) for a in self.operands]
        self.scratch += [pltpu.VMEM(h.shape, h.dtype) for h in halves]
        self.scratch += [
            pltpu.SemaphoreType.DMA((self.inputs,)),
            pltpu.SemaphoreType.DMA((self.outputs,)),
            pltpu.SemaphoreType.DMA((2,)),
        ]

    def tasks(self, seq, me, arrays, results, scratch, start_sides):
        start_sides()
        here, scratch = scratch[: self.inputs], scratch[self.inputs :]
        tiles, (in_sem, out_sem, side_sem) = scratch[: self.outputs], scratch[self.outputs :]
        loads = [
            pltpu.make_async_copy(arrays[i], here[i], in_sem.at[i]) for i in range(self.inputs)
        ]
        for load in loads:
            load.start()
        waited = set()
        self.open = []
        self.remote = None

        def multiply(p, k, first, last):
            left, right = self.pairs[p]
            out = tiles[2 * p + k]
            for i in (left, right):
                if i not in waited:
                    loads[i].wait()
                    waited.add(i)
            base = ((1 - seq) if k == 0 else seq) * out.shape[0]

            def step(i, carry):
                from_at = pl.ds(pl.multiple_of(base + i * GRAD_TILE, GRAD_TILE), GRAD_TILE)
                to_at = pl.ds(pl.multiple_of(i * GRAD_TILE, GRAD_TILE), GRAD_TILE)
                out[to_at, :] = contract_rows(here[left][:, from_at], here[right][...]).astype(
                    out.dtype
                )
                return carry

            lax.fori_loop(first, last, step, 0)
            if last * GRAD_TILE == out.shape[0]:
                if p == 0 and k == 0:
                    copy = remote(
                        out, results[0], side_sem.at[0], side_sem.at[1], (1 - seq, me)
                    )
                    self.remote = copy
                else:
                    copy = pltpu.make_async_copy(
                        out, results[2 * p + k], out_sem.at[2 * p + k]
                    )
                    self.open.append(copy)
                copy.start()

        found = []
        for p in range(len(self.pairs)):
            for k in range(2):
                count = tiles[2 * p + k].shape[0] // GRAD_TILE
                step = max(count // 2, 1)
                for first in range(0, count, step):
                    found.append(functools.partial(multiply, p, k, first, first + step))
        return found

    def finish(self):
        for copy in self.open:
            copy.wait()
        self.remote.wait()


class AttentionGrads(NoWork):
    def __init__(self, attn_in, d_qkv, mix_all, branch, weights, tokens, d_resid, gains, gain):
        self.operands = [attn_in, d_qkv, mix_all, branch, weights, tokens, d_resid, gains, gain]
        self.inputs, self.outputs = len(self.operands), 1
        low = attn_in.dtype
        blocks, rows = weights.shape[:2]
        self.local = d_qkv.shape[1] // 3
        self.part_shapes = [
            jax.ShapeDtypeStruct((blocks, rows, cols), low)
            for cols in (self.local, self.local, self.local, branch.shape[1])
        ]
        self.part_shapes.append(jax.ShapeDtypeStruct(gains.shape, low))
        self.order = (0, 1, 2, 4, 3)
        self.results = [jax.ShapeDtypeStruct(tokens.shape, low)]
        self.scratch = [pltpu.VMEM(a.shape, a.dtype) for a in self.operands]
        self.scratch += [
            pltpu.VMEM(tokens.shape, low),
            pltpu.VMEM((2,) + tokens.shape, low),
            pltpu.VMEM(tokens.shape, low),
            pltpu.VMEM((ROW_TILE, tokens.shape[1]), jnp.float32),
            pltpu.SemaphoreType.DMA((self.inputs,)),
            pltpu.SemaphoreType.DMA((3,)),
        ]

    def need(self, *numbers):
        for i in numbers:
            if i not in self.waited:
                self.loads[i].wait()
                self.waited.add(i)

    def fill(self, parts, a, base):
        part = parts[a]
        if a == 4:
            part[pl.ds(base, 4)] = self.here[7][pl.ds(base, 4)].astype(part.dtype)
            return
        left, right = (2, 3) if a == 3 else (0, 1)
        self.need(left, right)
        rows, cols = part.shape[1:]
        first = 0 if a == 3 else a * self.local

        def step(i, carry):
            at = pl.ds(pl.multiple_of((base + i) * rows, rows), rows)
            part[base + i] = contract_rows(
                self.here[left][:, at], self.here[right][:, first : first + cols]
            ).astype(part.dtype)
            return carry

        lax.fori_loop(0, 4, step, 0)

    def tasks(self, seq, me, arrays, results, scratch, start_sides):
        self.here, scratch = scratch[: self.inputs], scratch[self.inputs :]
        here = self.here
        grad, part, came, total, in_sem, sem = scratch
        self.loads = [
            pltpu.make_async_copy(arrays[i], here[i], in_sem.at[i]) for i in range(self.inputs)
        ]
        self.waited = set()
        for load in self.loads:
            load.start()
        blocks, rows = here[4].shape[:2]
        inner = here[1].shape[1]
        tok_rows, width = came.shape
        self.exchange = remote(part.at[1 - seq], came, sem.at[0], sem.at[1], (1 - seq, me))
        self.out = pltpu.make_async_copy(grad, results[0], sem.at[2])

        def multiply(first, last):
            self.need(1, 4)

            def step(i, carry):
                at = pl.ds(pl.multiple_of(2 * i * rows, 2 * rows), 2 * rows)
                weight = here[4][pl.ds(2 * i, 2), :, :inner].reshape(2 * rows, inner)
                result = contract_cols(here[1][...], weight)
                part[:, :, at] = result.reshape(2, tok_rows, 2 * rows).astype(part.dtype)
                return carry

            lax.fori_loop(first, last, step, 0)

        def send():
            self.exchange.start()
            start_sides()

        def norm_back():
            self.need(5, 6, 7, 8)
            self.exchange.wait_recv()
            total[...] = jnp.zeros_like(total)

            def step(i, carry):
                at = pl.ds(pl.multiple_of(i * ROW_TILE, ROW_TILE), ROW_TILE)
                values = here[5][at, :].astype(jnp.float32)
                scale = lax.rsqrt(jnp.mean(values * values, axis=-1, keepdims=True) + norm_eps)
                normed = values * scale
                d_out = part[seq, at, :].astype(jnp.float32) + came[at, :].astype(jnp.float32)
                total[...] += d_out * normed
                scaled = d_out * here[8][0:1, :]
                mean = jnp.mean(scaled * normed, axis=-1, keepdims=True)
                d_in = here[6][at, :] + scale * (scaled - normed * mean)
                grad[at, :] = d_in.astype(grad.dtype)
                return carry

            lax.fori_loop(0, tok_rows // ROW_TILE, step, 0)
            summed = jnp.sum(total[...], axis=0, keepdims=True)
            for n in range(blocks):
                here[7][n, 0:1, :] = summed[:, n * rows : (n + 1) * rows]
            self.out.start()

        pairs = blocks // 2
        found = [functools.partial(multiply, i, i + 2) for i in range(0, pairs, 2)]
        return found + [send, norm_back]

    def at_step(self, tasks, i, steps):
        parts = len(self.part_shapes) - 1
        last = 3 * (steps - AHEAD) // (parts + 1) - AHEAD - 1
        if i < len(tasks) - 2:
            return [tasks[i]] + ([tasks[-2]] if i == len(tasks) - 3 else [])
        return [tasks[-1]] if i == last else []

    def finish(self):
        self.exchange.wait_send()
        self.out.wait()


def scatter_sum(parts, collective_id, out_dtype, seq_count=1, sides=(), work=None):
    work = work or NoWork()
    count = lax.axis_size("shard")
    shapes = list(work.part_shapes) or parts
    arrays = len(shapes)
    lead = (seq_count,) if seq_count > 1 else ()
    others = max(seq_count - 1, 1)
    return pl.pallas_call(
        functools.partial(scatter_kernel, count, seq_count, arrays, len(sides), work),
        out_shape=[jax.ShapeDtypeStruct(lead + p.shape[1:], out_dtype) for p in shapes]
        + [jax.ShapeDtypeStruct(s.shape, s.dtype) for s in sides]
        + list(work.results),
        in_specs=[pl.BlockSpec(memory_space=pltpu.VMEM)] * len(parts)
        + [pl.BlockSpec(memory_space=pl.ANY)] * (len(sides) + work.inputs),
        out_specs=[pl.BlockSpec(memory_space=pltpu.VMEM)] * arrays
        + [pl.BlockSpec(memory_space=pl.ANY)] * (len(sides) + work.outputs),
        scratch_shapes=[pltpu.VMEM(p.shape, p.dtype) for p in list(work.part_shapes) + list(shapes)]
        + [
            pltpu.SemaphoreType.DMA((arrays, count)),
            pltpu.SemaphoreType.DMA((arrays, count)),
            pltpu.SemaphoreType.DMA((arrays, others)),
            pltpu.SemaphoreType.DMA((arrays, others)),
            pltpu.SemaphoreType.DMA((max(len(sides), 1),)),
            pltpu.SemaphoreType.DMA((max(len(sides), 1),)),
        ]
        + list(work.scratch),
        compiler_params=pltpu.CompilerParams(
            collective_id=collective_id, has_side_effects=True, vmem_limit_bytes=VMEM_LIMIT
        ),
        name="scatter_sum_%d" % collective_id,
    )(*parts, *sides, *work.operands)


def place_kernel(refs_in, seq_count, *refs):
    for i, o in enumerate(refs_in):
        out_ref, base = refs[len(refs_in) + o[0]], o[1]
        cols = refs[i].shape[2]
        for s in range(seq_count):
            out_ref[:, base + s * cols : base + (s + 1) * cols] = refs[i][s].astype(out_ref.dtype)


def place_rows(pieces, targets, out_cols):
    seq_count, rows, _ = pieces[0].shape
    return pl.pallas_call(
        functools.partial(place_kernel, targets, seq_count),
        out_shape=[jax.ShapeDtypeStruct((rows, cols), jnp.float32) for cols in out_cols],
        in_specs=[pl.BlockSpec(memory_space=pltpu.VMEM)] * len(pieces),
        out_specs=[pl.BlockSpec(memory_space=pltpu.VMEM)] * len(out_cols),
        name="place_rows",
    )(*pieces)


def expert_kernel(count, *refs):
    (ffn_own, grad_own, weight), refs = refs[:3], refs[3:]
    matrices, refs = refs[:3], refs[3:]
    (rows_out, hidden_out, mixed_out, expert_out, gate_out, up_out), refs = refs[:6], refs[6:]
    pair_out, refs = refs[:2], refs[2:]
    (ffn_all, grad_all, gate_w, up_w, down_w, gate_all, up_all), refs = refs[:7], refs[7:]
    (hidden_at, mixed_at, expert_at, gate_at, up_at, left_at, right_at), refs = refs[:7], refs[7:]
    ffn_send, ffn_recv, grad_send, grad_recv, load, own_sem, rows_sem, out_sem = refs
    me = lax.axis_index("shard")
    seq = lax.axis_index("seq")
    tiles = count // 2
    low, f32 = ffn_own.dtype, jnp.float32
    ffn = Line(count, ffn_own, ffn_all, ffn_send, ffn_recv, seq, 2)
    grad = Line(count, grad_own, grad_all, grad_send, grad_recv, seq, 2)
    ffn.meet()
    ffn.start(0)
    loads = [
        pltpu.make_async_copy(source, target, load.at[i])
        for i, (source, target) in enumerate(zip(matrices, (gate_w, up_w, down_w)))
    ]
    for copy in loads:
        copy.start()
    ffn_keep = pltpu.make_async_copy(ffn_own, ffn_all.at[me], own_sem.at[0])
    grad_keep = pltpu.make_async_copy(grad_own, grad_all.at[me], own_sem.at[1])
    ffn_keep.start()
    grad_keep.start()
    ffn_keep.wait()
    for copy in loads:
        copy.wait()

    tile_of = ffn.pair

    def put(number, slot, staged, target, tile):
        return pltpu.make_async_copy(staged.at[slot], target.at[tile], out_sem.at[number, slot])

    def keep_rows(tile):
        return pltpu.make_async_copy(
            ffn_all.at[pl.ds(2 * tile, 2)], rows_out.at[pl.ds(2 * tile, 2)], rows_sem.at[tile]
        )

    def arrivals(way, i, extra):
        done = 0
        for at in range(tiles):
            upto = way.order.index(2 * at) + 1 if at else 0
            order = way.order[done:upto]
            done = max(done, upto)

            @pl.when(i == at)
            def _(at=at, order=order):
                for r in order:
                    way.arrive(r)
                if at in extra:
                    extra[at]()
                way.wait_twin(2 * at)

    columns = gate_w.shape[1] // 2

    def forward(i, carry):
        arrivals(ffn, i, {tiles - 3: lambda: grad.start(0)})
        tile = tile_of(i)
        slot = lax.rem(i, 2)
        keep_rows(tile).start()

        @pl.when(i >= 2)
        def _():
            put(0, slot, hidden_at, hidden_out, tile_of(i - 2)).wait()
            put(1, slot, mixed_at, mixed_out, tile_of(i - 2)).wait()

        rows = ffn_all[pl.ds(2 * tile, 2)].reshape(-1, ffn_all.shape[2])
        for c in range(2):
            at = slice(c * columns, (c + 1) * columns)
            gate = jnp.dot(rows, gate_w[:, at], preferred_element_type=f32)
            up = jnp.dot(rows, up_w[:, at], preferred_element_type=f32)
            gate_all[i, :, at] = gate
            up_all[i, :, at] = up
            hidden_at[slot, :, at] = (gate * jax.nn.sigmoid(gate) * up).astype(low)
        put(0, slot, hidden_at, hidden_out, tile).start()
        half = down_w.shape[1] // 2
        for c in range(2):
            at = slice(c * half, (c + 1) * half)
            result = jnp.dot(hidden_at[slot], down_w[:, at], preferred_element_type=f32)
            mixed_at[slot, :, at] = (result.astype(low).astype(f32) * weight[tile]).astype(low)
        put(1, slot, mixed_at, mixed_out, tile).start()
        return carry

    lax.fori_loop(0, tiles, forward, 0)
    grad_keep.wait()

    def backward(i, carry):
        arrivals(grad, i, {})
        tile = tile_of(i)
        slot = lax.rem(i, 2)

        @pl.when(i >= 2)
        def _():
            before = tile_of(i - 2)
            put(2, slot, expert_at, expert_out, before).wait()
            put(3, slot, gate_at, gate_out, before).wait()
            put(4, slot, up_at, up_out, before).wait()
            put(5, slot, left_at, pair_out[0], before).wait()
            put(6, slot, right_at, pair_out[1], before).wait()

        rows = grad_all[pl.ds(2 * tile, 2)].reshape(-1, grad_all.shape[2])
        expert_at[slot] = (rows.astype(f32) * weight[tile]).astype(low)
        put(2, slot, expert_at, expert_out, tile).start()
        for c in range(2):
            at = slice(c * columns, (c + 1) * columns)
            d_hidden = contract_cols(expert_at[slot], down_w[at, :])
            gate, up = gate_all[i, :, at], up_all[i, :, at]
            sigma = jax.nn.sigmoid(gate)
            gate_at[slot, :, at] = (
                d_hidden * up * sigma * (1.0 + gate * (1.0 - sigma))
            ).astype(low)
            up_at[slot, :, at] = (d_hidden * (gate * sigma)).astype(low)
        put(3, slot, gate_at, gate_out, tile).start()
        put(4, slot, up_at, up_out, tile).start()
        half = gate_w.shape[0] // 2
        for c, staged in enumerate((left_at, right_at)):
            at = slice(c * half, (c + 1) * half)
            staged[slot] = (
                contract_cols(gate_at[slot], gate_w[at, :]) + contract_cols(up_at[slot], up_w[at, :])
            ).astype(low)
            put(5 + c, slot, staged, pair_out[c], tile).start()
        return carry

    lax.fori_loop(0, tiles, backward, 0)
    ffn.finish()
    grad.finish()
    for i in range(tiles):
        keep_rows(i).wait()
    outs = (hidden_out, mixed_out, expert_out, gate_out, up_out, pair_out[0], pair_out[1])
    staged = (hidden_at, mixed_at, expert_at, gate_at, up_at, left_at, right_at)
    for i in (tiles - 2, tiles - 1):
        for number in range(7):
            put(number, i % 2, staged[number], outs[number], tile_of(i)).wait()


def run_experts(ffn_in, own_grad, weight, gate_w, up_w, down_w, collective_id):
    count = lax.axis_size("shard")
    rows, width = ffn_in.shape
    inner = gate_w.shape[1]
    tiles, two = count // 2, 2 * rows
    low = ffn_in.dtype
    shape = jax.ShapeDtypeStruct
    wide, narrow = (tiles, two, width), (tiles, two, inner)
    outs = [shape((count, rows, width), low)]
    outs += [shape(s, low) for s in (narrow, wide, wide, narrow, narrow)]
    outs += [shape((tiles, two, width // 2), low)] * 2
    vmem, hbm = pl.BlockSpec(memory_space=pltpu.VMEM), pl.BlockSpec(memory_space=pl.ANY)
    staged = [inner, width, width, inner, inner, width // 2, width // 2]
    return pl.pallas_call(
        functools.partial(expert_kernel, count),
        out_shape=outs,
        in_specs=[vmem] * 3 + [hbm] * 3,
        out_specs=[hbm] * len(outs),
        scratch_shapes=[
            pltpu.VMEM((count, rows, width), low),
            pltpu.VMEM((count, rows, width), low),
            pltpu.VMEM(gate_w.shape, low),
            pltpu.VMEM(up_w.shape, low),
            pltpu.VMEM(down_w.shape, low),
            pltpu.VMEM((tiles, two, inner), jnp.float32),
            pltpu.VMEM((tiles, two, inner), jnp.float32),
        ]
        + [pltpu.VMEM((2, two, cols), low) for cols in staged]
        + [pltpu.SemaphoreType.DMA((2, count + 1))] * 4
        + [
            pltpu.SemaphoreType.DMA((3,)),
            pltpu.SemaphoreType.DMA((2,)),
            pltpu.SemaphoreType.DMA((tiles,)),
            pltpu.SemaphoreType.DMA((len(staged), 2)),
        ],
        compiler_params=pltpu.CompilerParams(
            collective_id=collective_id, has_side_effects=True, vmem_limit_bytes=VMEM_LIMIT
        ),
        name="run_experts",
    )(ffn_in, own_grad, weight, gate_w, up_w, down_w)


GAIN_LANES = 128


def pair_tables(expert_list, prob_list, expert_count):
    numbers = jnp.arange(expert_count, dtype=jnp.int32)
    named = expert_list[None, :, :] == numbers[:, None, None]
    return jnp.sum(jnp.where(named, prob_list[None], 0.0), axis=2)


def shards(
    layer_input,
    seq_lengths,
    seq_order,
    expert_ids,
    expert_probs,
    weight_qkv,
    weight_out,
    norm_gains,
    weight_gate,
    weight_up,
    weight_down,
    out_cotangent,
):
    width = layer_input.shape[-1]
    tok_rows = layer_input.shape[1]
    seq_count = lax.axis_size("seq")
    seq_at = lax.axis_index("seq")
    group_tok = tok_rows * seq_count
    experts = lax.axis_size("shard")
    shard_at = lax.axis_index("shard")
    weight_rows = weight_qkv.shape[0]
    heads_local = HEADS // seq_count
    local_width = heads_local * HEAD_DIM
    out_cols = width // seq_count
    score_scale = HEAD_DIM ** (-0.5)
    low = jnp.bfloat16
    f32 = jnp.float32

    def take_seq(array, axis):
        return lax.dynamic_index_in_dim(array, seq_at, axis, keepdims=False)

    def seq_sum(part):
        if seq_count != 2:
            return lax.psum_scatter(part, "seq", scatter_dimension=0, tiled=True).astype(f32)
        halves = part.reshape(2, part.shape[0] // 2, part.shape[1])
        there = lax.dynamic_index_in_dim(halves, 1 - seq_at, 0, keepdims=False)
        here = lax.dynamic_index_in_dim(halves, seq_at, 0, keepdims=False)
        came = lax.ppermute(there, "seq", [(0, 1), (1, 0)])
        return here.astype(f32) + came.astype(f32)

    own_cols = take_seq(weight_qkv.reshape(weight_rows, 3, seq_count, local_width), 2)
    own_gains = jnp.pad(norm_gains, ((0, 0), (0, GAIN_LANES - norm_gains.shape[1])))
    table = pair_tables(expert_ids[0], expert_probs[0], experts)
    own_block = jnp.concatenate(
        [own_cols.reshape(weight_rows, 3 * local_width), own_gains], axis=1
    )
    qkv_cols, tables_all = gather_blocks([own_block, table], 1, ((0, 1),), (2, 1))
    own_out, qkv_cols = lax.optimization_barrier((weight_out, qkv_cols))
    full_out = lax.all_gather(own_out, "shard", axis=0, tiled=True)
    qkv_all = qkv_cols
    qkv_cols = qkv_cols.reshape(width, 3 * local_width + GAIN_LANES)
    gain_cols = qkv_cols[:, 3 * local_width :][:, : norm_gains.shape[1]].astype(f32)
    qkv_cols = qkv_cols[:, : 3 * local_width]
    group_in = lax.all_gather(layer_input[0], "seq", axis=0, tiled=True).astype(f32)
    pair_weight = lax.dynamic_index_in_dim(tables_all, shard_at, 1, keepdims=False)

    segment, position = group_layout(seq_lengths[0], seq_order[0], group_tok)
    places = jnp.arange(group_tok, dtype=jnp.int32)
    allowed = (segment[:, None] == segment[None, :]) & (places[None, :] <= places[:, None])
    cosine, sine_part = rope_tables(position, HEAD_DIM)

    def rope(values):
        return rotate(
            values.reshape(group_tok, heads_local, HEAD_DIM), cosine, sine_part
        ).reshape(group_tok, local_width)

    def rope_back(grads):
        return rotate(
            grads.reshape(group_tok, heads_local, HEAD_DIM), cosine, -sine_part
        ).reshape(group_tok, local_width)

    gain_q = lax.dynamic_slice_in_dim(gain_cols[:, 1], seq_at * local_width, local_width)
    gain_k = lax.dynamic_slice_in_dim(gain_cols[:, 2], seq_at * local_width, local_width)

    group_r = lax.rsqrt(jnp.mean(group_in * group_in, axis=-1, keepdims=True) + norm_eps)
    group_n = group_in * group_r
    attn_in = (group_n * gain_cols[:, 0]).astype(low)
    projected = jnp.dot(attn_in, qkv_cols, preferred_element_type=f32)
    q_raw = projected[:, :local_width]
    k_raw = projected[:, local_width : 2 * local_width]
    value = projected[:, 2 * local_width :].astype(low)
    squares = jnp.stack([jnp.sum(q_raw * q_raw, axis=-1), jnp.sum(k_raw * k_raw, axis=-1)])
    squares = lax.psum(squares, "seq")
    q_r, k_r = (lax.rsqrt(row / width + norm_eps)[:, None] for row in squares)
    q_n = q_raw * q_r
    k_n = k_raw * k_r
    query = rope(q_n * gain_q).astype(low)
    key = rope(k_n * gain_k).astype(low)
    query_head = query.reshape(group_tok, heads_local, HEAD_DIM)
    key_head = key.reshape(group_tok, heads_local, HEAD_DIM)
    value_head = value.reshape(group_tok, heads_local, HEAD_DIM)
    scores = jnp.einsum("ihd,jhd->hij", query_head, key_head, preferred_element_type=f32)
    scores = jnp.where(allowed[None], scores * score_scale, -1e30)
    score_peak = jnp.max(scores, axis=-1, keepdims=True)
    weights_exp = jnp.exp(scores - score_peak)
    attn_probs = weights_exp / jnp.sum(weights_exp, axis=-1, keepdims=True)
    probs_low = attn_probs.astype(low)
    mix_head = jnp.einsum("hij,jhd->ihd", probs_low, value_head, preferred_element_type=f32)
    mix_head = mix_head.astype(low).reshape(group_tok, local_width)
    attn_mix = lax.all_to_all(mix_head, "seq", split_axis=0, concat_axis=1, tiled=True)
    mix_all = lax.all_gather(mix_head, "seq", axis=1, tiled=True)
    resid = layer_input[0].astype(f32) + jnp.dot(attn_mix, full_out, preferred_element_type=f32)
    ffn_r = lax.rsqrt(jnp.mean(resid * resid, axis=-1, keepdims=True) + norm_eps)
    ffn_n = resid * ffn_r
    ffn_in = (ffn_n * gain_cols[:, 3]).astype(low)

    pairs = seq_count == 2
    gate_weight = weight_gate[0]
    up_weight = weight_up[0]
    down_weight = weight_down[0]
    if experts == LINE:
        tile_weight = pair_weight.reshape(experts // 2, 2 * tok_rows, 1)
        results = run_experts(
            ffn_in, out_cotangent[0], tile_weight, gate_weight, up_weight, down_weight, 2
        )
        rows_in, hidden, out_part, d_expert, d_gate, d_up, *halves = (
            result.reshape(experts * tok_rows, -1) for result in results
        )
    else:
        slot_weight = pair_weight.reshape(-1, 1)
        (ffn_all, grad_all) = gather_blocks(
            [ffn_in, out_cotangent[0]], 2, ((0,), (1,)), (1, 1)
        )
        rows_in = ffn_all.reshape(-1, width)
        gate = jnp.dot(rows_in, gate_weight, preferred_element_type=f32)
        up = jnp.dot(rows_in, up_weight, preferred_element_type=f32)
        sigma = jax.nn.sigmoid(gate)
        silu = gate * sigma
        hidden = (silu * up).astype(low)
        expert_out = jnp.dot(hidden, down_weight, preferred_element_type=f32).astype(low)
        out_part = (expert_out.astype(f32) * slot_weight).astype(low)
        d_expert = (grad_all.reshape(-1, width).astype(f32) * slot_weight).astype(low)
        d_hidden = contract_cols(d_expert, down_weight)
        d_gate = (d_hidden * up * sigma * (1.0 + gate * (1.0 - sigma))).astype(low)
        d_up = (d_hidden * silu).astype(low)
        d_pair = contract_cols(d_gate, gate_weight) + contract_cols(d_up, up_weight)
        halves = jnp.split(d_pair.astype(low), 2, axis=1)
    halves = [part.reshape(experts, tok_rows, -1) for part in halves]
    products = [(hidden, d_expert), (rows_in, d_gate), (rows_in, d_up)]
    if pairs:
        results = scatter_sum(halves, 3, f32, work=ExpertGrads(products))
        d_left, d_right, down_came, down_mine, gate_there, gate_mine, up_there, up_mine = results
    else:
        d_left, d_right = scatter_sum(halves, 3, f32)
    d_ffn_in = jnp.concatenate([d_left, d_right], axis=1)
    out_part, d_ffn_in = lax.optimization_barrier((out_part, d_ffn_in))
    mixed_out = lax.psum_scatter(
        out_part, "shard", scatter_dimension=0, tiled=True
    )

    grad_tokens = out_cotangent[0].astype(f32)
    d_scaled = d_ffn_in * gain_cols[:, 3]
    d_resid = grad_tokens + ffn_r * (
        d_scaled - ffn_n * jnp.mean(d_scaled * ffn_n, axis=-1, keepdims=True)
    )
    grad_g_ffn = jnp.sum(d_ffn_in * ffn_n, axis=0)
    d_branch = d_resid.astype(low)
    d_mix = contract_cols(d_branch, full_out).astype(low)
    d_mix_head = lax.all_to_all(d_mix, "seq", split_axis=1, concat_axis=0, tiled=True).reshape(
        group_tok, heads_local, HEAD_DIM
    )
    branch_cols = lax.all_to_all(d_branch, "seq", split_axis=1, concat_axis=0, tiled=True)
    d_probs = jnp.einsum("ihd,jhd->hij", d_mix_head, value_head, preferred_element_type=f32)
    delta_rows = jnp.sum(attn_probs * d_probs, axis=-1, keepdims=True)
    d_scores = (attn_probs * (d_probs - delta_rows)).astype(low)
    d_query = (
        jnp.einsum("hij,jhd->ihd", d_scores, key_head, preferred_element_type=f32) * score_scale
    ).astype(low)
    d_key = (
        jnp.einsum("hij,ihd->jhd", d_scores, query_head, preferred_element_type=f32) * score_scale
    ).astype(low)
    d_value = jnp.einsum(
        "hij,ihd->jhd", probs_low, d_mix_head, preferred_element_type=f32
    ).astype(low)
    dq_rot = rope_back(d_query.reshape(group_tok, local_width).astype(f32))
    dk_rot = rope_back(d_key.reshape(group_tok, local_width).astype(f32))
    grad_g_q = jnp.sum(dq_rot * q_n, axis=0)
    grad_g_k = jnp.sum(dk_rot * k_n, axis=0)
    dq_scaled = dq_rot * gain_q
    dk_scaled = dk_rot * gain_k
    dots = jnp.stack([jnp.sum(dq_scaled * q_n, axis=-1), jnp.sum(dk_scaled * k_n, axis=-1)])
    dots = lax.psum(dots, "seq") / width
    if pairs:
        dots, gate_there = lax.optimization_barrier((dots, gate_there))
        gate_came = lax.ppermute(gate_there, "seq", [(0, 1), (1, 0)])
    dq_raw = q_r * (dq_scaled - q_n * dots[0][:, None])
    dk_raw = k_r * (dk_scaled - k_n * dots[1][:, None])
    d_qkv = jnp.concatenate(
        [dq_raw.astype(low), dk_raw.astype(low), d_value.reshape(group_tok, local_width)], axis=1
    )
    zeros = jnp.zeros((width,), f32)
    gain_rows = [
        zeros,
        lax.dynamic_update_slice_in_dim(zeros, grad_g_q, seq_at * local_width, 0),
        lax.dynamic_update_slice_in_dim(zeros, grad_g_k, seq_at * local_width, 0),
        grad_g_ffn,
    ]
    if pairs:
        gain_terms = jnp.stack(gain_rows).reshape(len(gain_rows), experts, weight_rows)
        gain_terms = jnp.pad(
            jnp.swapaxes(gain_terms, 0, 1), ((0, 0), (0, ROW_TILE - len(gain_rows)), (0, 0))
        )
        work = AttentionGrads(
            attn_in,
            d_qkv,
            mix_all,
            branch_cols,
            qkv_all,
            layer_input[0],
            d_resid,
            gain_terms,
            jnp.broadcast_to(gain_cols[:, 0], (8, width)),
        )
        *sums, sum_gains, up_came, input_grad = scatter_sum(
            [], 4, low, seq_count, sides=[up_there], work=work
        )
        sum_gate, sum_up, sum_down = (
            mine.astype(f32) + came.astype(f32)
            for mine, came in ((gate_mine, gate_came), (up_mine, up_came), (down_mine, down_came))
        )
        rows_gain = jnp.sum(sum_gains[:, : norm_gains.shape[1]].astype(f32), axis=0).T
    else:
        d_attn_in = seq_sum(contract_cols(d_qkv, qkv_cols).astype(low))
        own_n = lax.dynamic_slice_in_dim(group_n, seq_at * tok_rows, tok_rows)
        own_r = lax.dynamic_slice_in_dim(group_r, seq_at * tok_rows, tok_rows)
        dx_scaled = d_attn_in * gain_cols[:, 0]
        dx_norm = own_r * (
            dx_scaled - own_n * jnp.mean(dx_scaled * own_n, axis=-1, keepdims=True)
        )
        gain_rows[0] = jnp.sum(d_attn_in * own_n, axis=0)
        input_grad = (d_resid + dx_norm).astype(low)
        gain_terms = jnp.stack(gain_rows, axis=1)
        gain_terms = jnp.pad(gain_terms, ((0, 0), (0, GAIN_LANES - gain_terms.shape[1])))
        terms = [
            contract_rows(attn_in, d_qkv[:, i * local_width : (i + 1) * local_width])
            for i in range(3)
        ]
        terms += [contract_rows(mix_all, branch_cols), gain_terms]
        terms = [term.astype(low).reshape(experts, weight_rows, -1) for term in terms]
        *sums, sum_gains = scatter_sum(terms, 4, low, seq_count)
        sum_down, sum_gate, sum_up = (
            lax.psum_scatter(
                contract_rows(left, right).astype(low), "seq", scatter_dimension=0, tiled=True
            ).astype(f32)
            for left, right in products
        )
        rows_gain = jnp.sum(sum_gains[:, :, : norm_gains.shape[1]].astype(f32), axis=0)
    mixed_out, sums[0] = lax.optimization_barrier((mixed_out, sums[0]))
    layer_output = (resid + mixed_out.astype(f32)).astype(low)
    targets = [(0, 0), (0, width), (0, 2 * width), (1, 0)]
    rows_qkv, rows_out = place_rows(sums, targets, (3 * width, width))
    return (
        layer_output[None],
        input_grad[None],
        rows_qkv,
        rows_out,
        rows_gain,
        sum_gate[None],
        sum_up[None],
        sum_down[None],
    )


def solution(mesh):
    in_specs = (
        P("shard", "seq", None),
        P("shard", None),
        P("shard", None),
        P("shard", "seq", None),
        P("shard", "seq", None),
        P("shard", None),
        P("shard", None),
        P("shard", None),
        P("shard", None, None),
        P("shard", None, None),
        P("shard", None, None),
        P("shard", "seq", None),
    )
    out_specs = (
        P("shard", "seq", None),
        P("shard", "seq", None),
        P("shard", None),
        P("shard", None),
        P("shard", None),
        P("shard", "seq", None),
        P("shard", "seq", None),
        P("shard", "seq", None),
    )
    return jax.shard_map(shards, mesh=mesh, in_specs=in_specs, out_specs=out_specs, check_vma=False)
```

```python
import functools

import jax
import jax.numpy as jnp
from jax import lax
from jax.experimental import pallas as pl
from jax.experimental.pallas import tpu as pltpu
from jax.sharding import PartitionSpec as P

HEADS = 16
HEAD_DIM = 128


norm_eps = 1e-05
rope_base = 10000.0


def rms_scale(values, gain_col):
    return (
        values * lax.rsqrt(jnp.mean(values * values, axis=-1, keepdims=True) + norm_eps) * gain_col
    )


def rotate(values, cosine, sine_part):
    half_dim = values.shape[-1] // 2
    first_half = values[..., :half_dim]
    second_half = values[..., half_dim:]
    return jnp.concatenate(
        [
            first_half * cosine - second_half * sine_part,
            second_half * cosine + first_half * sine_part,
        ],
        axis=-1,
    )


def rope_tables(position, head_size):
    half_dim = head_size // 2
    frequency = rope_base ** (-2.0 * jnp.arange(half_dim, dtype=jnp.float32) / head_size)
    angles = position.astype(jnp.float32)[:, None] * frequency[None, :]
    return (jnp.cos(angles)[:, None, :], jnp.sin(angles)[:, None, :])


def group_layout(lengths, seq_perm, group_tok):
    seq_count = lengths.shape[0]
    numbers = jnp.arange(seq_count, dtype=jnp.int32)
    packed = jnp.sum(jnp.where(seq_perm[:, None] == numbers[None, :], lengths[None, :], 0), axis=1)
    seq_ends = jnp.cumsum(packed)
    seq_starts = seq_ends - packed
    places = jnp.arange(group_tok, dtype=jnp.int32)
    segment = jnp.sum((places[:, None] >= seq_ends[None, :]).astype(jnp.int32), axis=1)
    begins = jnp.sum(
        jnp.where(segment[:, None] == numbers[None, :], seq_starts[None, :], 0), axis=1
    )
    return (segment, places - begins)


def contract_rows(left_side, right_side):
    return lax.dot_general(
        left_side, right_side, (((0,), (0,)), ((), ())), preferred_element_type=jnp.float32
    )


def contract_cols(left_side, right_side):
    return lax.dot_general(
        left_side, right_side, (((1,), (1,)), ((), ())), preferred_element_type=jnp.float32
    )


MESH_ID = pl.DeviceIdType.MESH
VMEM_LIMIT = 60 * 1024 * 1024
ROW_TILE = 16
GRAD_TILE = 256


def low_bit(index):
    return index & -index


def bit_list(count):
    return [1 << b for b in range(count.bit_length() - 1)]


def relative_place(count, me):
    values = [(bit, lax.rem(me // bit, 2)) for bit in bit_list(count)]

    def place(r):
        total = 0
        for bit, value in values:
            total = total + bit * ((1 - value) if r & bit else value)
        return total

    return place


def meet(count, place, seq, seq_count=1):
    barrier = pltpu.get_barrier_semaphore()
    for bit in bit_list(count):
        pl.semaphore_signal(barrier, 1, device_id=(seq, place(bit)), device_id_type=MESH_ID)
    for j in range(1, seq_count):
        pl.semaphore_signal(
            barrier, 1, device_id=(lax.rem(seq + j, seq_count), place(0)), device_id_type=MESH_ID
        )
    pl.semaphore_wait(barrier, len(bit_list(count)) + seq_count - 1)


def remote(src, dst, send_sem, recv_sem, device):
    return pltpu.make_async_remote_copy(
        src_ref=src,
        dst_ref=dst,
        send_sem=send_sem,
        recv_sem=recv_sem,
        device_id=device,
        device_id_type=MESH_ID,
    )


def arrival_order(count):
    def key(r):
        later = r >> 2
        return (later + ((r >> 1) & 1), (r >> 1) & 1)

    return sorted(range(2, count, 2), key=key)


LINE = 16


class Line:
    def __init__(self, count, own, full, send, recv, seq, pieces=1):
        me = lax.axis_index("shard")
        spot = me // 4
        self.upper = spot // 2
        self.inner = spot + self.upper * (3 - 2 * spot)
        self.y = lax.rem(me // 2, 2)
        self.core = lax.rem(me, 2)
        low = lax.rem(me, 4)
        near = (seq, self.block(1) * 4 + low)
        far = (seq, (3 - spot) * 4 + low)
        across = (seq, spot * 4 + (1 - self.y) * 2 + self.core)
        twin = (seq, spot * 4 + self.y * 2 + 1 - self.core)
        self.peers = (near, far, across, twin)
        self.copies = []
        self.inward = []
        rows = own.shape[0] // pieces
        for p in range(pieces):
            at = pl.ds(p * rows, rows)
            target = [full.at[self.place(r), at] for r in range(count)]
            source = [own.at[at]] + target[1:]

            def copy(r, sent, received, device, source=source, target=target, p=p):
                return remote(
                    source[r], target[r], send.at[p, sent], recv.at[p, received], device
                )

            copies = {4: copy(0, 4, 4, near)}
            for r in range(0, count, 4):
                copies[r | 2] = copy(r, r | 2, r | 2, across)
            for r in range(0, count, 2):
                copies[r | 1] = copy(r, r | 1, r | 1, twin)
            inward = {0: copy(0, 8, 8, far), 4: copy(4, 12, 12, far)}
            inward[8] = copy(8, 0, 8, near)
            inward[12] = copy(12, count, 12, near)
            copies[8] = inward[0]
            copies[12] = inward[4]
            self.copies.append(copies)
            self.inward.append(inward)

    def block(self, k):
        if isinstance(k, int):
            spot = k if k >= 2 else self.inner + k * (1 - 2 * self.inner)
        else:
            far = k // 2
            spot = far * k + (1 - far) * lax.rem(k + self.inner, 2)
        return spot + self.upper * (3 - 2 * spot)

    def place(self, r):
        y = (1 - self.y) if r & 2 else self.y
        core = (1 - self.core) if r & 1 else self.core
        return self.block(r >> 2) * 4 + y * 2 + core

    def pair(self, i):
        k, y = i // 2, lax.rem(i, 2)
        return self.block(k) * 2 + self.y + y - 2 * self.y * y

    def meet(self):
        barrier = pltpu.get_barrier_semaphore()
        for peer in self.peers:
            pl.semaphore_signal(barrier, 1, device_id=peer, device_id_type=MESH_ID)
        pl.semaphore_wait(barrier, len(self.peers))

    def start(self, r):
        for p in range(len(self.copies)):
            self.start_piece(p, r)

    def start_piece(self, p, r):
        copies, inward = self.copies[p], self.inward[p]
        if r == 0:
            copies[4].start()
        if r % 4 == 0:

            @pl.when(self.inner == 1)
            def _():
                inward[r].start()

            copies[r | 2].start()
        copies[r | 1].start()

    def arrive(self, r):
        for p in range(len(self.copies)):
            self.copies[p][r].wait_recv()
            self.start_piece(p, r)

    def wait_twin(self, r):
        for copies in self.copies:
            copies[r | 1].wait_recv()

    order = (4, 2, 8, 6, 12, 10, 14)

    def finish(self):
        for copies, inward in zip(self.copies, self.inward):
            for r in (4, 2, 6, 10, 14, 1, 3, 5, 7, 9, 11, 13, 15):
                copies[r].wait_send()

            @pl.when(self.inner == 1)
            def _(inward=inward):
                for copy in inward.values():
                    copy.wait_send()


class Tree:
    def __init__(self, count, own, full, send, recv, seq, pieces=1):
        self.count, self.seq = count, seq
        self.place = relative_place(count, lax.axis_index("shard"))
        self.order = arrival_order(count)
        self.copies = {}
        for r in range(count):
            below = low_bit(r) if r else count
            for bit in bit_list(count):
                if bit < below:
                    self.copies[r | bit] = remote(
                        own if r == 0 else full.at[self.place(r)],
                        full.at[self.place(r)],
                        send.at[0, r | bit],
                        recv.at[0, r | bit],
                        (seq, self.place(bit)),
                    )

    def meet(self):
        meet(self.count, self.place, self.seq)

    def start(self, r):
        below = low_bit(r) if r else self.count
        bits = [bit for bit in bit_list(self.count) if bit < below]
        for bit in sorted(bits, key=lambda bit: (bit < 4, bit)):
            self.copies[r | bit].start()

    def arrive(self, r):
        self.copies[r].wait_recv()
        self.start(r)

    def wait_twin(self, r):
        self.copies[r | 1].wait_recv()

    def finish(self):
        for copy in self.copies.values():
            copy.wait_send()


def gather_kernel(count, groups, pieces, *refs):
    arrays = sum(len(group) for group in groups)
    own, full = refs[:arrays], refs[arrays : 2 * arrays]
    send, recv, local = refs[2 * arrays :]
    me = lax.axis_index("shard")
    seq = lax.axis_index("seq")
    kind = Line if count == LINE else Tree
    ways = [
        kind(count, own[a], full[a], send.at[a], recv.at[a], seq, pieces[a])
        for a in range(arrays)
    ]
    ways[0].meet()
    keeps = []
    for a in range(arrays):
        keep = pltpu.make_async_copy(own[a], full[a].at[me], local.at[a])
        keep.start()
        keeps.append(keep)
    for group in groups:
        for a in group:
            ways[a].start(0)
        for r in ways[0].order:
            for a in group:
                ways[a].arrive(r)
    for a in range(arrays):
        for r in range(0, count, 2):
            ways[a].wait_twin(r)
    for way in ways:
        way.finish()
    for keep in keeps:
        keep.wait()


def gather_blocks(blocks, collective_id, groups=((0,),), pieces=(1,)):
    count = lax.axis_size("shard")
    arrays = len(blocks)
    return pl.pallas_call(
        functools.partial(gather_kernel, count, groups, pieces),
        out_shape=[jax.ShapeDtypeStruct((count,) + b.shape, b.dtype) for b in blocks],
        in_specs=[pl.BlockSpec(memory_space=pltpu.VMEM)] * arrays,
        out_specs=[pl.BlockSpec(memory_space=pl.ANY)] * arrays,
        scratch_shapes=[
            pltpu.SemaphoreType.DMA((arrays, max(pieces), count + 1)),
            pltpu.SemaphoreType.DMA((arrays, max(pieces), count + 1)),
            pltpu.SemaphoreType.DMA((arrays,)),
        ],
        compiler_params=pltpu.CompilerParams(collective_id=collective_id, has_side_effects=True),
        name="gather_blocks_%d" % collective_id,
    )(*blocks)


def scatter_kernel(count, seq_count, arrays, sides, work, *refs):
    given = 0 if work.part_shapes else arrays
    parts, refs = refs[:given], refs[given:]
    side_from, refs = refs[:sides], refs[sides:]
    work_in, refs = refs[: work.inputs], refs[work.inputs :]
    totals, refs = refs[:arrays], refs[arrays:]
    side_to, refs = refs[:sides], refs[sides:]
    work_out, refs = refs[: work.outputs], refs[work.outputs :]
    if work.part_shapes:
        parts, refs = refs[:arrays], refs[arrays:]
    held, refs = refs[:arrays], refs[arrays:]
    send, recv, seq_send, seq_recv, side_send, side_recv = refs[:6]
    planes = seq_count if seq_count > 1 else 1 + (sides > 0 or work.outputs > 0)
    me = lax.axis_index("shard")
    seq = lax.axis_index("seq")
    place = relative_place(count, me)
    bits = bit_list(count)
    meet(count, place, seq, planes)
    copies = {}
    shared = []

    def start_sides():
        for i in range(sides):
            copy = remote(
                side_from[i], side_to[i], side_send.at[i], side_recv.at[i], (1 - seq, me)
            )
            copy.start()
            shared.append(copy)

    def share(a):
        for j in range(1, seq_count):
            copy = remote(
                totals[a].at[seq],
                totals[a].at[seq],
                seq_send.at[a, j - 1],
                seq_recv.at[a, j - 1],
                (lax.rem(seq + j, seq_count), me),
            )
            copy.start()
            shared.append(copy)

    def start(a, r, source):
        copy = remote(
            source, held[a].at[r], send.at[a, r], recv.at[a, r], (seq, place(low_bit(r)))
        )
        copy.start()
        copies[a, r] = copy

    def fold(a, r, bit):
        came = r | bit
        copies[a, came].wait_recv()
        rows = held[a].shape[1]
        last = bit == bits[-1]

        def step(i, carry):
            at = pl.ds(pl.multiple_of(i * ROW_TILE, ROW_TILE), ROW_TILE)
            if bit == 1:
                mine = parts[a][place(r), at, :]
            else:
                mine = held[a][r | (bit >> 1), at, :]
            value = mine.astype(jnp.float32) + held[a][came, at, :].astype(jnp.float32)
            if last and seq_count > 1:
                totals[a][seq, at, :] = value.astype(totals[a].dtype)
            elif last:
                totals[a][at, :] = value.astype(totals[a].dtype)
            else:
                held[a][came, at, :] = value.astype(held[a].dtype)
            return carry

        lax.fori_loop(0, rows // ROW_TILE, step, 0)
        upper = bit << 1
        if last:
            share(a)
        elif r & upper:
            start(a, r, held[a].at[came])

    chunks = [
        (a, u) for a in work.order or range(arrays) for u in reversed(range(count // 4))
    ]

    def prepare(a, u):
        work.fill(parts, a, place(4 * u) - lax.rem(me, 4))
        for r in (4 * u + 3, 4 * u + 1):
            start(a, r, parts[a].at[place(r)])

    tasks = work.tasks(seq, me, work_in, work_out, refs[6:], start_sides)
    lead = work.ahead if work.part_shapes else len(chunks)
    for a, u in chunks[:lead]:
        prepare(a, u)
    steps = len(chunks) + work.ahead
    for i in range(steps):
        if i + lead < len(chunks):
            prepare(*chunks[i + lead])
        if i < len(chunks):
            a, u = chunks[i]
            fold(a, 4 * u + 2, 1)
            fold(a, 4 * u, 1)
        if i >= work.ahead:
            a, u = chunks[i - work.ahead]
            for bit in bits[1:]:
                if 4 * u % (2 * bit) == 0:
                    fold(a, 4 * u, bit)
        for task in work.at_step(tasks, i, steps):
            task()
    for copy in shared:
        copy.wait_recv()
    for copy in list(copies.values()) + shared:
        copy.wait_send()
    work.finish()


class NoWork:
    inputs = outputs = 0
    operands, results, scratch, part_shapes, order = (), (), (), (), ()
    ahead = 2

    def fill(self, parts, a, base):
        pass

    def tasks(self, seq, me, arrays, results, scratch, start_sides):
        start_sides()
        return []

    def at_step(self, tasks, i, steps):
        return tasks[len(tasks) * i // steps : len(tasks) * (i + 1) // steps]

    def finish(self):
        pass


class ExpertGrads(NoWork):
    def __init__(self, products):
        self.operands = []
        for pair in products:
            for array in pair:
                if not any(array is other for other in self.operands):
                    self.operands.append(array)
        self.pairs = [
            tuple(next(i for i, o in enumerate(self.operands) if o is array) for array in pair)
            for pair in products
        ]
        low = products[0][0].dtype
        shapes = [(left.shape[1] // 2, right.shape[1]) for left, right in products]
        halves = [jax.ShapeDtypeStruct(shape, low) for shape in shapes for _ in range(2)]
        self.results = halves
        self.inputs, self.outputs = len(self.operands), len(self.results)
        self.scratch = [pltpu.VMEM(a.shape, a.dtype) for a in self.operands]
        self.scratch += [pltpu.VMEM(h.shape, h.dtype) for h in halves]
        self.scratch += [
            pltpu.SemaphoreType.DMA((self.inputs,)),
            pltpu.SemaphoreType.DMA((self.outputs,)),
            pltpu.SemaphoreType.DMA((2,)),
        ]

    def tasks(self, seq, me, arrays, results, scratch, start_sides):
        start_sides()
        here, scratch = scratch[: self.inputs], scratch[self.inputs :]
        tiles, (in_sem, out_sem, side_sem) = scratch[: self.outputs], scratch[self.outputs :]
        loads = [
            pltpu.make_async_copy(arrays[i], here[i], in_sem.at[i]) for i in range(self.inputs)
        ]
        for load in loads:
            load.start()
        waited = set()
        self.open = []
        self.remote = None

        def multiply(p, k, first, last):
            left, right = self.pairs[p]
            out = tiles[2 * p + k]
            for i in (left, right):
                if i not in waited:
                    loads[i].wait()
                    waited.add(i)
            base = ((1 - seq) if k == 0 else seq) * out.shape[0]

            def step(i, carry):
                from_at = pl.ds(pl.multiple_of(base + i * GRAD_TILE, GRAD_TILE), GRAD_TILE)
                to_at = pl.ds(pl.multiple_of(i * GRAD_TILE, GRAD_TILE), GRAD_TILE)
                out[to_at, :] = contract_rows(here[left][:, from_at], here[right][...]).astype(
                    out.dtype
                )
                return carry

            lax.fori_loop(first, last, step, 0)
            if last * GRAD_TILE == out.shape[0]:
                if p == 0 and k == 0:
                    copy = remote(
                        out, results[0], side_sem.at[0], side_sem.at[1], (1 - seq, me)
                    )
                    self.remote = copy
                else:
                    copy = pltpu.make_async_copy(
                        out, results[2 * p + k], out_sem.at[2 * p + k]
                    )
                    self.open.append(copy)
                copy.start()

        found = []
        for p in range(len(self.pairs)):
            for k in range(2):
                count = tiles[2 * p + k].shape[0] // GRAD_TILE
                step = max(count // 2, 1)
                for first in range(0, count, step):
                    found.append(functools.partial(multiply, p, k, first, first + step))
        return found

    def finish(self):
        for copy in self.open:
            copy.wait()
        self.remote.wait()


class AttentionGrads(NoWork):
    def __init__(self, attn_in, d_qkv, mix_all, branch, weights, tokens, d_resid, gains, gain):
        self.operands = [attn_in, d_qkv, mix_all, branch, weights, tokens, d_resid, gains, gain]
        self.inputs, self.outputs = len(self.operands), 1
        low = attn_in.dtype
        blocks, rows = weights.shape[:2]
        self.local = d_qkv.shape[1] // 3
        self.part_shapes = [
            jax.ShapeDtypeStruct((blocks, rows, cols), low)
            for cols in 3 * (self.local,) + 2 * (branch.shape[1] // 2,)
        ]
        self.part_shapes.append(jax.ShapeDtypeStruct(gains.shape, low))
        self.order = (3, 0, 1, 2, 5, 4)
        self.ahead = 4
        self.results = [jax.ShapeDtypeStruct(tokens.shape, low)]
        self.scratch = [pltpu.VMEM(a.shape, a.dtype) for a in self.operands]
        self.scratch += [
            pltpu.VMEM(tokens.shape, low),
            pltpu.VMEM((2,) + tokens.shape, low),
            pltpu.VMEM(tokens.shape, low),
            pltpu.VMEM((ROW_TILE, tokens.shape[1]), jnp.float32),
            pltpu.SemaphoreType.DMA((self.inputs,)),
            pltpu.SemaphoreType.DMA((3,)),
        ]

    def need(self, *numbers):
        for i in numbers:
            if i not in self.waited:
                self.loads[i].wait()
                self.waited.add(i)

    def fill(self, parts, a, base):
        part = parts[a]
        if a == 5:
            part[pl.ds(base, 4)] = self.here[7][pl.ds(base, 4)].astype(part.dtype)
            return
        left, right = (2, 3) if a >= 3 else (0, 1)
        self.need(left, right)
        rows, cols = part.shape[1:]
        first = (a - 3 if a >= 3 else a) * cols

        def step(i, carry):
            at = pl.ds(pl.multiple_of((base + i) * rows, rows), rows)
            part[base + i] = contract_rows(
                self.here[left][:, at], self.here[right][:, first : first + cols]
            ).astype(part.dtype)
            return carry

        lax.fori_loop(0, 4, step, 0)

    def tasks(self, seq, me, arrays, results, scratch, start_sides):
        self.here, scratch = scratch[: self.inputs], scratch[self.inputs :]
        here = self.here
        grad, part, came, total, in_sem, sem = scratch
        self.loads = [
            pltpu.make_async_copy(arrays[i], here[i], in_sem.at[i]) for i in range(self.inputs)
        ]
        self.waited = set()
        for load in self.loads:
            load.start()
        blocks, rows = here[4].shape[:2]
        inner = here[1].shape[1]
        tok_rows, width = came.shape
        self.exchange = remote(part.at[1 - seq], came, sem.at[0], sem.at[1], (1 - seq, me))
        self.out = pltpu.make_async_copy(grad, results[0], sem.at[2])

        def multiply(first, last):
            self.need(1, 4)

            def step(i, carry):
                at = pl.ds(pl.multiple_of(2 * i * rows, 2 * rows), 2 * rows)
                weight = here[4][pl.ds(2 * i, 2), :, :inner].reshape(2 * rows, inner)
                result = contract_cols(here[1][...], weight)
                part[:, :, at] = result.reshape(2, tok_rows, 2 * rows).astype(part.dtype)
                return carry

            lax.fori_loop(first, last, step, 0)

        def send():
            self.exchange.start()
            start_sides()

        def norm_back():
            self.need(5, 6, 7, 8)
            self.exchange.wait_recv()
            total[...] = jnp.zeros_like(total)

            def step(i, carry):
                at = pl.ds(pl.multiple_of(i * ROW_TILE, ROW_TILE), ROW_TILE)
                values = here[5][at, :].astype(jnp.float32)
                scale = lax.rsqrt(jnp.mean(values * values, axis=-1, keepdims=True) + norm_eps)
                normed = values * scale
                d_out = part[seq, at, :].astype(jnp.float32) + came[at, :].astype(jnp.float32)
                total[...] += d_out * normed
                scaled = d_out * here[8][0:1, :]
                mean = jnp.mean(scaled * normed, axis=-1, keepdims=True)
                d_in = here[6][at, :] + scale * (scaled - normed * mean)
                grad[at, :] = d_in.astype(grad.dtype)
                return carry

            lax.fori_loop(0, tok_rows // ROW_TILE, step, 0)
            summed = jnp.sum(total[...], axis=0, keepdims=True)
            for n in range(blocks):
                here[7][n, 0:1, :] = summed[:, n * rows : (n + 1) * rows]
            self.out.start()

        pairs = blocks // 2
        found = [functools.partial(multiply, i, i + 2) for i in range(0, pairs, 2)]
        return found + [send, norm_back]

    def at_step(self, tasks, i, steps):
        rounds = (steps - self.ahead) // len(self.order)
        last = rounds * self.order.index(5) - self.ahead - 1
        if i < len(tasks) - 2:
            return [tasks[i]] + ([tasks[-2]] if i == len(tasks) - 3 else [])
        return [tasks[-1]] if i == last else []

    def finish(self):
        self.exchange.wait_send()
        self.out.wait()


def scatter_sum(parts, collective_id, out_dtype, seq_count=1, sides=(), work=None):
    work = work or NoWork()
    count = lax.axis_size("shard")
    shapes = list(work.part_shapes) or parts
    arrays = len(shapes)
    lead = (seq_count,) if seq_count > 1 else ()
    others = max(seq_count - 1, 1)
    return pl.pallas_call(
        functools.partial(scatter_kernel, count, seq_count, arrays, len(sides), work),
        out_shape=[jax.ShapeDtypeStruct(lead + p.shape[1:], out_dtype) for p in shapes]
        + [jax.ShapeDtypeStruct(s.shape, s.dtype) for s in sides]
        + list(work.results),
        in_specs=[pl.BlockSpec(memory_space=pltpu.VMEM)] * len(parts)
        + [pl.BlockSpec(memory_space=pl.ANY)] * (len(sides) + work.inputs),
        out_specs=[pl.BlockSpec(memory_space=pltpu.VMEM)] * arrays
        + [pl.BlockSpec(memory_space=pl.ANY)] * (len(sides) + work.outputs),
        scratch_shapes=[pltpu.VMEM(p.shape, p.dtype) for p in list(work.part_shapes) + list(shapes)]
        + [
            pltpu.SemaphoreType.DMA((arrays, count)),
            pltpu.SemaphoreType.DMA((arrays, count)),
            pltpu.SemaphoreType.DMA((arrays, others)),
            pltpu.SemaphoreType.DMA((arrays, others)),
            pltpu.SemaphoreType.DMA((max(len(sides), 1),)),
            pltpu.SemaphoreType.DMA((max(len(sides), 1),)),
        ]
        + list(work.scratch),
        compiler_params=pltpu.CompilerParams(
            collective_id=collective_id, has_side_effects=True, vmem_limit_bytes=VMEM_LIMIT
        ),
        name="scatter_sum_%d" % collective_id,
    )(*parts, *sides, *work.operands)


def place_kernel(refs_in, seq_count, *refs):
    for i, o in enumerate(refs_in):
        out_ref, base = refs[len(refs_in) + o[0]], o[1]
        cols = refs[i].shape[2]
        for s in range(seq_count):
            at = base + s * o[2]
            out_ref[:, at : at + cols] = refs[i][s].astype(out_ref.dtype)


def place_rows(pieces, targets, out_cols):
    seq_count, rows, _ = pieces[0].shape
    return pl.pallas_call(
        functools.partial(place_kernel, targets, seq_count),
        out_shape=[jax.ShapeDtypeStruct((rows, cols), jnp.float32) for cols in out_cols],
        in_specs=[pl.BlockSpec(memory_space=pltpu.VMEM)] * len(pieces),
        out_specs=[pl.BlockSpec(memory_space=pltpu.VMEM)] * len(out_cols),
        name="place_rows",
    )(*pieces)


def expert_kernel(count, *refs):
    (ffn_own, grad_own, weight), refs = refs[:3], refs[3:]
    matrices, refs = refs[:3], refs[3:]
    (rows_out, grad_out, hidden_out, mixed_out, gate_out, up_out), refs = refs[:6], refs[6:]
    pair_out, refs = refs[:2], refs[2:]
    (ffn_all, grad_all, both_w, down_w, gate_by, up_by), refs = refs[:6], refs[6:]
    (hidden_at, mixed_at, both_at, left_at, right_at), refs = refs[:5], refs[5:]
    ffn_send, ffn_recv, grad_send, grad_recv, load, own_sem, rows_sem, out_sem = refs
    me = lax.axis_index("shard")
    seq = lax.axis_index("seq")
    tiles = count // 2
    low, f32 = ffn_own.dtype, jnp.float32
    ffn = Line(count, ffn_own, ffn_all, ffn_send, ffn_recv, seq, 2)
    grad = Line(count, grad_own, grad_all, grad_send, grad_recv, seq, 2)
    ffn.meet()
    ffn.start(0)
    inner = down_w.shape[0]
    gate_span, up_span = slice(0, inner), slice(inner, 2 * inner)
    places = (both_w.at[:, gate_span], both_w.at[:, up_span], down_w)
    loads = [
        pltpu.make_async_copy(source, target, load.at[i])
        for i, (source, target) in enumerate(zip(matrices, places))
    ]
    for copy in loads:
        copy.start()
    ffn_keep = pltpu.make_async_copy(ffn_own, ffn_all.at[me], own_sem.at[0])
    grad_keep = pltpu.make_async_copy(grad_own, grad_all.at[me], own_sem.at[1])
    ffn_keep.start()
    grad_keep.start()
    ffn_keep.wait()
    for copy in loads:
        copy.wait()

    tile_of = ffn.pair

    def put(number, slot, staged, target, tile):
        return pltpu.make_async_copy(staged.at[slot], target.at[tile], out_sem.at[number, slot])

    def keep_rows(number, rows, target, tile):
        at = pl.ds(2 * tile, 2)
        return pltpu.make_async_copy(rows.at[at], target.at[at], rows_sem.at[number, tile])

    def arrivals(way, i, extra):
        done = 0
        for at in range(tiles):
            upto = way.order.index(2 * at) + 1 if at else 0
            order = way.order[done:upto]
            done = max(done, upto)

            @pl.when(i == at)
            def _(at=at, order=order):
                for r in order:
                    way.arrive(r)
                if at in extra:
                    extra[at]()
                way.wait_twin(2 * at)

    columns = inner // 2

    def beyond(at):
        return slice(inner + at.start, inner + at.stop)

    def forward(i, carry):
        arrivals(ffn, i, {tiles - 3: lambda: grad.start(0)})
        tile = tile_of(i)
        slot = lax.rem(i, 2)
        keep_rows(0, ffn_all, rows_out, tile).start()

        @pl.when(i >= 2)
        def _():
            put(0, slot, hidden_at, hidden_out, tile_of(i - 2)).wait()
            put(1, slot, mixed_at, mixed_out, tile_of(i - 2)).wait()

        rows = ffn_all[pl.ds(2 * tile, 2)].reshape(-1, ffn_all.shape[2])
        for c in range(2):
            at = slice(c * columns, (c + 1) * columns)
            gate = jnp.dot(rows, both_w[:, at], preferred_element_type=f32)
            up = jnp.dot(rows, both_w[:, beyond(at)], preferred_element_type=f32)
            sigma = jax.nn.sigmoid(gate)
            weighted = weight[tile] * sigma
            silu = weighted * gate
            hidden_at[slot, :, at] = (silu * up).astype(low)
            gate_by[i, :, at] = up * (weighted + silu * (1.0 - sigma))
            up_by[i, :, at] = silu
        put(0, slot, hidden_at, hidden_out, tile).start()
        half = down_w.shape[1] // 2
        for c in range(2):
            at = slice(c * half, (c + 1) * half)
            result = jnp.dot(hidden_at[slot], down_w[:, at], preferred_element_type=f32)
            mixed_at[slot, :, at] = result.astype(low)
        put(1, slot, mixed_at, mixed_out, tile).start()
        return carry

    lax.fori_loop(0, tiles, forward, 0)
    grad_keep.wait()

    def backward(i, carry):
        arrivals(grad, i, {})
        tile = tile_of(i)
        slot = lax.rem(i, 2)

        keep_rows(1, grad_all, grad_out, tile).start()

        @pl.when(i >= 2)
        def _():
            before = tile_of(i - 2)
            put(2, slot, both_at.at[:, :, gate_span], gate_out, before).wait()
            put(3, slot, both_at.at[:, :, up_span], up_out, before).wait()
            put(4, slot, left_at, pair_out[0], before).wait()
            put(5, slot, right_at, pair_out[1], before).wait()

        rows = grad_all[pl.ds(2 * tile, 2)].reshape(-1, grad_all.shape[2])
        for c in range(2):
            at = slice(c * columns, (c + 1) * columns)
            d_hidden = contract_cols(rows, down_w[at, :])
            both_at[slot, :, at] = (d_hidden * gate_by[i, :, at]).astype(low)
            both_at[slot, :, beyond(at)] = (d_hidden * up_by[i, :, at]).astype(low)
        put(2, slot, both_at.at[:, :, gate_span], gate_out, tile).start()
        put(3, slot, both_at.at[:, :, up_span], up_out, tile).start()
        half = both_w.shape[0] // 2
        for c, staged in enumerate((left_at, right_at)):
            at = slice(c * half, (c + 1) * half)
            staged[slot] = contract_cols(both_at[slot], both_w[at, :]).astype(low)
            put(4 + c, slot, staged, pair_out[c], tile).start()
        return carry

    lax.fori_loop(0, tiles, backward, 0)
    ffn.finish()
    grad.finish()
    for i in range(tiles):
        keep_rows(0, ffn_all, rows_out, i).wait()
        keep_rows(1, grad_all, grad_out, i).wait()
    outs = (hidden_out, mixed_out, gate_out, up_out, pair_out[0], pair_out[1])
    parts = (both_at.at[:, :, gate_span], both_at.at[:, :, up_span])
    staged = (hidden_at, mixed_at) + parts + (left_at, right_at)
    for i in (tiles - 2, tiles - 1):
        for number in range(len(outs)):
            put(number, i % 2, staged[number], outs[number], tile_of(i)).wait()


def run_experts(ffn_in, own_grad, weight, gate_w, up_w, down_w, collective_id):
    count = lax.axis_size("shard")
    rows, width = ffn_in.shape
    inner = gate_w.shape[1]
    tiles, two = count // 2, 2 * rows
    low = ffn_in.dtype
    shape = jax.ShapeDtypeStruct
    wide, narrow = (tiles, two, width), (tiles, two, inner)
    outs = [shape((count, rows, width), low)] * 2
    outs += [shape(s, low) for s in (narrow, wide, narrow, narrow)]
    outs += [shape((tiles, two, width // 2), low)] * 2
    vmem, hbm = pl.BlockSpec(memory_space=pltpu.VMEM), pl.BlockSpec(memory_space=pl.ANY)
    staged = [inner, width, 2 * inner, width // 2, width // 2]
    return pl.pallas_call(
        functools.partial(expert_kernel, count),
        out_shape=outs,
        in_specs=[vmem] * 3 + [hbm] * 3,
        out_specs=[hbm] * len(outs),
        scratch_shapes=[
            pltpu.VMEM((count, rows, width), low),
            pltpu.VMEM((count, rows, width), low),
            pltpu.VMEM((width, 2 * inner), low),
            pltpu.VMEM(down_w.shape, low),
            pltpu.VMEM((tiles, two, inner), jnp.float32),
            pltpu.VMEM((tiles, two, inner), jnp.float32),
        ]
        + [pltpu.VMEM((2, two, cols), low) for cols in staged]
        + [pltpu.SemaphoreType.DMA((2, count + 1))] * 4
        + [
            pltpu.SemaphoreType.DMA((3,)),
            pltpu.SemaphoreType.DMA((2,)),
            pltpu.SemaphoreType.DMA((2, tiles)),
            pltpu.SemaphoreType.DMA((len(staged) + 1, 2)),
        ],
        compiler_params=pltpu.CompilerParams(
            collective_id=collective_id, has_side_effects=True, vmem_limit_bytes=VMEM_LIMIT
        ),
        name="run_experts",
    )(ffn_in, own_grad, weight, gate_w, up_w, down_w)


GAIN_LANES = 128


def pair_tables(expert_list, prob_list, expert_count):
    numbers = jnp.arange(expert_count, dtype=jnp.int32)
    named = expert_list[None, :, :] == numbers[:, None, None]
    return jnp.sum(jnp.where(named, prob_list[None], 0.0), axis=2)


def shards(
    layer_input,
    seq_lengths,
    seq_order,
    expert_ids,
    expert_probs,
    weight_qkv,
    weight_out,
    norm_gains,
    weight_gate,
    weight_up,
    weight_down,
    out_cotangent,
):
    width = layer_input.shape[-1]
    tok_rows = layer_input.shape[1]
    seq_count = lax.axis_size("seq")
    seq_at = lax.axis_index("seq")
    group_tok = tok_rows * seq_count
    experts = lax.axis_size("shard")
    shard_at = lax.axis_index("shard")
    weight_rows = weight_qkv.shape[0]
    heads_local = HEADS // seq_count
    local_width = heads_local * HEAD_DIM
    out_cols = width // seq_count
    score_scale = HEAD_DIM ** (-0.5)
    low = jnp.bfloat16
    f32 = jnp.float32

    def take_seq(array, axis):
        return lax.dynamic_index_in_dim(array, seq_at, axis, keepdims=False)

    def seq_sum(part):
        if seq_count != 2:
            return lax.psum_scatter(part, "seq", scatter_dimension=0, tiled=True).astype(f32)
        halves = part.reshape(2, part.shape[0] // 2, part.shape[1])
        there = lax.dynamic_index_in_dim(halves, 1 - seq_at, 0, keepdims=False)
        here = lax.dynamic_index_in_dim(halves, seq_at, 0, keepdims=False)
        came = lax.ppermute(there, "seq", [(0, 1), (1, 0)])
        return here.astype(f32) + came.astype(f32)

    own_cols = take_seq(weight_qkv.reshape(weight_rows, 3, seq_count, local_width), 2)
    own_gains = jnp.pad(norm_gains, ((0, 0), (0, GAIN_LANES - norm_gains.shape[1])))
    table = pair_tables(expert_ids[0], expert_probs[0], experts)
    own_block = jnp.concatenate(
        [own_cols.reshape(weight_rows, 3 * local_width), own_gains], axis=1
    )
    qkv_cols, tables_all = gather_blocks([own_block, table], 1, ((0, 1),), (2, 1))
    own_out, qkv_cols = lax.optimization_barrier((weight_out, qkv_cols))
    full_out = lax.all_gather(own_out, "shard", axis=0, tiled=True)
    qkv_all = qkv_cols
    qkv_cols = qkv_cols.reshape(width, 3 * local_width + GAIN_LANES)
    gain_cols = qkv_cols[:, 3 * local_width :][:, : norm_gains.shape[1]].astype(f32)
    qkv_cols = qkv_cols[:, : 3 * local_width]
    group_in = lax.all_gather(layer_input[0], "seq", axis=0, tiled=True).astype(f32)
    pair_weight = lax.dynamic_index_in_dim(tables_all, shard_at, 1, keepdims=False)

    segment, position = group_layout(seq_lengths[0], seq_order[0], group_tok)
    places = jnp.arange(group_tok, dtype=jnp.int32)
    allowed = (segment[:, None] == segment[None, :]) & (places[None, :] <= places[:, None])
    cosine, sine_part = rope_tables(position, HEAD_DIM)

    def rope(values):
        return rotate(
            values.reshape(group_tok, heads_local, HEAD_DIM), cosine, sine_part
        ).reshape(group_tok, local_width)

    def rope_back(grads):
        return rotate(
            grads.reshape(group_tok, heads_local, HEAD_DIM), cosine, -sine_part
        ).reshape(group_tok, local_width)

    gain_q = lax.dynamic_slice_in_dim(gain_cols[:, 1], seq_at * local_width, local_width)
    gain_k = lax.dynamic_slice_in_dim(gain_cols[:, 2], seq_at * local_width, local_width)

    group_r = lax.rsqrt(jnp.mean(group_in * group_in, axis=-1, keepdims=True) + norm_eps)
    group_n = group_in * group_r
    attn_in = (group_n * gain_cols[:, 0]).astype(low)
    projected = jnp.dot(attn_in, qkv_cols, preferred_element_type=f32)
    q_raw = projected[:, :local_width]
    k_raw = projected[:, local_width : 2 * local_width]
    value = projected[:, 2 * local_width :].astype(low)
    squares = jnp.stack([jnp.sum(q_raw * q_raw, axis=-1), jnp.sum(k_raw * k_raw, axis=-1)])
    squares = lax.psum(squares, "seq")
    q_r, k_r = (lax.rsqrt(row / width + norm_eps)[:, None] for row in squares)
    q_n = q_raw * q_r
    k_n = k_raw * k_r
    query = rope(q_n * gain_q).astype(low)
    key = rope(k_n * gain_k).astype(low)
    query_head = query.reshape(group_tok, heads_local, HEAD_DIM)
    key_head = key.reshape(group_tok, heads_local, HEAD_DIM)
    value_head = value.reshape(group_tok, heads_local, HEAD_DIM)
    scores = jnp.einsum("ihd,jhd->hij", query_head, key_head, preferred_element_type=f32)
    scores = jnp.where(allowed[None], scores * score_scale, -1e30)
    score_peak = jnp.max(scores, axis=-1, keepdims=True)
    weights_exp = jnp.exp(scores - score_peak)
    attn_probs = weights_exp / jnp.sum(weights_exp, axis=-1, keepdims=True)
    probs_low = attn_probs.astype(low)
    mix_head = jnp.einsum("hij,jhd->ihd", probs_low, value_head, preferred_element_type=f32)
    mix_head = mix_head.astype(low).reshape(group_tok, local_width)
    attn_mix = lax.all_to_all(mix_head, "seq", split_axis=0, concat_axis=1, tiled=True)
    mix_all = lax.all_gather(mix_head, "seq", axis=1, tiled=True)
    resid = layer_input[0].astype(f32) + jnp.dot(attn_mix, full_out, preferred_element_type=f32)
    ffn_r = lax.rsqrt(jnp.mean(resid * resid, axis=-1, keepdims=True) + norm_eps)
    ffn_n = resid * ffn_r
    ffn_in = (ffn_n * gain_cols[:, 3]).astype(low)

    pairs = seq_count == 2
    gate_weight = weight_gate[0]
    up_weight = weight_up[0]
    down_weight = weight_down[0]
    if experts == LINE:
        tile_weight = pair_weight.reshape(experts // 2, 2 * tok_rows, 1)
        results = run_experts(
            ffn_in, out_cotangent[0], tile_weight, gate_weight, up_weight, down_weight, 2
        )
        rows_in, d_expert, hidden, out_part, d_gate, d_up, *halves = (
            result.reshape(experts * tok_rows, -1) for result in results
        )
    else:
        slot_weight = pair_weight.reshape(-1, 1)
        (ffn_all, grad_all) = gather_blocks(
            [ffn_in, out_cotangent[0]], 2, ((0,), (1,)), (1, 1)
        )
        rows_in = ffn_all.reshape(-1, width)
        gate = jnp.dot(rows_in, gate_weight, preferred_element_type=f32)
        up = jnp.dot(rows_in, up_weight, preferred_element_type=f32)
        sigma = jax.nn.sigmoid(gate)
        silu = gate * sigma
        hidden = (silu * up).astype(low)
        expert_out = jnp.dot(hidden, down_weight, preferred_element_type=f32).astype(low)
        out_part = (expert_out.astype(f32) * slot_weight).astype(low)
        d_expert = (grad_all.reshape(-1, width).astype(f32) * slot_weight).astype(low)
        d_hidden = contract_cols(d_expert, down_weight)
        d_gate = (d_hidden * up * sigma * (1.0 + gate * (1.0 - sigma))).astype(low)
        d_up = (d_hidden * silu).astype(low)
        d_pair = contract_cols(d_gate, gate_weight) + contract_cols(d_up, up_weight)
        halves = jnp.split(d_pair.astype(low), 2, axis=1)
    halves = [part.reshape(experts, tok_rows, -1) for part in halves]
    products = [(hidden, d_expert), (rows_in, d_gate), (rows_in, d_up)]
    if pairs:
        results = scatter_sum(halves, 3, f32, work=ExpertGrads(products))
        d_left, d_right, down_came, down_mine, gate_there, gate_mine, up_there, up_mine = results
    else:
        d_left, d_right = scatter_sum(halves, 3, f32)
    d_ffn_in = jnp.concatenate([d_left, d_right], axis=1)
    out_part, d_ffn_in = lax.optimization_barrier((out_part, d_ffn_in))
    mixed_out = lax.psum_scatter(
        out_part, "shard", scatter_dimension=0, tiled=True
    )

    grad_tokens = out_cotangent[0].astype(f32)
    d_scaled = d_ffn_in * gain_cols[:, 3]
    d_resid = grad_tokens + ffn_r * (
        d_scaled - ffn_n * jnp.mean(d_scaled * ffn_n, axis=-1, keepdims=True)
    )
    grad_g_ffn = jnp.sum(d_ffn_in * ffn_n, axis=0)
    d_branch = d_resid.astype(low)
    d_mix = contract_cols(d_branch, full_out).astype(low)
    d_mix_head = lax.all_to_all(d_mix, "seq", split_axis=1, concat_axis=0, tiled=True).reshape(
        group_tok, heads_local, HEAD_DIM
    )
    branch_cols = lax.all_to_all(d_branch, "seq", split_axis=1, concat_axis=0, tiled=True)
    d_probs = jnp.einsum("ihd,jhd->hij", d_mix_head, value_head, preferred_element_type=f32)
    delta_rows = jnp.sum(attn_probs * d_probs, axis=-1, keepdims=True)
    d_scores = (attn_probs * (d_probs - delta_rows)).astype(low)
    d_query = (
        jnp.einsum("hij,jhd->ihd", d_scores, key_head, preferred_element_type=f32) * score_scale
    ).astype(low)
    d_key = (
        jnp.einsum("hij,ihd->jhd", d_scores, query_head, preferred_element_type=f32) * score_scale
    ).astype(low)
    d_value = jnp.einsum(
        "hij,ihd->jhd", probs_low, d_mix_head, preferred_element_type=f32
    ).astype(low)
    dq_rot = rope_back(d_query.reshape(group_tok, local_width).astype(f32))
    dk_rot = rope_back(d_key.reshape(group_tok, local_width).astype(f32))
    grad_g_q = jnp.sum(dq_rot * q_n, axis=0)
    grad_g_k = jnp.sum(dk_rot * k_n, axis=0)
    dq_scaled = dq_rot * gain_q
    dk_scaled = dk_rot * gain_k
    dots = jnp.stack([jnp.sum(dq_scaled * q_n, axis=-1), jnp.sum(dk_scaled * k_n, axis=-1)])
    dots = lax.psum(dots, "seq") / width
    if pairs:
        dots, gate_there = lax.optimization_barrier((dots, gate_there))
        gate_came = lax.ppermute(gate_there, "seq", [(0, 1), (1, 0)])
    dq_raw = q_r * (dq_scaled - q_n * dots[0][:, None])
    dk_raw = k_r * (dk_scaled - k_n * dots[1][:, None])
    d_qkv = jnp.concatenate(
        [dq_raw.astype(low), dk_raw.astype(low), d_value.reshape(group_tok, local_width)], axis=1
    )
    zeros = jnp.zeros((width,), f32)
    gain_rows = [
        zeros,
        lax.dynamic_update_slice_in_dim(zeros, grad_g_q, seq_at * local_width, 0),
        lax.dynamic_update_slice_in_dim(zeros, grad_g_k, seq_at * local_width, 0),
        grad_g_ffn,
    ]
    if pairs:
        gain_terms = jnp.stack(gain_rows).reshape(len(gain_rows), experts, weight_rows)
        gain_terms = jnp.pad(
            jnp.swapaxes(gain_terms, 0, 1), ((0, 0), (0, ROW_TILE - len(gain_rows)), (0, 0))
        )
        work = AttentionGrads(
            attn_in,
            d_qkv,
            mix_all,
            branch_cols,
            qkv_all,
            layer_input[0],
            d_resid,
            gain_terms,
            jnp.broadcast_to(gain_cols[:, 0], (8, width)),
        )
        *sums, sum_gains, up_came, input_grad = scatter_sum(
            [], 4, low, seq_count, sides=[up_there], work=work
        )
        sum_gate, sum_up, sum_down = (
            mine.astype(f32) + came.astype(f32)
            for mine, came in ((gate_mine, gate_came), (up_mine, up_came), (down_mine, down_came))
        )
        rows_gain = jnp.sum(sum_gains[:, : norm_gains.shape[1]].astype(f32), axis=0).T
    else:
        d_attn_in = seq_sum(contract_cols(d_qkv, qkv_cols).astype(low))
        own_n = lax.dynamic_slice_in_dim(group_n, seq_at * tok_rows, tok_rows)
        own_r = lax.dynamic_slice_in_dim(group_r, seq_at * tok_rows, tok_rows)
        dx_scaled = d_attn_in * gain_cols[:, 0]
        dx_norm = own_r * (
            dx_scaled - own_n * jnp.mean(dx_scaled * own_n, axis=-1, keepdims=True)
        )
        gain_rows[0] = jnp.sum(d_attn_in * own_n, axis=0)
        input_grad = (d_resid + dx_norm).astype(low)
        gain_terms = jnp.stack(gain_rows, axis=1)
        gain_terms = jnp.pad(gain_terms, ((0, 0), (0, GAIN_LANES - gain_terms.shape[1])))
        terms = [
            contract_rows(attn_in, d_qkv[:, i * local_width : (i + 1) * local_width])
            for i in range(3)
        ]
        terms += [contract_rows(mix_all, branch_cols), gain_terms]
        terms = [term.astype(low).reshape(experts, weight_rows, -1) for term in terms]
        *sums, sum_gains = scatter_sum(terms, 4, low, seq_count)
        sum_down, sum_gate, sum_up = (
            lax.psum_scatter(
                contract_rows(left, right).astype(low), "seq", scatter_dimension=0, tiled=True
            ).astype(f32)
            for left, right in products
        )
        rows_gain = jnp.sum(sum_gains[:, :, : norm_gains.shape[1]].astype(f32), axis=0)
    mixed_out, sums[0] = lax.optimization_barrier((mixed_out, sums[0]))
    layer_output = (resid + mixed_out.astype(f32)).astype(low)
    targets = [(0, i * width, local_width) for i in range(3)]
    targets += [(1, i * sums[3].shape[2], out_cols) for i in range(len(sums) - 3)]
    rows_qkv, rows_out = place_rows(sums, targets, (3 * width, width))
    return (
        layer_output[None],
        input_grad[None],
        rows_qkv,
        rows_out,
        rows_gain,
        sum_gate[None],
        sum_up[None],
        sum_down[None],
    )


def solution(mesh):
    in_specs = (
        P("shard", "seq", None),
        P("shard", None),
        P("shard", None),
        P("shard", "seq", None),
        P("shard", "seq", None),
        P("shard", None),
        P("shard", None),
        P("shard", None),
        P("shard", None, None),
        P("shard", None, None),
        P("shard", None, None),
        P("shard", "seq", None),
    )
    out_specs = (
        P("shard", "seq", None),
        P("shard", "seq", None),
        P("shard", None),
        P("shard", None),
        P("shard", None),
        P("shard", "seq", None),
        P("shard", "seq", None),
        P("shard", "seq", None),
    )
    return jax.shard_map(shards, mesh=mesh, in_specs=in_specs, out_specs=out_specs, check_vma=False)
```

```python
import functools

import jax
import jax.numpy as jnp
from jax import lax
from jax.experimental import pallas as pl
from jax.experimental.pallas import tpu as pltpu
from jax.sharding import PartitionSpec as P

HEADS = 16
HEAD_DIM = 128


norm_eps = 1e-05
rope_base = 10000.0


def rms_scale(values, gain_col):
    return (
        values * lax.rsqrt(jnp.mean(values * values, axis=-1, keepdims=True) + norm_eps) * gain_col
    )


def rotate(values, cosine, sine_part):
    half_dim = values.shape[-1] // 2
    first_half = values[..., :half_dim]
    second_half = values[..., half_dim:]
    return jnp.concatenate(
        [
            first_half * cosine - second_half * sine_part,
            second_half * cosine + first_half * sine_part,
        ],
        axis=-1,
    )


def rope_tables(position, head_size):
    half_dim = head_size // 2
    frequency = rope_base ** (-2.0 * jnp.arange(half_dim, dtype=jnp.float32) / head_size)
    angles = position.astype(jnp.float32)[:, None] * frequency[None, :]
    return (jnp.cos(angles)[:, None, :], jnp.sin(angles)[:, None, :])


def group_layout(lengths, seq_perm, group_tok):
    seq_count = lengths.shape[0]
    numbers = jnp.arange(seq_count, dtype=jnp.int32)
    packed = jnp.sum(jnp.where(seq_perm[:, None] == numbers[None, :], lengths[None, :], 0), axis=1)
    seq_ends = jnp.cumsum(packed)
    seq_starts = seq_ends - packed
    places = jnp.arange(group_tok, dtype=jnp.int32)
    segment = jnp.sum((places[:, None] >= seq_ends[None, :]).astype(jnp.int32), axis=1)
    begins = jnp.sum(
        jnp.where(segment[:, None] == numbers[None, :], seq_starts[None, :], 0), axis=1
    )
    return (segment, places - begins)


def contract_rows(left_side, right_side):
    return lax.dot_general(
        left_side, right_side, (((0,), (0,)), ((), ())), preferred_element_type=jnp.float32
    )


def contract_cols(left_side, right_side):
    return lax.dot_general(
        left_side, right_side, (((1,), (1,)), ((), ())), preferred_element_type=jnp.float32
    )


MESH_ID = pl.DeviceIdType.MESH
VMEM_LIMIT = 60 * 1024 * 1024
ROW_TILE = 16
GRAD_TILE = 256


def low_bit(index):
    return index & -index


def bit_list(count):
    return [1 << b for b in range(count.bit_length() - 1)]


def relative_place(count, me):
    values = [(bit, lax.rem(me // bit, 2)) for bit in bit_list(count)]

    def place(r):
        total = 0
        for bit, value in values:
            total = total + bit * ((1 - value) if r & bit else value)
        return total

    return place


def meet(count, place, seq, seq_count=1):
    barrier = pltpu.get_barrier_semaphore()
    for bit in bit_list(count):
        pl.semaphore_signal(barrier, 1, device_id=(seq, place(bit)), device_id_type=MESH_ID)
    for j in range(1, seq_count):
        pl.semaphore_signal(
            barrier, 1, device_id=(lax.rem(seq + j, seq_count), place(0)), device_id_type=MESH_ID
        )
    pl.semaphore_wait(barrier, len(bit_list(count)) + seq_count - 1)


def remote(src, dst, send_sem, recv_sem, device):
    return pltpu.make_async_remote_copy(
        src_ref=src,
        dst_ref=dst,
        send_sem=send_sem,
        recv_sem=recv_sem,
        device_id=device,
        device_id_type=MESH_ID,
    )


def arrival_order(count):
    def key(r):
        later = r >> 2
        return (later + ((r >> 1) & 1), (r >> 1) & 1)

    return sorted(range(2, count, 2), key=key)


LINE = 16


class Line:
    def __init__(self, count, own, full, send, recv, seq, pieces=1):
        me = lax.axis_index("shard")
        spot = me // 4
        self.upper = spot // 2
        self.inner = spot + self.upper * (3 - 2 * spot)
        self.y = lax.rem(me // 2, 2)
        self.core = lax.rem(me, 2)
        low = lax.rem(me, 4)
        near = (seq, self.block(1) * 4 + low)
        far = (seq, (3 - spot) * 4 + low)
        across = (seq, spot * 4 + (1 - self.y) * 2 + self.core)
        twin = (seq, spot * 4 + self.y * 2 + 1 - self.core)
        self.peers = (near, far, across, twin)
        self.copies = []
        self.inward = []
        rows = own.shape[0] // pieces
        for p in range(pieces):
            at = pl.ds(p * rows, rows)
            target = [full.at[self.place(r), at] for r in range(count)]
            source = [own.at[at]] + target[1:]

            def copy(r, sent, received, device, source=source, target=target, p=p):
                return remote(
                    source[r], target[r], send.at[p, sent], recv.at[p, received], device
                )

            copies = {4: copy(0, 4, 4, near)}
            for r in range(0, count, 4):
                copies[r | 2] = copy(r, r | 2, r | 2, across)
            for r in range(0, count, 2):
                copies[r | 1] = copy(r, r | 1, r | 1, twin)
            inward = {0: copy(0, 8, 8, far), 4: copy(4, 12, 12, far)}
            inward[8] = copy(8, 0, 8, near)
            inward[12] = copy(12, count, 12, near)
            copies[8] = inward[0]
            copies[12] = inward[4]
            self.copies.append(copies)
            self.inward.append(inward)

    def block(self, k):
        if isinstance(k, int):
            spot = k if k >= 2 else self.inner + k * (1 - 2 * self.inner)
        else:
            far = k // 2
            spot = far * k + (1 - far) * lax.rem(k + self.inner, 2)
        return spot + self.upper * (3 - 2 * spot)

    def place(self, r):
        y = (1 - self.y) if r & 2 else self.y
        core = (1 - self.core) if r & 1 else self.core
        return self.block(r >> 2) * 4 + y * 2 + core

    def pair(self, i):
        k, y = i // 2, lax.rem(i, 2)
        return self.block(k) * 2 + self.y + y - 2 * self.y * y

    def meet(self):
        barrier = pltpu.get_barrier_semaphore()
        for peer in self.peers:
            pl.semaphore_signal(barrier, 1, device_id=peer, device_id_type=MESH_ID)
        pl.semaphore_wait(barrier, len(self.peers))

    def start(self, r):
        for p in range(len(self.copies)):
            self.start_piece(p, r)

    def start_piece(self, p, r):
        copies, inward = self.copies[p], self.inward[p]
        if r == 0:
            copies[4].start()
        if r % 4 == 0:

            @pl.when(self.inner == 1)
            def _():
                inward[r].start()

            copies[r | 2].start()
        copies[r | 1].start()

    def arrive(self, r):
        for p in range(len(self.copies)):
            self.copies[p][r].wait_recv()
            self.start_piece(p, r)

    def wait_twin(self, r):
        for copies in self.copies:
            copies[r | 1].wait_recv()

    order = (4, 2, 8, 6, 12, 10, 14)

    def finish(self):
        for copies, inward in zip(self.copies, self.inward):
            for r in (4, 2, 6, 10, 14, 1, 3, 5, 7, 9, 11, 13, 15):
                copies[r].wait_send()

            @pl.when(self.inner == 1)
            def _(inward=inward):
                for copy in inward.values():
                    copy.wait_send()


class Tree:
    def __init__(self, count, own, full, send, recv, seq, pieces=1):
        self.count, self.seq = count, seq
        self.place = relative_place(count, lax.axis_index("shard"))
        self.order = arrival_order(count)
        self.copies = {}
        for r in range(count):
            below = low_bit(r) if r else count
            for bit in bit_list(count):
                if bit < below:
                    self.copies[r | bit] = remote(
                        own if r == 0 else full.at[self.place(r)],
                        full.at[self.place(r)],
                        send.at[0, r | bit],
                        recv.at[0, r | bit],
                        (seq, self.place(bit)),
                    )

    def meet(self):
        meet(self.count, self.place, self.seq)

    def start(self, r):
        below = low_bit(r) if r else self.count
        bits = [bit for bit in bit_list(self.count) if bit < below]
        for bit in sorted(bits, key=lambda bit: (bit < 4, bit)):
            self.copies[r | bit].start()

    def arrive(self, r):
        self.copies[r].wait_recv()
        self.start(r)

    def wait_twin(self, r):
        self.copies[r | 1].wait_recv()

    def finish(self):
        for copy in self.copies.values():
            copy.wait_send()


def gather_kernel(count, groups, pieces, *refs):
    arrays = sum(len(group) for group in groups)
    own, full = refs[:arrays], refs[arrays : 2 * arrays]
    send, recv, local = refs[2 * arrays :]
    me = lax.axis_index("shard")
    seq = lax.axis_index("seq")
    kind = Line if count == LINE else Tree
    ways = [
        kind(count, own[a], full[a], send.at[a], recv.at[a], seq, pieces[a])
        for a in range(arrays)
    ]
    ways[0].meet()
    keeps = []
    for a in range(arrays):
        keep = pltpu.make_async_copy(own[a], full[a].at[me], local.at[a])
        keep.start()
        keeps.append(keep)
    for group in groups:
        for a in group:
            ways[a].start(0)
        for r in ways[0].order:
            for a in group:
                ways[a].arrive(r)
    for a in range(arrays):
        for r in range(0, count, 2):
            ways[a].wait_twin(r)
    for way in ways:
        way.finish()
    for keep in keeps:
        keep.wait()


def gather_blocks(blocks, collective_id, groups=((0,),), pieces=(1,)):
    count = lax.axis_size("shard")
    arrays = len(blocks)
    return pl.pallas_call(
        functools.partial(gather_kernel, count, groups, pieces),
        out_shape=[jax.ShapeDtypeStruct((count,) + b.shape, b.dtype) for b in blocks],
        in_specs=[pl.BlockSpec(memory_space=pltpu.VMEM)] * arrays,
        out_specs=[pl.BlockSpec(memory_space=pl.ANY)] * arrays,
        scratch_shapes=[
            pltpu.SemaphoreType.DMA((arrays, max(pieces), count + 1)),
            pltpu.SemaphoreType.DMA((arrays, max(pieces), count + 1)),
            pltpu.SemaphoreType.DMA((arrays,)),
        ],
        compiler_params=pltpu.CompilerParams(collective_id=collective_id, has_side_effects=True),
        name="gather_blocks_%d" % collective_id,
    )(*blocks)


def scatter_kernel(count, seq_count, arrays, sides, work, *refs):
    given = 0 if work.part_shapes else arrays
    parts, refs = refs[:given], refs[given:]
    side_from, refs = refs[:sides], refs[sides:]
    work_in, refs = refs[: work.inputs], refs[work.inputs :]
    totals, refs = refs[:arrays], refs[arrays:]
    side_to, refs = refs[:sides], refs[sides:]
    work_out, refs = refs[: work.outputs], refs[work.outputs :]
    if work.part_shapes:
        parts, refs = refs[:arrays], refs[arrays:]
    held, refs = refs[:arrays], refs[arrays:]
    send, recv, seq_send, seq_recv, side_send, side_recv = refs[:6]
    planes = seq_count if seq_count > 1 else 1 + (sides > 0 or work.outputs > 0)
    me = lax.axis_index("shard")
    seq = lax.axis_index("seq")
    place = relative_place(count, me)
    bits = bit_list(count)
    meet(count, place, seq, planes)
    copies = {}
    shared = []

    def start_sides():
        for i in range(sides):
            copy = remote(
                side_from[i], side_to[i], side_send.at[i], side_recv.at[i], (1 - seq, me)
            )
            copy.start()
            shared.append(copy)

    def share(a):
        for j in range(1, seq_count):
            copy = remote(
                totals[a].at[seq],
                totals[a].at[seq],
                seq_send.at[a, j - 1],
                seq_recv.at[a, j - 1],
                (lax.rem(seq + j, seq_count), me),
            )
            copy.start()
            shared.append(copy)

    def start(a, r, source):
        copy = remote(
            source, held[a].at[r], send.at[a, r], recv.at[a, r], (seq, place(low_bit(r)))
        )
        copy.start()
        copies[a, r] = copy

    def fold(a, r, bit):
        came = r | bit
        copies[a, came].wait_recv()
        rows = held[a].shape[1]
        last = bit == bits[-1]

        def step(i, carry):
            at = pl.ds(pl.multiple_of(i * ROW_TILE, ROW_TILE), ROW_TILE)
            if bit == 1:
                mine = parts[a][place(r), at, :]
            else:
                mine = held[a][r | (bit >> 1), at, :]
            value = mine.astype(jnp.float32) + held[a][came, at, :].astype(jnp.float32)
            if last and seq_count > 1:
                totals[a][seq, at, :] = value.astype(totals[a].dtype)
            elif last:
                totals[a][at, :] = value.astype(totals[a].dtype)
            else:
                held[a][came, at, :] = value.astype(held[a].dtype)
            return carry

        lax.fori_loop(0, rows // ROW_TILE, step, 0)
        upper = bit << 1
        if last:
            share(a)
        elif r & upper:
            start(a, r, held[a].at[came])

    chunks = [
        (a, u) for a in work.order or range(arrays) for u in reversed(range(count // 4))
    ]

    def prepare(a, u):
        work.fill(parts, a, place(4 * u) - lax.rem(me, 4))
        for r in (4 * u + 3, 4 * u + 1):
            start(a, r, parts[a].at[place(r)])

    tasks = work.tasks(seq, me, work_in, work_out, refs[6:], start_sides)
    lead = work.ahead if work.part_shapes else len(chunks)
    for a, u in chunks[:lead]:
        prepare(a, u)
    steps = len(chunks) + work.ahead
    for i in range(steps):
        if i + lead < len(chunks):
            prepare(*chunks[i + lead])
        if i < len(chunks):
            a, u = chunks[i]
            fold(a, 4 * u + 2, 1)
            fold(a, 4 * u, 1)
        if i >= work.ahead:
            a, u = chunks[i - work.ahead]
            for bit in bits[1:]:
                if 4 * u % (2 * bit) == 0:
                    fold(a, 4 * u, bit)
        for task in work.at_step(tasks, i, steps):
            task()
    for copy in shared:
        copy.wait_recv()
    for copy in list(copies.values()) + shared:
        copy.wait_send()
    work.finish()


class NoWork:
    inputs = outputs = 0
    operands, results, scratch, part_shapes, order = (), (), (), (), ()
    ahead = 2

    def fill(self, parts, a, base):
        pass

    def tasks(self, seq, me, arrays, results, scratch, start_sides):
        start_sides()
        return []

    def at_step(self, tasks, i, steps):
        return tasks[len(tasks) * i // steps : len(tasks) * (i + 1) // steps]

    def finish(self):
        pass


class ExpertGrads(NoWork):
    def __init__(self, products):
        self.operands = []
        for pair in products:
            for array in pair:
                if not any(array is other for other in self.operands):
                    self.operands.append(array)
        self.pairs = [
            tuple(next(i for i, o in enumerate(self.operands) if o is array) for array in pair)
            for pair in products
        ]
        low = products[0][0].dtype
        shapes = [(left.shape[1] // 2, right.shape[1]) for left, right in products]
        halves = [jax.ShapeDtypeStruct(shape, low) for shape in shapes for _ in range(2)]
        self.results = halves
        self.inputs, self.outputs = len(self.operands), len(self.results)
        self.scratch = [pltpu.VMEM(a.shape, a.dtype) for a in self.operands]
        self.scratch += [pltpu.VMEM(h.shape, h.dtype) for h in halves]
        self.scratch += [
            pltpu.SemaphoreType.DMA((self.inputs,)),
            pltpu.SemaphoreType.DMA((self.outputs,)),
            pltpu.SemaphoreType.DMA((2,)),
        ]

    def tasks(self, seq, me, arrays, results, scratch, start_sides):
        start_sides()
        here, scratch = scratch[: self.inputs], scratch[self.inputs :]
        tiles, (in_sem, out_sem, side_sem) = scratch[: self.outputs], scratch[self.outputs :]
        loads = [
            pltpu.make_async_copy(arrays[i], here[i], in_sem.at[i]) for i in range(self.inputs)
        ]
        for load in loads:
            load.start()
        waited = set()
        self.open = []
        self.remote = None

        def multiply(p, k, first, last):
            left, right = self.pairs[p]
            out = tiles[2 * p + k]
            for i in (left, right):
                if i not in waited:
                    loads[i].wait()
                    waited.add(i)
            base = ((1 - seq) if k == 0 else seq) * out.shape[0]

            def step(i, carry):
                from_at = pl.ds(pl.multiple_of(base + i * GRAD_TILE, GRAD_TILE), GRAD_TILE)
                to_at = pl.ds(pl.multiple_of(i * GRAD_TILE, GRAD_TILE), GRAD_TILE)
                out[to_at, :] = contract_rows(here[left][:, from_at], here[right][...]).astype(
                    out.dtype
                )
                return carry

            lax.fori_loop(first, last, step, 0)
            if last * GRAD_TILE == out.shape[0]:
                if p == 0 and k == 0:
                    copy = remote(
                        out, results[0], side_sem.at[0], side_sem.at[1], (1 - seq, me)
                    )
                    self.remote = copy
                else:
                    copy = pltpu.make_async_copy(
                        out, results[2 * p + k], out_sem.at[2 * p + k]
                    )
                    self.open.append(copy)
                copy.start()

        found = []
        for p in range(len(self.pairs)):
            for k in range(2):
                count = tiles[2 * p + k].shape[0] // GRAD_TILE
                step = max(count // 2, 1)
                for first in range(0, count, step):
                    found.append(functools.partial(multiply, p, k, first, first + step))
        return found

    def finish(self):
        for copy in self.open:
            copy.wait()
        self.remote.wait()


class AttentionGrads(NoWork):
    def __init__(self, attn_in, d_qkv, mix_all, branch, weights, tokens, d_resid, gains, gain):
        self.operands = [attn_in, d_qkv, mix_all, branch, weights, tokens, d_resid, gains, gain]
        self.inputs, self.outputs = len(self.operands), 1
        low = attn_in.dtype
        blocks, rows = weights.shape[:2]
        self.local = d_qkv.shape[1] // 3
        self.part_shapes = [
            jax.ShapeDtypeStruct((blocks, rows, cols), low)
            for cols in 3 * (self.local,) + 2 * (branch.shape[1] // 2,)
        ]
        self.part_shapes.append(jax.ShapeDtypeStruct(gains.shape, low))
        self.order = (3, 0, 1, 2, 5, 4)
        self.ahead = 4
        self.results = [jax.ShapeDtypeStruct(tokens.shape, low)]
        self.scratch = [pltpu.VMEM(a.shape, a.dtype) for a in self.operands]
        self.scratch += [
            pltpu.VMEM(tokens.shape, low),
            pltpu.VMEM((2,) + tokens.shape, low),
            pltpu.VMEM(tokens.shape, low),
            pltpu.VMEM((ROW_TILE, tokens.shape[1]), jnp.float32),
            pltpu.SemaphoreType.DMA((self.inputs,)),
            pltpu.SemaphoreType.DMA((3,)),
        ]

    def need(self, *numbers):
        for i in numbers:
            if i not in self.waited:
                self.loads[i].wait()
                self.waited.add(i)

    def fill(self, parts, a, base):
        part = parts[a]
        if a == 5:
            part[pl.ds(base, 4)] = self.here[7][pl.ds(base, 4)].astype(part.dtype)
            return
        left, right = (2, 3) if a >= 3 else (0, 1)
        self.need(left, right)
        rows, cols = part.shape[1:]
        first = (a - 3 if a >= 3 else a) * cols

        def step(i, carry):
            at = pl.ds(pl.multiple_of((base + i) * rows, rows), rows)
            part[base + i] = contract_rows(
                self.here[left][:, at], self.here[right][:, first : first + cols]
            ).astype(part.dtype)
            return carry

        lax.fori_loop(0, 4, step, 0)

    def tasks(self, seq, me, arrays, results, scratch, start_sides):
        self.here, scratch = scratch[: self.inputs], scratch[self.inputs :]
        here = self.here
        grad, part, came, total, in_sem, sem = scratch
        self.loads = [
            pltpu.make_async_copy(arrays[i], here[i], in_sem.at[i]) for i in range(self.inputs)
        ]
        self.waited = set()
        for load in self.loads:
            load.start()
        blocks, rows = here[4].shape[:2]
        inner = here[1].shape[1]
        tok_rows, width = came.shape
        self.exchange = remote(part.at[1 - seq], came, sem.at[0], sem.at[1], (1 - seq, me))
        self.out = pltpu.make_async_copy(grad, results[0], sem.at[2])

        def multiply(first, last):
            self.need(1, 4)

            def step(i, carry):
                at = pl.ds(pl.multiple_of(2 * i * rows, 2 * rows), 2 * rows)
                weight = here[4][pl.ds(2 * i, 2), :, :inner].reshape(2 * rows, inner)
                result = contract_cols(here[1][...], weight)
                part[:, :, at] = result.reshape(2, tok_rows, 2 * rows).astype(part.dtype)
                return carry

            lax.fori_loop(first, last, step, 0)

        def send():
            self.exchange.start()
            start_sides()

        def norm_back():
            self.need(5, 6, 7, 8)
            self.exchange.wait_recv()
            total[...] = jnp.zeros_like(total)

            def step(i, carry):
                at = pl.ds(pl.multiple_of(i * ROW_TILE, ROW_TILE), ROW_TILE)
                values = here[5][at, :].astype(jnp.float32)
                scale = lax.rsqrt(jnp.mean(values * values, axis=-1, keepdims=True) + norm_eps)
                normed = values * scale
                d_out = part[seq, at, :].astype(jnp.float32) + came[at, :].astype(jnp.float32)
                total[...] += d_out * normed
                scaled = d_out * here[8][0:1, :]
                mean = jnp.mean(scaled * normed, axis=-1, keepdims=True)
                d_in = here[6][at, :] + scale * (scaled - normed * mean)
                grad[at, :] = d_in.astype(grad.dtype)
                return carry

            lax.fori_loop(0, tok_rows // ROW_TILE, step, 0)
            summed = jnp.sum(total[...], axis=0, keepdims=True)
            for n in range(blocks):
                here[7][n, 0:1, :] = summed[:, n * rows : (n + 1) * rows]
            self.out.start()

        pairs = blocks // 2
        found = [functools.partial(multiply, i, i + 2) for i in range(0, pairs, 2)]
        return found + [send, norm_back]

    def at_step(self, tasks, i, steps):
        rounds = (steps - self.ahead) // len(self.order)
        last = rounds * self.order.index(5) - self.ahead - 1
        if i < len(tasks) - 2:
            return [tasks[i]] + ([tasks[-2]] if i == len(tasks) - 3 else [])
        return [tasks[-1]] if i == last else []

    def finish(self):
        self.exchange.wait_send()
        self.out.wait()


def scatter_sum(parts, collective_id, out_dtype, seq_count=1, sides=(), work=None):
    work = work or NoWork()
    count = lax.axis_size("shard")
    shapes = list(work.part_shapes) or parts
    arrays = len(shapes)
    lead = (seq_count,) if seq_count > 1 else ()
    others = max(seq_count - 1, 1)
    return pl.pallas_call(
        functools.partial(scatter_kernel, count, seq_count, arrays, len(sides), work),
        out_shape=[jax.ShapeDtypeStruct(lead + p.shape[1:], out_dtype) for p in shapes]
        + [jax.ShapeDtypeStruct(s.shape, s.dtype) for s in sides]
        + list(work.results),
        in_specs=[pl.BlockSpec(memory_space=pltpu.VMEM)] * len(parts)
        + [pl.BlockSpec(memory_space=pl.ANY)] * (len(sides) + work.inputs),
        out_specs=[pl.BlockSpec(memory_space=pltpu.VMEM)] * arrays
        + [pl.BlockSpec(memory_space=pl.ANY)] * (len(sides) + work.outputs),
        scratch_shapes=[pltpu.VMEM(p.shape, p.dtype) for p in list(work.part_shapes) + list(shapes)]
        + [
            pltpu.SemaphoreType.DMA((arrays, count)),
            pltpu.SemaphoreType.DMA((arrays, count)),
            pltpu.SemaphoreType.DMA((arrays, others)),
            pltpu.SemaphoreType.DMA((arrays, others)),
            pltpu.SemaphoreType.DMA((max(len(sides), 1),)),
            pltpu.SemaphoreType.DMA((max(len(sides), 1),)),
        ]
        + list(work.scratch),
        compiler_params=pltpu.CompilerParams(
            collective_id=collective_id, has_side_effects=True, vmem_limit_bytes=VMEM_LIMIT
        ),
        name="scatter_sum_%d" % collective_id,
    )(*parts, *sides, *work.operands)


def place_kernel(refs_in, seq_count, *refs):
    for i, o in enumerate(refs_in):
        out_ref, base = refs[len(refs_in) + o[0]], o[1]
        cols = refs[i].shape[2]
        for s in range(seq_count):
            at = base + s * o[2]
            out_ref[:, at : at + cols] = refs[i][s].astype(out_ref.dtype)


def place_rows(pieces, targets, out_cols):
    seq_count, rows, _ = pieces[0].shape
    return pl.pallas_call(
        functools.partial(place_kernel, targets, seq_count),
        out_shape=[jax.ShapeDtypeStruct((rows, cols), jnp.float32) for cols in out_cols],
        in_specs=[pl.BlockSpec(memory_space=pltpu.VMEM)] * len(pieces),
        out_specs=[pl.BlockSpec(memory_space=pltpu.VMEM)] * len(out_cols),
        name="place_rows",
    )(*pieces)


def expert_kernel(count, *refs):
    (ffn_own, grad_own, weight), refs = refs[:3], refs[3:]
    matrices, refs = refs[:3], refs[3:]
    (rows_out, grad_out, hidden_out, mixed_out, gate_out, up_out), refs = refs[:6], refs[6:]
    pair_out, refs = refs[:2], refs[2:]
    (ffn_all, grad_all, both_w, down_w, gate_by, up_by), refs = refs[:6], refs[6:]
    (hidden_at, mixed_at, both_at, left_at, right_at), refs = refs[:5], refs[5:]
    ffn_send, ffn_recv, grad_send, grad_recv, load, own_sem, rows_sem, out_sem = refs
    me = lax.axis_index("shard")
    seq = lax.axis_index("seq")
    tiles = count // 2
    low, f32 = ffn_own.dtype, jnp.float32
    ffn = Line(count, ffn_own, ffn_all, ffn_send, ffn_recv, seq, 2)
    grad = Line(count, grad_own, grad_all, grad_send, grad_recv, seq, 2)
    ffn.meet()
    ffn.start(0)
    inner = down_w.shape[0]
    gate_span, up_span = slice(0, inner), slice(inner, 2 * inner)
    places = (both_w.at[:, gate_span], both_w.at[:, up_span], down_w)
    loads = [
        pltpu.make_async_copy(source, target, load.at[i])
        for i, (source, target) in enumerate(zip(matrices, places))
    ]
    for copy in loads:
        copy.start()
    ffn_keep = pltpu.make_async_copy(ffn_own, ffn_all.at[me], own_sem.at[0])
    grad_keep = pltpu.make_async_copy(grad_own, grad_all.at[me], own_sem.at[1])
    ffn_keep.start()
    grad_keep.start()
    ffn_keep.wait()
    for copy in loads:
        copy.wait()

    tile_of = ffn.pair

    def put(number, slot, staged, target, tile):
        return pltpu.make_async_copy(staged.at[slot], target.at[tile], out_sem.at[number, slot])

    def keep_rows(number, rows, target, tile):
        at = pl.ds(2 * tile, 2)
        return pltpu.make_async_copy(rows.at[at], target.at[at], rows_sem.at[number, tile])

    def arrivals(way, i, extra):
        done = 0
        for at in range(tiles):
            upto = way.order.index(2 * at) + 1 if at else 0
            order = way.order[done:upto]
            done = max(done, upto)

            @pl.when(i == at)
            def _(at=at, order=order):
                for r in order:
                    way.arrive(r)
                if at in extra:
                    extra[at]()
                way.wait_twin(2 * at)

    columns = inner // 2

    def beyond(at):
        return slice(inner + at.start, inner + at.stop)

    def forward(i, carry):
        arrivals(ffn, i, {tiles - 2: lambda: grad.start(0)})
        tile = tile_of(i)
        slot = lax.rem(i, 2)
        keep_rows(0, ffn_all, rows_out, tile).start()

        @pl.when(i >= 2)
        def _():
            put(0, slot, hidden_at, hidden_out, tile_of(i - 2)).wait()
            put(1, slot, mixed_at, mixed_out, tile_of(i - 2)).wait()

        rows = ffn_all[pl.ds(2 * tile, 2)].reshape(-1, ffn_all.shape[2])
        for c in range(2):
            at = slice(c * columns, (c + 1) * columns)
            gate = jnp.dot(rows, both_w[:, at], preferred_element_type=f32)
            up = jnp.dot(rows, both_w[:, beyond(at)], preferred_element_type=f32)
            sigma = jax.nn.sigmoid(gate)
            weighted = weight[tile] * sigma
            silu = weighted * gate
            hidden_at[slot, :, at] = (silu * up).astype(low)
            gate_by[i, :, at] = up * (weighted + silu * (1.0 - sigma))
            up_by[i, :, at] = silu
        put(0, slot, hidden_at, hidden_out, tile).start()
        half = down_w.shape[1] // 2
        for c in range(2):
            at = slice(c * half, (c + 1) * half)
            result = jnp.dot(hidden_at[slot], down_w[:, at], preferred_element_type=f32)
            mixed_at[slot, :, at] = result.astype(low)
        put(1, slot, mixed_at, mixed_out, tile).start()
        return carry

    lax.fori_loop(0, tiles, forward, 0)
    grad_keep.wait()

    def backward(i, carry):
        arrivals(grad, i, {})
        tile = tile_of(i)
        slot = lax.rem(i, 2)

        keep_rows(1, grad_all, grad_out, tile).start()

        @pl.when(i >= 2)
        def _():
            before = tile_of(i - 2)
            put(2, slot, both_at.at[:, :, gate_span], gate_out, before).wait()
            put(3, slot, both_at.at[:, :, up_span], up_out, before).wait()
            put(4, slot, left_at, pair_out[0], before).wait()
            put(5, slot, right_at, pair_out[1], before).wait()

        rows = grad_all[pl.ds(2 * tile, 2)].reshape(-1, grad_all.shape[2])
        for c in range(2):
            at = slice(c * columns, (c + 1) * columns)
            d_hidden = contract_cols(rows, down_w[at, :])
            both_at[slot, :, at] = (d_hidden * gate_by[i, :, at]).astype(low)
            both_at[slot, :, beyond(at)] = (d_hidden * up_by[i, :, at]).astype(low)
        put(2, slot, both_at.at[:, :, gate_span], gate_out, tile).start()
        put(3, slot, both_at.at[:, :, up_span], up_out, tile).start()
        half = both_w.shape[0] // 2
        for c, staged in enumerate((left_at, right_at)):
            at = slice(c * half, (c + 1) * half)
            staged[slot] = contract_cols(both_at[slot], both_w[at, :]).astype(low)
            put(4 + c, slot, staged, pair_out[c], tile).start()
        return carry

    lax.fori_loop(0, tiles, backward, 0)
    ffn.finish()
    grad.finish()
    for i in range(tiles):
        keep_rows(0, ffn_all, rows_out, i).wait()
        keep_rows(1, grad_all, grad_out, i).wait()
    outs = (hidden_out, mixed_out, gate_out, up_out, pair_out[0], pair_out[1])
    parts = (both_at.at[:, :, gate_span], both_at.at[:, :, up_span])
    staged = (hidden_at, mixed_at) + parts + (left_at, right_at)
    for i in (tiles - 2, tiles - 1):
        for number in range(len(outs)):
            put(number, i % 2, staged[number], outs[number], tile_of(i)).wait()


def run_experts(ffn_in, own_grad, weight, gate_w, up_w, down_w, collective_id):
    count = lax.axis_size("shard")
    rows, width = ffn_in.shape
    inner = gate_w.shape[1]
    tiles, two = count // 2, 2 * rows
    low = ffn_in.dtype
    shape = jax.ShapeDtypeStruct
    wide, narrow = (tiles, two, width), (tiles, two, inner)
    outs = [shape((count, rows, width), low)] * 2
    outs += [shape(s, low) for s in (narrow, wide, narrow, narrow)]
    outs += [shape((tiles, two, width // 2), low)] * 2
    vmem, hbm = pl.BlockSpec(memory_space=pltpu.VMEM), pl.BlockSpec(memory_space=pl.ANY)
    staged = [inner, width, 2 * inner, width // 2, width // 2]
    return pl.pallas_call(
        functools.partial(expert_kernel, count),
        out_shape=outs,
        in_specs=[vmem] * 3 + [hbm] * 3,
        out_specs=[hbm] * len(outs),
        scratch_shapes=[
            pltpu.VMEM((count, rows, width), low),
            pltpu.VMEM((count, rows, width), low),
            pltpu.VMEM((width, 2 * inner), low),
            pltpu.VMEM(down_w.shape, low),
            pltpu.VMEM((tiles, two, inner), jnp.float32),
            pltpu.VMEM((tiles, two, inner), jnp.float32),
        ]
        + [pltpu.VMEM((2, two, cols), low) for cols in staged]
        + [pltpu.SemaphoreType.DMA((2, count + 1))] * 4
        + [
            pltpu.SemaphoreType.DMA((3,)),
            pltpu.SemaphoreType.DMA((2,)),
            pltpu.SemaphoreType.DMA((2, tiles)),
            pltpu.SemaphoreType.DMA((len(staged) + 1, 2)),
        ],
        compiler_params=pltpu.CompilerParams(
            collective_id=collective_id, has_side_effects=True, vmem_limit_bytes=VMEM_LIMIT
        ),
        name="run_experts",
    )(ffn_in, own_grad, weight, gate_w, up_w, down_w)


GAIN_LANES = 128


def pair_tables(expert_list, prob_list, expert_count):
    numbers = jnp.arange(expert_count, dtype=jnp.int32)
    named = expert_list[None, :, :] == numbers[:, None, None]
    return jnp.sum(jnp.where(named, prob_list[None], 0.0), axis=2)


def shards(
    layer_input,
    seq_lengths,
    seq_order,
    expert_ids,
    expert_probs,
    weight_qkv,
    weight_out,
    norm_gains,
    weight_gate,
    weight_up,
    weight_down,
    out_cotangent,
):
    width = layer_input.shape[-1]
    tok_rows = layer_input.shape[1]
    seq_count = lax.axis_size("seq")
    seq_at = lax.axis_index("seq")
    group_tok = tok_rows * seq_count
    experts = lax.axis_size("shard")
    shard_at = lax.axis_index("shard")
    weight_rows = weight_qkv.shape[0]
    heads_local = HEADS // seq_count
    local_width = heads_local * HEAD_DIM
    out_cols = width // seq_count
    score_scale = HEAD_DIM ** (-0.5)
    low = jnp.bfloat16
    f32 = jnp.float32

    def take_seq(array, axis):
        return lax.dynamic_index_in_dim(array, seq_at, axis, keepdims=False)

    def seq_sum(part):
        if seq_count != 2:
            return lax.psum_scatter(part, "seq", scatter_dimension=0, tiled=True).astype(f32)
        halves = part.reshape(2, part.shape[0] // 2, part.shape[1])
        there = lax.dynamic_index_in_dim(halves, 1 - seq_at, 0, keepdims=False)
        here = lax.dynamic_index_in_dim(halves, seq_at, 0, keepdims=False)
        came = lax.ppermute(there, "seq", [(0, 1), (1, 0)])
        return here.astype(f32) + came.astype(f32)

    own_cols = take_seq(weight_qkv.reshape(weight_rows, 3, seq_count, local_width), 2)
    own_gains = jnp.pad(norm_gains, ((0, 0), (0, GAIN_LANES - norm_gains.shape[1])))
    table = pair_tables(expert_ids[0], expert_probs[0], experts)
    own_block = jnp.concatenate(
        [own_cols.reshape(weight_rows, 3 * local_width), own_gains], axis=1
    )
    qkv_cols, tables_all = gather_blocks([own_block, table], 1, ((0, 1),), (2, 1))
    own_out, qkv_cols = lax.optimization_barrier((weight_out, qkv_cols))
    full_out = lax.all_gather(own_out, "shard", axis=0, tiled=True)
    qkv_all = qkv_cols
    qkv_cols = qkv_cols.reshape(width, 3 * local_width + GAIN_LANES)
    gain_cols = qkv_cols[:, 3 * local_width :][:, : norm_gains.shape[1]].astype(f32)
    qkv_cols = qkv_cols[:, : 3 * local_width]
    group_in = lax.all_gather(layer_input[0], "seq", axis=0, tiled=True).astype(f32)
    pair_weight = lax.dynamic_index_in_dim(tables_all, shard_at, 1, keepdims=False)

    segment, position = group_layout(seq_lengths[0], seq_order[0], group_tok)
    places = jnp.arange(group_tok, dtype=jnp.int32)
    allowed = (segment[:, None] == segment[None, :]) & (places[None, :] <= places[:, None])
    cosine, sine_part = rope_tables(position, HEAD_DIM)

    def rope(values):
        return rotate(
            values.reshape(group_tok, heads_local, HEAD_DIM), cosine, sine_part
        ).reshape(group_tok, local_width)

    def rope_back(grads):
        return rotate(
            grads.reshape(group_tok, heads_local, HEAD_DIM), cosine, -sine_part
        ).reshape(group_tok, local_width)

    gain_q = lax.dynamic_slice_in_dim(gain_cols[:, 1], seq_at * local_width, local_width)
    gain_k = lax.dynamic_slice_in_dim(gain_cols[:, 2], seq_at * local_width, local_width)

    group_r = lax.rsqrt(jnp.mean(group_in * group_in, axis=-1, keepdims=True) + norm_eps)
    group_n = group_in * group_r
    attn_in = (group_n * gain_cols[:, 0]).astype(low)
    projected = jnp.dot(attn_in, qkv_cols, preferred_element_type=f32)
    q_raw = projected[:, :local_width]
    k_raw = projected[:, local_width : 2 * local_width]
    value = projected[:, 2 * local_width :].astype(low)
    squares = jnp.stack([jnp.sum(q_raw * q_raw, axis=-1), jnp.sum(k_raw * k_raw, axis=-1)])
    squares = lax.psum(squares, "seq")
    q_r, k_r = (lax.rsqrt(row / width + norm_eps)[:, None] for row in squares)
    q_n = q_raw * q_r
    k_n = k_raw * k_r
    query = rope(q_n * gain_q).astype(low)
    key = rope(k_n * gain_k).astype(low)
    query_head = query.reshape(group_tok, heads_local, HEAD_DIM)
    key_head = key.reshape(group_tok, heads_local, HEAD_DIM)
    value_head = value.reshape(group_tok, heads_local, HEAD_DIM)
    scores = jnp.einsum("ihd,jhd->hij", query_head, key_head, preferred_element_type=f32)
    scores = jnp.where(allowed[None], scores * score_scale, -1e30)
    score_peak = jnp.max(scores, axis=-1, keepdims=True)
    weights_exp = jnp.exp(scores - score_peak)
    attn_probs = weights_exp / jnp.sum(weights_exp, axis=-1, keepdims=True)
    probs_low = attn_probs.astype(low)
    mix_head = jnp.einsum("hij,jhd->ihd", probs_low, value_head, preferred_element_type=f32)
    mix_head = mix_head.astype(low).reshape(group_tok, local_width)
    attn_mix = lax.all_to_all(mix_head, "seq", split_axis=0, concat_axis=1, tiled=True)
    mix_all = lax.all_gather(mix_head, "seq", axis=1, tiled=True)
    resid = layer_input[0].astype(f32) + jnp.dot(attn_mix, full_out, preferred_element_type=f32)
    ffn_r = lax.rsqrt(jnp.mean(resid * resid, axis=-1, keepdims=True) + norm_eps)
    ffn_n = resid * ffn_r
    ffn_in = (ffn_n * gain_cols[:, 3]).astype(low)

    pairs = seq_count == 2
    gate_weight = weight_gate[0]
    up_weight = weight_up[0]
    down_weight = weight_down[0]
    if experts == LINE:
        tile_weight = pair_weight.reshape(experts // 2, 2 * tok_rows, 1)
        results = run_experts(
            ffn_in, out_cotangent[0], tile_weight, gate_weight, up_weight, down_weight, 2
        )
        rows_in, d_expert, hidden, out_part, d_gate, d_up, *halves = (
            result.reshape(experts * tok_rows, -1) for result in results
        )
    else:
        slot_weight = pair_weight.reshape(-1, 1)
        (ffn_all, grad_all) = gather_blocks(
            [ffn_in, out_cotangent[0]], 2, ((0,), (1,)), (1, 1)
        )
        rows_in = ffn_all.reshape(-1, width)
        gate = jnp.dot(rows_in, gate_weight, preferred_element_type=f32)
        up = jnp.dot(rows_in, up_weight, preferred_element_type=f32)
        sigma = jax.nn.sigmoid(gate)
        silu = gate * sigma
        hidden = (silu * up).astype(low)
        expert_out = jnp.dot(hidden, down_weight, preferred_element_type=f32).astype(low)
        out_part = (expert_out.astype(f32) * slot_weight).astype(low)
        d_expert = (grad_all.reshape(-1, width).astype(f32) * slot_weight).astype(low)
        d_hidden = contract_cols(d_expert, down_weight)
        d_gate = (d_hidden * up * sigma * (1.0 + gate * (1.0 - sigma))).astype(low)
        d_up = (d_hidden * silu).astype(low)
        d_pair = contract_cols(d_gate, gate_weight) + contract_cols(d_up, up_weight)
        halves = jnp.split(d_pair.astype(low), 2, axis=1)
    halves = [part.reshape(experts, tok_rows, -1) for part in halves]
    products = [(hidden, d_expert), (rows_in, d_gate), (rows_in, d_up)]
    if pairs:
        results = scatter_sum(halves, 3, f32, work=ExpertGrads(products))
        d_left, d_right, down_came, down_mine, gate_there, gate_mine, up_there, up_mine = results
    else:
        d_left, d_right = scatter_sum(halves, 3, f32)
    d_ffn_in = jnp.concatenate([d_left, d_right], axis=1)
    out_part, d_ffn_in = lax.optimization_barrier((out_part, d_ffn_in))
    mixed_out = lax.psum_scatter(
        out_part, "shard", scatter_dimension=0, tiled=True
    )

    grad_tokens = out_cotangent[0].astype(f32)
    d_scaled = d_ffn_in * gain_cols[:, 3]
    d_resid = grad_tokens + ffn_r * (
        d_scaled - ffn_n * jnp.mean(d_scaled * ffn_n, axis=-1, keepdims=True)
    )
    grad_g_ffn = jnp.sum(d_ffn_in * ffn_n, axis=0)
    d_branch = d_resid.astype(low)
    d_mix = contract_cols(d_branch, full_out).astype(low)
    d_mix_head = lax.all_to_all(d_mix, "seq", split_axis=1, concat_axis=0, tiled=True).reshape(
        group_tok, heads_local, HEAD_DIM
    )
    branch_cols = lax.all_to_all(d_branch, "seq", split_axis=1, concat_axis=0, tiled=True)
    d_probs = jnp.einsum("ihd,jhd->hij", d_mix_head, value_head, preferred_element_type=f32)
    delta_rows = jnp.sum(attn_probs * d_probs, axis=-1, keepdims=True)
    d_scores = (attn_probs * (d_probs - delta_rows)).astype(low)
    d_query = (
        jnp.einsum("hij,jhd->ihd", d_scores, key_head, preferred_element_type=f32) * score_scale
    ).astype(low)
    d_key = (
        jnp.einsum("hij,ihd->jhd", d_scores, query_head, preferred_element_type=f32) * score_scale
    ).astype(low)
    d_value = jnp.einsum(
        "hij,ihd->jhd", probs_low, d_mix_head, preferred_element_type=f32
    ).astype(low)
    dq_rot = rope_back(d_query.reshape(group_tok, local_width).astype(f32))
    dk_rot = rope_back(d_key.reshape(group_tok, local_width).astype(f32))
    grad_g_q = jnp.sum(dq_rot * q_n, axis=0)
    grad_g_k = jnp.sum(dk_rot * k_n, axis=0)
    dq_scaled = dq_rot * gain_q
    dk_scaled = dk_rot * gain_k
    dots = jnp.stack([jnp.sum(dq_scaled * q_n, axis=-1), jnp.sum(dk_scaled * k_n, axis=-1)])
    dots = lax.psum(dots, "seq") / width
    if pairs:
        dots, gate_there = lax.optimization_barrier((dots, gate_there))
        gate_came = lax.ppermute(gate_there, "seq", [(0, 1), (1, 0)])
    dq_raw = q_r * (dq_scaled - q_n * dots[0][:, None])
    dk_raw = k_r * (dk_scaled - k_n * dots[1][:, None])
    d_qkv = jnp.concatenate(
        [dq_raw.astype(low), dk_raw.astype(low), d_value.reshape(group_tok, local_width)], axis=1
    )
    zeros = jnp.zeros((width,), f32)
    gain_rows = [
        zeros,
        lax.dynamic_update_slice_in_dim(zeros, grad_g_q, seq_at * local_width, 0),
        lax.dynamic_update_slice_in_dim(zeros, grad_g_k, seq_at * local_width, 0),
        grad_g_ffn,
    ]
    if pairs:
        gain_terms = jnp.stack(gain_rows).reshape(len(gain_rows), experts, weight_rows)
        gain_terms = jnp.pad(
            jnp.swapaxes(gain_terms, 0, 1), ((0, 0), (0, ROW_TILE - len(gain_rows)), (0, 0))
        )
        work = AttentionGrads(
            attn_in,
            d_qkv,
            mix_all,
            branch_cols,
            qkv_all,
            layer_input[0],
            d_resid,
            gain_terms,
            jnp.broadcast_to(gain_cols[:, 0], (8, width)),
        )
        *sums, sum_gains, up_came, input_grad = scatter_sum(
            [], 4, low, seq_count, sides=[up_there], work=work
        )
        sum_gate, sum_up, sum_down = (
            mine.astype(f32) + came.astype(f32)
            for mine, came in ((gate_mine, gate_came), (up_mine, up_came), (down_mine, down_came))
        )
        rows_gain = jnp.sum(sum_gains[:, : norm_gains.shape[1]].astype(f32), axis=0).T
    else:
        d_attn_in = seq_sum(contract_cols(d_qkv, qkv_cols).astype(low))
        own_n = lax.dynamic_slice_in_dim(group_n, seq_at * tok_rows, tok_rows)
        own_r = lax.dynamic_slice_in_dim(group_r, seq_at * tok_rows, tok_rows)
        dx_scaled = d_attn_in * gain_cols[:, 0]
        dx_norm = own_r * (
            dx_scaled - own_n * jnp.mean(dx_scaled * own_n, axis=-1, keepdims=True)
        )
        gain_rows[0] = jnp.sum(d_attn_in * own_n, axis=0)
        input_grad = (d_resid + dx_norm).astype(low)
        gain_terms = jnp.stack(gain_rows, axis=1)
        gain_terms = jnp.pad(gain_terms, ((0, 0), (0, GAIN_LANES - gain_terms.shape[1])))
        terms = [
            contract_rows(attn_in, d_qkv[:, i * local_width : (i + 1) * local_width])
            for i in range(3)
        ]
        terms += [contract_rows(mix_all, branch_cols), gain_terms]
        terms = [term.astype(low).reshape(experts, weight_rows, -1) for term in terms]
        *sums, sum_gains = scatter_sum(terms, 4, low, seq_count)
        sum_down, sum_gate, sum_up = (
            lax.psum_scatter(
                contract_rows(left, right).astype(low), "seq", scatter_dimension=0, tiled=True
            ).astype(f32)
            for left, right in products
        )
        rows_gain = jnp.sum(sum_gains[:, :, : norm_gains.shape[1]].astype(f32), axis=0)
    mixed_out, sums[0] = lax.optimization_barrier((mixed_out, sums[0]))
    layer_output = (resid + mixed_out.astype(f32)).astype(low)
    targets = [(0, i * width, local_width) for i in range(3)]
    targets += [(1, i * sums[3].shape[2], out_cols) for i in range(len(sums) - 3)]
    rows_qkv, rows_out = place_rows(sums, targets, (3 * width, width))
    return (
        layer_output[None],
        input_grad[None],
        rows_qkv,
        rows_out,
        rows_gain,
        sum_gate[None],
        sum_up[None],
        sum_down[None],
    )


def solution(mesh):
    in_specs = (
        P("shard", "seq", None),
        P("shard", None),
        P("shard", None),
        P("shard", "seq", None),
        P("shard", "seq", None),
        P("shard", None),
        P("shard", None),
        P("shard", None),
        P("shard", None, None),
        P("shard", None, None),
        P("shard", None, None),
        P("shard", "seq", None),
    )
    out_specs = (
        P("shard", "seq", None),
        P("shard", "seq", None),
        P("shard", None),
        P("shard", None),
        P("shard", None),
        P("shard", "seq", None),
        P("shard", "seq", None),
        P("shard", "seq", None),
    )
    return jax.shard_map(shards, mesh=mesh, in_specs=in_specs, out_specs=out_specs, check_vma=False)
```
